1024 devices in a mesh: sfc: 128 (over y, z), sub: 8 (over x, core).
Axes of the slice: x: 4, y: 4, z: 32, core: 2. Of those that a mesh axis runs over, the one named last changes fastest.
Arguments:
- right_side: float32 [8, 8, 8, 128, 16, 128], P(None, None, None, 'sfc', 'sub'), may hold values from -7 to 7
- coefficient: float32 [128, 16, 128], P('sfc', 'sub'), may hold values from 0.3 to 3
- stiffness: float32 [8, 8], replicated, may hold values from -0.3 to 3.5, as said below
Outputs:
- solution: float32 [8, 8, 8, 128, 16, 128], P(None, None, None, 'sfc', 'sub')
The draws below stay inside these ranges and needn't reach their ends.
Inputs may be any that keep to these rules, and one draw needn't show every extreme that they name: `stiffness`: symmetric.
All inputs are finite; a program needn't handle non-finite values.
Results may differ from the reference program's by a relative error of at most 0.0002.
Values sent between devices are 32-bit elements; how exact they have to be, the bound alone decides.
No kernel may reach another device: no remote copies, remote signals or barrier semaphores. Data moves between devices by JAX's collectives and lax.ppermute only.
A program may use at most 32 MiB of HBM per device.

```python
import math
import jax
import jax.numpy as jnp
from jax import lax

NODES = 8
ELX = 128
PLANES = 128
SPANS = 16


def draw_right_side(key, part):
    first_key, second_key = jax.random.split(key)
    shape = (NODES, NODES, NODES, PLANES, SPANS, ELX)
    base = jnp.clip(jax.random.normal(first_key, shape, jnp.float32), -6.0, 6.0)
    planes = jax.random.uniform(second_key, (PLANES,), jnp.float32, -1.0, 1.0)
    return base + planes[None, None, None, :, None, None]


def draw_stiffness(key, part):
    first_key, second_key = jax.random.split(key)
    raw = jax.random.uniform(first_key, (NODES, NODES), jnp.float32, -0.3, 0.3)
    symmetric = (raw + raw.T) * 0.5
    diagonal = jax.random.uniform(second_key, (NODES,), jnp.float32, 2.5, 3.5)
    identity = jnp.eye(NODES, dtype=jnp.float32)
    return symmetric * (1.0 - identity) + identity * diagonal[None, :]


def shard_levels(own_key, extent, shards, smallest, high):
    def one(axis_at, blocks):
        steps = jax.random.uniform(jax.random.fold_in(jax.random.fold_in(own_key, 6), axis_at), (blocks,), jnp.float32, smallest / len(shards), high / len(shards))
        return jnp.repeat(jnp.exp(steps), extent[axis_at] // blocks).reshape((-1,) + (1,) * (len(extent) - axis_at - 1))

    gain = one(*shards[0])
    for cut in shards[1:]:
        gain = gain * one(*cut)
    return gain


def setup_inputs(seed: int = 0) -> dict:
    splits = jax.random.split(jax.random.key(seed), 4)
    return {
        "right_side": draw_right_side(jax.random.fold_in(splits[3], 71), 0),
        "coefficient": jnp.clip(jnp.exp(math.log(3.0) - 2.3025851 * jax.random.uniform(splits[1], (PLANES, SPANS, ELX), jnp.float32) ** shard_levels(splits[1], (PLANES, SPANS, ELX), ((0, 128), (1, 8)), -0.2, 0.2)), 0.3, 3.0),
        "stiffness": draw_stiffness(jax.random.fold_in(splits[3], 71), 0),
    }


penalty = 4.0
shift_mass = 0.02
cheb_centre = 1.25
cheb_half = 0.95
exact = lax.Precision.HIGHEST


def stiff_part(nodal_field, stiffness, coefficient):
    along_first = jnp.einsum('ia,abcpqr->ibcpqr', stiffness, nodal_field, precision=exact)
    along_second = jnp.einsum('jb,abcpqr->ajcpqr', stiffness, nodal_field, precision=exact)
    along_third = jnp.einsum('kc,abcpqr->abkpqr', stiffness, nodal_field, precision=exact)
    return coefficient * (along_first + along_second + along_third)


def face_terms(lower_face, upper_face, coefficient, prev_upper, prev_coef, next_lower, next_coef):
    upper_term = penalty * 0.5 * (coefficient + next_coef) * (upper_face - next_lower)
    lower_term = penalty * 0.5 * (coefficient + prev_coef) * (lower_face - prev_upper)
    return lower_term, upper_term


def add_faces(result, lower_term, upper_term, node_axis):
    leading = (slice(None),) * node_axis
    return result.at[leading + (0,)].add(lower_term).at[leading + (-1,)].add(upper_term)


def apply_operator(nodal_field, stiffness, coefficient):
    result = stiff_part(nodal_field, stiffness, coefficient)
    lower_face = nodal_field[:, :, 0]
    upper_face = nodal_field[:, :, -1]
    terms = face_terms(lower_face, upper_face, coefficient, jnp.roll(upper_face, 1, 4), jnp.roll(coefficient, 1, 2), jnp.roll(lower_face, -1, 4), jnp.roll(coefficient, -1, 2))
    result = add_faces(result, terms[0], terms[1], 2)
    lower_face = nodal_field[0]
    upper_face = nodal_field[-1]
    zero_face = jnp.zeros_like(upper_face[:, :, :1])
    zero_coef = jnp.zeros_like(coefficient[:1])
    terms = face_terms(lower_face, upper_face, coefficient,
                       jnp.concatenate([zero_face, upper_face[:, :, :-1]], 2), jnp.concatenate([zero_coef, coefficient[:-1]], 0),
                       jnp.concatenate([lower_face[:, :, 1:], zero_face], 2), jnp.concatenate([coefficient[1:], zero_coef], 0))
    result = add_faces(result, terms[0], terms[1], 0)
    lower_face = nodal_field[:, 0]
    upper_face = nodal_field[:, -1]
    terms = face_terms(lower_face, upper_face, coefficient, jnp.roll(upper_face, 1, 3), jnp.roll(coefficient, 1, 1), jnp.roll(lower_face, -1, 3), jnp.roll(coefficient, -1, 1))
    result = add_faces(result, terms[0], terms[1], 1)
    return result


def inverse_diagonal(stiffness, coefficient):
    count = stiffness.shape[0]
    ladder = jnp.arange(count)
    edges = ((ladder == 0) | (ladder == count - 1)).astype(stiffness.dtype)
    main = jnp.diagonal(stiffness) + penalty * 0.5 * edges
    total = main[:, None, None] + main[None, :, None] + main[None, None, :]
    return 1.0 / (total[:, :, :, None, None, None] * coefficient)


def second_step(right_side, iterate, previous_step, inverse, stiffness, coefficient):
    residual = right_side - apply_operator(iterate, stiffness, coefficient)
    rho_first = cheb_half / cheb_centre
    rho_second = 1.0 / (2.0 * cheb_centre / cheb_half - rho_first)
    update = rho_second * rho_first * previous_step + (2.0 * rho_second / cheb_half) * (residual * inverse)
    return iterate + update


def plane_solve(gains, means):
    zero = jnp.zeros((1,), gains.dtype)
    lower_band = jnp.concatenate([zero, -penalty * gains[:-1]])
    upper_band = jnp.concatenate([-penalty * gains[:-1], zero])
    diag_band = penalty * jnp.concatenate([gains[:1], gains[:-1]]) + (penalty + shift_mass) * gains

    def forward(carry, row):
        slope_prev, offset_prev = carry
        low_entry, diag_entry, up_entry, rhs_entry = row
        denom = diag_entry - low_entry * slope_prev
        slope = up_entry / denom
        offset = (rhs_entry - low_entry * offset_prev) / denom
        return (slope, offset), (slope, offset)

    start = gains[0] * 0.0
    _, (slopes, offsets) = lax.scan(forward, (start, start), (lower_band, diag_band, upper_band, means))

    def backward(next_value, row):
        slope, offset = row
        value = offset - slope * next_value
        return value, value

    _, solved = lax.scan(backward, start, (slopes, offsets), reverse=True)
    return solved


def reference(right_side, coefficient, stiffness):
    inverse = inverse_diagonal(stiffness, coefficient)
    first_step = right_side * inverse / cheb_centre
    iterate = second_step(right_side, first_step, first_step, inverse, stiffness, coefficient)
    residual = right_side - apply_operator(iterate, stiffness, coefficient)
    plane_mean = jnp.mean(residual, axis=(0, 1, 2, 4, 5))
    plane_coef = jnp.mean(coefficient, axis=(1, 2))
    correction = plane_solve(plane_coef, plane_mean)
    iterate = iterate + correction[None, None, None, :, None, None]
    residual = right_side - apply_operator(iterate, stiffness, coefficient)
    post_step = residual * inverse / cheb_centre
    iterate = iterate + post_step
    return second_step(right_side, iterate, post_step, inverse, stiffness, coefficient)
```

```python
import jax
import jax.numpy as jnp
from jax import lax
from jax.experimental import pallas as pl
from jax.experimental.pallas import tpu as pltpu
from jax.sharding import Mesh
from jax.sharding import PartitionSpec as P


N = 8
TILES = 2 * N * N
ROWS = TILES * N
penalty = 4.0
shift_mass = 0.02
centre = 1.25
half = 0.95
rho1 = half / centre
rho2 = 1.0 / (2.0 * centre / half - rho1)
keep = rho2 * rho1
gain2 = 2.0 * rho2 / half
exact = lax.Precision.HIGHEST
f32 = jnp.float32
bf16 = jnp.bfloat16
SFC = ("y", "z")
SUB = ("x", "c")


def tile(ref, t):
    return ref[pl.ds(t * N, N), :]


def put(ref, t, value):
    ref[pl.ds(t * N, N), :] = value


def at(q, a, b):
    return (q * N + a) * N + b


def node_scalars(st):
    diag = [st[i, i] + (2.0 if i in (0, N - 1) else 0.0) for i in range(N)]
    sums = []
    for i in range(N):
        total = st[i, 0]
        for j in range(1, N):
            total = total + st[i, j]
        sums.append(total)
    return diag, sums


def spread(values, index):
    out = jnp.where(index == 0, values[0], 0.0)
    for k in range(1, N):
        out = jnp.where(index == k, values[k], out)
    return out


def pair_index():
    row = lax.broadcasted_iota(jnp.int32, (N * N, 128), 0)
    return row // N, row % N


def raw(ref, q, a, b):
    return ref[pl.ds(at(0, a, b) * 2 * N + q, N, stride=2), :]


def pack_first(rs, coef, st, to_n, to_s, to_e, to_w):
    diag, _ = node_scalars(st)
    sub = lax.broadcasted_iota(jnp.int32, (N, 128), 0)
    mc = spread(diag, sub)
    c = [coef[pl.ds(q, 1), :] for q in range(2)]
    scale = [1.0 / (centre * c[q]) for q in range(2)]

    def value(q, a, b):
        return raw(rs, q, a, b) * scale[q] / ((diag[a] + diag[b]) + mc)

    zero = jnp.zeros((N, 128), f32)
    both = jnp.where(sub == 0, c[0], jnp.where(sub == 1, c[1], zero))
    for q in range(2):
        for b in range(N):
            put(to_n, q * N + b, value(q, N - 1, b))
            put(to_s, q * N + b, value(q, 0, b))
    put(to_n, 2 * N, both)
    put(to_s, 2 * N, both)
    for a in range(N):
        put(to_e, a, value(1, a, N - 1))
        put(to_w, a, value(0, a, 0))
    put(to_e, N, zero + c[1])
    put(to_w, N, zero + c[0])


def stiff(u, kk, st, acc):
    for a in range(N):
        lo = u[pl.ds(at(0, a, 0) * N, N * N), :]
        hi = u[pl.ds(at(1, a, 0) * N, N * N), :]
        x = jnp.concatenate([lo, hi], axis=1)
        xh = x.astype(bf16)
        xl = (x - xh.astype(f32)).astype(bf16)
        main = jnp.dot(kk[...], xh, preferred_element_type=f32)
        rest = jnp.dot(kk[pl.ds(0, N * N), :], xl, preferred_element_type=f32)
        y = main[: N * N] + (main[N * N :] + rest)
        acc[pl.ds(at(0, a, 0) * N, N * N), :] = y[:, :128]
        acc[pl.ds(at(1, a, 0) * N, N * N), :] = y[:, 128:]
    for q in range(2):
        for b in range(N):
            us = [tile(u, at(q, j, b)) for j in range(N)]
            for i in range(N):
                t = tile(acc, at(q, i, b))
                for j in range(N):
                    t = t + st[i, j] * us[j]
                put(acc, at(q, i, b), t)


def inner_faces(u, coef, acc):
    c = [coef[pl.ds(q, 1), :] for q in range(2)]
    for q in range(2):
        rc = 2.0 / c[q]
        up = 2.0 + pltpu.roll(c[q], 127, 1) * rc
        down = 2.0 + pltpu.roll(c[q], 1, 1) * rc
        for a in range(N):
            base = at(q, a, 0) * N
            first = pl.ds(base, N, stride=N)
            last = pl.ds(base + N - 1, N, stride=N)
            lower, upper = u[first, :], u[last, :]
            acc[last, :] += up * (upper - pltpu.roll(lower, 127, 1))
            acc[first, :] += down * (lower - pltpu.roll(upper, 1, 1))
    w0 = 2.0 + 2.0 * c[1] / c[0]
    w1 = 2.0 + 2.0 * c[0] / c[1]
    for a in range(N):
        d = tile(u, at(0, a, N - 1)) - tile(u, at(1, a, 0))
        put(acc, at(0, a, N - 1), tile(acc, at(0, a, N - 1)) + w0 * d)
        put(acc, at(1, a, 0), tile(acc, at(1, a, 0)) - w1 * d)


def block(ref, q, a):
    return ref[pl.ds(at(q, a, 0) * N, N * N), :]


def set_block(ref, q, a, value):
    ref[pl.ds(at(q, a, 0) * N, N * N), :] = value


def start(rs, coef, st, sv, g, rt, rb, kk, first, part):
    diag, sums = node_scalars(st)
    bi, ci = pair_index()
    mbc = spread(diag, bi) + spread(diag, ci)
    rb[...] = spread(sums, bi) + spread(sums, ci)
    row = lax.broadcasted_iota(jnp.int32, (N * N, N), 0)
    col = lax.broadcasted_iota(jnp.int32, (N * N, N), 1)
    pb = (row // N == col).astype(f32)
    pc = (row % N == col).astype(f32)
    wide = (((1,), (1,)), ((), ()))

    def outer(p):
        ps = jnp.dot(p, sv[...], precision=exact, preferred_element_type=f32)
        return lax.dot_general(ps, p, wide, precision=exact, preferred_element_type=f32)

    i = lax.broadcasted_iota(jnp.int32, (N * N, N * N), 0)
    j = lax.broadcasted_iota(jnp.int32, (N * N, N * N), 1)
    k = jnp.where(i % N == j % N, outer(pb), 0.0) + jnp.where(i // N == j // N, outer(pc), 0.0)
    kh = k.astype(bf16)
    kk[pl.ds(0, N * N), :] = kh
    kk[pl.ds(N * N, N * N), :] = (k - kh.astype(f32)).astype(bf16)
    rc = [1.0 / coef[pl.ds(q, 1), :] for q in range(2)]
    for a in range(N):
        r = 1.0 / (diag[a] + mbc)
        rt[pl.ds(a * N * N, N * N), :] = r
        for q in range(2):
            for b in range(N):
                t = raw(rs, q, a, b) * rc[q]
                put(g, at(q, a, b), t)
                put(first, at(q, a, b), t * r[b * N : (b + 1) * N] * (1.0 / centre))
    stiff(first, kk, st, part)
    inner_faces(first, coef, part)
    for q in range(2):
        for a in range(N):
            r = rt[pl.ds(a * N * N, N * N), :]
            v = (1.0 + keep) * block(first, q, a) + gain2 * r * (block(g, q, a) - block(part, q, a))
            set_block(part, q, a, v)


def middle(where, coef, st, g, rt, rb, kk, first, part, from_n, from_s, from_e, from_w, it, post, sums_out, to_e, to_w):
    c = [coef[pl.ds(q, 1), :] for q in range(2)]
    it[...] = part[...]
    wn = [2.0 + 2.0 * from_n[pl.ds(2 * N * N + q, 1), :] / c[q] for q in range(2)]
    ws = [2.0 + 2.0 * from_s[pl.ds(2 * N * N + q, 1), :] / c[q] for q in range(2)]
    we = 2.0 + 2.0 * from_e[pl.ds(N * N, 1), :] / c[1]
    ww = 2.0 + 2.0 * from_w[pl.ds(N * N, 1), :] / c[0]

    def add(q, a, b, w, other):
        k = at(q, a, b)
        put(it, k, tile(it, k) - gain2 * tile(rt, a * N + b) * (w * (tile(first, k) - other)))

    for q in range(2):
        for b in range(N):
            add(q, N - 1, b, wn[q], tile(from_n, q * N + b))
            add(q, 0, b, ws[q], tile(from_s, q * N + b))
    for a in range(N):
        add(1, a, N - 1, we, tile(from_e, a))
        add(0, a, 0, ww, tile(from_w, a))
    own = jnp.zeros((N, 128), f32)
    above = jnp.zeros((N, 128), f32)
    below = jnp.zeros((N, 128), f32)
    _, sums = node_scalars(st)
    for q in range(2):
        z = jnp.zeros((N * N, 128), f32)
        for a in range(N):
            z = z + (block(g, q, a) - (sums[a] + rb[...]) * block(it, q, a))
        t = z[:N]
        up = tile(it, at(q, N - 1, 0))
        dn = tile(it, at(q, 0, 0))
        for b in range(1, N):
            t = t + z[b * N : (b + 1) * N]
            up = up + tile(it, at(q, N - 1, b))
            dn = dn + tile(it, at(q, 0, b))
        up = (c[q] * wn[q]) * up
        dn = (c[q] * ws[q]) * dn
        own = own + (c[q] * t - (up + dn))
        above = above + up
        below = below + dn
    sub = lax.broadcasted_iota(jnp.int32, (N, 128), 0)
    lane = lax.broadcasted_iota(jnp.int32, (1, 128), 1)

    def total(x):
        return jnp.sum(x, axis=0, keepdims=True)

    stack = jnp.where(sub == 0, total(own), 0.0)
    stack = jnp.where(sub == 1, total(above), stack)
    stack = jnp.where(sub == 2, total(below), stack)
    stack = jnp.where(sub == 3, c[0] + c[1], stack)
    s = jnp.sum(stack, axis=1, keepdims=True)
    p = where[0]
    means = jnp.where(lane == p, s[0:1], 0.0)
    means = means + jnp.where(lane == p + 1, s[1:2], 0.0) + jnp.where(lane == p - 1, s[2:3], 0.0)
    sums_out[pl.ds(0, 1), :] = means
    sums_out[pl.ds(1, 1), :] = jnp.where(lane == p, s[3:4], 0.0)
    stiff(it, kk, st, post)
    inner_faces(it, coef, post)
    for q in range(2):
        for a in range(N):
            r = rt[pl.ds(a * N * N, N * N), :] * (1.0 / centre)
            set_block(post, q, a, block(it, q, a) + r * (block(g, q, a) - block(post, q, a)))
    for a in range(N):
        put(to_e, a, tile(it, at(1, a, N - 1)))
        put(to_e, N + a, tile(post, at(1, a, N - 1)))
        put(to_w, a, tile(it, at(0, a, 0)))
        put(to_w, N + a, tile(post, at(0, a, 0)))


def side(coef, rt, it, post_in, from_e, from_w, got_e, got_w, post, to_n, to_s):
    c = [coef[pl.ds(q, 1), :] for q in range(2)]
    ce = from_e[pl.ds(N * N, 1), :]
    cw = from_w[pl.ds(N * N, 1), :]
    we = 2.0 + 2.0 * ce / c[1]
    ww = 2.0 + 2.0 * cw / c[0]
    post[...] = post_in[...]
    for a in range(N):
        for q, b, w, got in ((1, N - 1, we, got_e), (0, 0, ww, got_w)):
            k = at(q, a, b)
            r = tile(rt, a * N + b) * (1.0 / centre)
            put(post, k, tile(post, k) - r * (w * (tile(it, k) - tile(got, a))))
    sub = lax.broadcasted_iota(jnp.int32, (N, 128), 0)
    outer = jnp.where(sub == 0, ce, jnp.where(sub == 1, cw, 0.0))
    for a, to in ((N - 1, to_n), (0, to_s)):
        for q in range(2):
            for b in range(N):
                put(to, q * N + b, tile(it, at(q, a, b)))
                put(to, 2 * N + q * N + b, tile(post, at(q, a, b)))
        put(to, 4 * N, tile(got_e, a))
        put(to, 4 * N + 1, tile(got_w, a))
        put(to, 4 * N + 2, outer)


def coarse(planes, gains, means):
    lane = lax.broadcasted_iota(jnp.int32, (1, 128), 1)
    before = jnp.where(lane == 0, gains, pltpu.roll(gains, 1, 1))
    diag = penalty * before + (penalty + shift_mass) * gains
    upper = jnp.where(lane < planes - 1, -penalty * gains, 0.0)
    diag = jnp.where(lane < planes, diag, 1.0)
    lower = jnp.where(lane == 0, 0.0, pltpu.roll(upper, 1, 1))
    right = jnp.where(lane < planes, means, 0.0)
    step = 1
    while step < planes:
        inv = 1.0 / diag
        lo = -lower * pltpu.roll(inv, step, 1)
        hi = -upper * pltpu.roll(inv, 128 - step, 1)
        right = right + lo * pltpu.roll(right, step, 1) + hi * pltpu.roll(right, 128 - step, 1)
        diag = diag + lo * pltpu.roll(upper, step, 1) + hi * pltpu.roll(lower, 128 - step, 1)
        lower = lo * pltpu.roll(lower, step, 1)
        upper = hi * pltpu.roll(upper, 128 - step, 1)
        step *= 2
    return right / diag


def finish(planes, per_plane, where, coef, st, g, rt, rb, kk, it, post, ring, from_n, from_s, from_e, from_w, got_e, got_w, got_n, got_s, out, acc, v):
    scaled = ring[0]
    for k in range(1, ring.shape[0]):
        scaled = scaled + ring[k]
    corr = coarse(planes, scaled[1:2] * (1.0 / per_plane), scaled[0:1] * (1.0 / (per_plane * N * N * N)))
    p = where[0]
    lane = lax.broadcasted_iota(jnp.int32, (1, 128), 1)

    def pick(k):
        return jnp.sum(jnp.where(lane == k, corr, 0.0), axis=1, keepdims=True) + jnp.zeros((1, 128), f32)

    mid, high, low = pick(p), pick(p + 1), pick(p - 1)
    has_n = (where[0] < planes - 1).astype(f32)
    has_s = (where[0] > 0).astype(f32)
    _, sums = node_scalars(st)
    inner = 1.0 / centre
    c = [coef[pl.ds(q, 1), :] for q in range(2)]
    cn = [from_n[pl.ds(2 * N * N + q, 1), :] for q in range(2)]
    cs = [from_s[pl.ds(2 * N * N + q, 1), :] for q in range(2)]
    ce = from_e[pl.ds(N * N, 1), :]
    cw = from_w[pl.ds(N * N, 1), :]
    wn = [2.0 + 2.0 * cn[q] / c[q] for q in range(2)]
    ws = [2.0 + 2.0 * cs[q] / c[q] for q in range(2)]
    we = 2.0 + 2.0 * ce / c[1]
    ww = 2.0 + 2.0 * cw / c[0]

    def r_at(a, b):
        return tile(rt, a * N + b)

    def weight(a, b):
        return 1.0 - inner * r_at(a, b) * (sums[a] + rb[pl.ds(b * N, N), :])

    for q in range(2):
        for a in range(N):
            r = rt[pl.ds(a * N * N, N * N), :]
            set_block(v, q, a, block(post, q, a) + mid * (1.0 - inner * r * (sums[a] + rb[...])))
        for b in range(N):
            for a, w, other, got in ((N - 1, wn[q], high, got_n), (0, ws[q], low, got_s)):
                k = at(q, a, b)
                jump = (tile(it, k) - tile(got, q * N + b)) + (mid - other)
                put(v, k, tile(v, k) - inner * r_at(a, b) * (w * jump))
    stiff(v, kk, st, acc)
    inner_faces(v, coef, acc)

    def add(k, w, other):
        put(acc, k, tile(acc, k) + w * (tile(v, k) - other))

    for q in range(2):
        for a, b0, w, has, got, far, cfar in (
            (N - 1, 0, wn[q], has_n, got_n, high, cn[q]),
            (0, N - 1, ws[q], has_s, got_s, low, cs[q]),
        ):
            back = 2.0 + 2.0 * c[q] / jnp.where(cfar > 0.0, cfar, 1.0)
            for b in range(N):
                k = at(q, a, b)
                jump = (tile(got, q * N + b) - tile(it, k)) + (far - mid)
                other = tile(got, 2 * N + q * N + b) + far * weight(b0, b) - inner * r_at(b0, b) * (back * jump)
                add(k, w, has * other)
    for q, b, far_b, w, got, line, row, cfar in (
        (1, N - 1, 0, we, got_e, 4 * N, 0, ce),
        (0, 0, N - 1, ww, got_w, 4 * N + 1, 1, cw),
    ):
        back = 2.0 + 2.0 * c[q] / cfar
        for a in range(N):
            k = at(q, a, b)
            loss = back * (tile(got, a) - tile(it, k))
            for edge, from_far, other in ((N - 1, got_n, high), (0, got_s, low)):
                if a == edge:
                    wf = 2.0 + 2.0 * from_far[pl.ds((4 * N + 2) * N + row, 1), :] / cfar
                    loss = loss + wf * ((tile(got, a) - tile(from_far, line)) + (mid - other))
            other = tile(got, N + a) + mid * weight(a, far_b) - inner * r_at(a, far_b) * loss
            add(k, w, other)
    for q in range(2):
        for a in range(N):
            r = rt[pl.ds(a * N * N, N * N), :]
            x = block(v, q, a)
            last = x + keep * ((x - block(it, q, a)) - mid) + gain2 * r * (block(g, q, a) - block(acc, q, a))
            for b in range(N):
                out[pl.ds(at(0, a, b) * 2 * N + q, N, stride=2), :] = last[b * N : (b + 1) * N]


def call(kernel, in_kinds, out_shapes, scratch=(), cost=None):
    kinds = {
        "v": pl.BlockSpec(memory_space=pltpu.VMEM),
        "s": pl.BlockSpec(memory_space=pltpu.SMEM),
    }
    return pl.pallas_call(
        kernel,
        out_shape=out_shapes,
        in_specs=[kinds[k] for k in in_kinds],
        out_specs=[kinds["v"]] * len(out_shapes),
        scratch_shapes=list(scratch),
        compiler_params=pltpu.CompilerParams(vmem_limit_bytes=24 << 20),
        cost_estimate=pl.CostEstimate(flops=cost or 10**6, bytes_accessed=10**5, transcendentals=0),
    )


def rows(n, dtype=f32, lanes=128):
    return jax.ShapeDtypeStruct((n, lanes), dtype)


def exchange(block_up, block_down, axis, count, periodic):
    up = [(i, i + 1) for i in range(count - 1)]
    if periodic:
        up.append((count - 1, 0))
    down = [(j, i) for i, j in up]
    return lax.ppermute(block_down, axis, down), lax.ppermute(block_up, axis, up)


def share(block, axis, count):
    return lax.all_to_all(jnp.broadcast_to(block[None], (count, *block.shape)), axis, 0, 0)


def solution(mesh):
    n_sfc, n_sub = mesh.shape["sfc"], mesh.shape["sub"]
    ny = 4 if n_sfc % 16 == 0 else 2
    nz = n_sfc // ny
    mesh4 = Mesh(mesh.devices.reshape(ny, nz, n_sub // 2, 2), ("y", "z", "x", "c"))

    def per_device(right_side, coefficient, stiffness):
        rs = right_side.reshape(ROWS, 128)
        coef = coefficient.reshape(2, 128)
        place = lax.axis_index(SFC).astype(jnp.int32)
        where = place.reshape(1)
        layer, strip = rows((2 * N + 1) * N), rows((N + 1) * N)
        to_n, to_s, to_e, to_w = call(pack_first, "vvs", [layer, layer, strip, strip])(rs, coef, stiffness)
        from_n, from_s = exchange(to_n, to_s, SFC, n_sfc, False)
        from_e, from_w = exchange(to_e, to_w, SUB, n_sub, True)
        field = rows(ROWS)
        g, rt, rb, kk, first, part = call(
            start, "vvsv", [field, rows(N * N * N), rows(N * N), rows(2 * N * N, bf16, N * N), field, field], cost=10**9
        )(rs, coef, stiffness, stiffness)
        it, post, sums, to_e, to_w = call(
            middle,
            "svsvvvvvvvvvv",
            [field, field, rows(2), rows(2 * N * N), rows(2 * N * N)],
        )(where, coef, stiffness, g, rt, rb, kk, first, part, from_n, from_s, from_e, from_w)
        got_e, got_w = exchange(to_e, to_w, SUB, n_sub, True)
        near = share(sums, ("y", "x", "c"), ny * n_sub).sum(0)
        post, to_n, to_s = call(side, "vvvvvvvv", [field, rows((4 * N + 3) * N), rows((4 * N + 3) * N)])(
            coef, rt, it, post, from_e, from_w, got_e, got_w
        )
        got_n, got_s = exchange(to_n, to_s, SFC, n_sfc, False)
        ring = share(near, "z", nz)

        def last(*refs):
            finish(n_sfc, float(2 * n_sub * 128), *refs)

        (out,) = call(
            last, "svs" + "v" * 15, [field], [pltpu.VMEM((ROWS, 128), f32), pltpu.VMEM((ROWS, 128), f32)]
        )(where, coef, stiffness, g, rt, rb, kk, it, post, ring, from_n, from_s, from_e, from_w, got_e, got_w, got_n, got_s)
        return out.reshape(right_side.shape)

    field_spec = P(None, None, None, SFC, SUB, None)
    return jax.shard_map(
        per_device, mesh=mesh4, in_specs=(field_spec, P(SFC, SUB, None), P()), out_specs=field_spec, check_vma=False
    )
```

```python
import jax
import jax.numpy as jnp
from jax import lax
from jax.experimental import pallas as pl
from jax.experimental.pallas import tpu as pltpu
from jax.sharding import Mesh
from jax.sharding import PartitionSpec as P


N = 8
TILES = 2 * N * N
ROWS = TILES * N
penalty = 4.0
shift_mass = 0.02
centre = 1.25
half = 0.95
rho1 = half / centre
rho2 = 1.0 / (2.0 * centre / half - rho1)
keep = rho2 * rho1
gain2 = 2.0 * rho2 / half
exact = lax.Precision.HIGHEST
f32 = jnp.float32
bf16 = jnp.bfloat16
SFC = ("y", "z")
SUB = ("x", "c")


def tile(ref, t):
    return ref[pl.ds(t * N, N), :]


def put(ref, t, value):
    ref[pl.ds(t * N, N), :] = value


def at(q, a, b):
    return (q * N + a) * N + b


def node_columns(sv):
    i = lax.broadcasted_iota(jnp.int32, (N, N), 0)
    j = lax.broadcasted_iota(jnp.int32, (N, N), 1)
    s = sv[...]
    edge = jnp.where((i == j) & ((i == 0) | (i == N - 1)), 2.0, 0.0)
    diag = jnp.sum(jnp.where(i == j, s, 0.0) + edge, axis=1, keepdims=True)
    zero = jnp.zeros((N, 128), f32)
    return diag + zero, jnp.sum(s, axis=1, keepdims=True) + zero


def line(x, k, count=N):
    return jnp.broadcast_to(x[k : k + 1], (count, 128))


def pair_sum(x):
    return jnp.concatenate([line(x, b) + x for b in range(N)], axis=0)


def raw(ref, q, a, b):
    return ref[pl.ds(at(0, a, b) * 2 * N + q, N, stride=2), :]


def pack_first(rs_far, coef_far, sv_far, to_n, to_s, to_e, to_w, rs, coef, sv, sems):
    copies = [
        pltpu.make_async_copy(src, dst, sems.at[k])
        for k, (src, dst) in enumerate(((sv_far, sv), (coef_far, coef), (rs_far, rs)))
    ]
    for copy in copies:
        copy.start()
    copies[0].wait()
    copies[1].wait()
    mc, _ = node_columns(sv)
    sub = lax.broadcasted_iota(jnp.int32, (N, 128), 0)
    c = [coef[pl.ds(q, 1), :] for q in range(2)]
    scale = [1.0 / (centre * c[q]) for q in range(2)]
    zero = jnp.zeros((N, 128), f32)
    both = jnp.where(sub == 0, c[0], jnp.where(sub == 1, c[1], zero))
    copies[2].wait()

    def value(q, a, b):
        return raw(rs, q, a, b) * scale[q] / ((line(mc, a) + line(mc, b)) + mc)

    for q in range(2):
        for b in range(N):
            put(to_n, q * N + b, value(q, N - 1, b))
            put(to_s, q * N + b, value(q, 0, b))
    put(to_n, 2 * N, both)
    put(to_s, 2 * N, both)
    for a in range(N):
        put(to_e, a, value(1, a, N - 1))
        put(to_w, a, value(0, a, 0))
    put(to_e, N, zero + c[1])
    put(to_w, N, zero + c[0])


def stiff(u, kk, st, acc):
    for a in range(N):
        lo = u[pl.ds(at(0, a, 0) * N, N * N), :]
        hi = u[pl.ds(at(1, a, 0) * N, N * N), :]
        x = jnp.concatenate([lo, hi], axis=1)
        xh = x.astype(bf16)
        xl = (x - xh.astype(f32)).astype(bf16)
        main = jnp.dot(kk[...], xh, preferred_element_type=f32)
        rest = jnp.dot(kk[pl.ds(0, N * N), :], xl, preferred_element_type=f32)
        y = main[: N * N] + (main[N * N :] + rest)
        acc[pl.ds(at(0, a, 0) * N, N * N), :] = y[:, :128]
        acc[pl.ds(at(1, a, 0) * N, N * N), :] = y[:, 128:]
    for q in range(2):
        for b in range(N):
            us = [tile(u, at(q, j, b)) for j in range(N)]
            for i in range(N):
                t = tile(acc, at(q, i, b))
                for j in range(N):
                    t = t + tile(st, i * N + j) * us[j]
                put(acc, at(q, i, b), t)


def inner_faces(u, coef, acc):
    c = [coef[pl.ds(q, 1), :] for q in range(2)]
    for q in range(2):
        rc = 2.0 / c[q]
        up = 2.0 + pltpu.roll(c[q], 127, 1) * rc
        down = 2.0 + pltpu.roll(c[q], 1, 1) * rc
        for a in range(N):
            base = at(q, a, 0) * N
            first = pl.ds(base, N, stride=N)
            last = pl.ds(base + N - 1, N, stride=N)
            lower, upper = u[first, :], u[last, :]
            acc[last, :] += up * (upper - pltpu.roll(lower, 127, 1))
            acc[first, :] += down * (lower - pltpu.roll(upper, 1, 1))
    w0 = 2.0 + 2.0 * c[1] / c[0]
    w1 = 2.0 + 2.0 * c[0] / c[1]
    for a in range(N):
        d = tile(u, at(0, a, N - 1)) - tile(u, at(1, a, 0))
        put(acc, at(0, a, N - 1), tile(acc, at(0, a, N - 1)) + w0 * d)
        put(acc, at(1, a, 0), tile(acc, at(1, a, 0)) - w1 * d)


def block(ref, q, a):
    return ref[pl.ds(at(q, a, 0) * N, N * N), :]


def set_block(ref, q, a, value):
    ref[pl.ds(at(q, a, 0) * N, N * N), :] = value


def start(rs, coef, sv, g, rt, rb, kk, st, first, part):
    diag, sums = node_columns(sv)
    mbc = pair_sum(diag)
    pairs = pair_sum(sums)
    for a in range(N):
        rb[pl.ds(a * N * N, N * N), :] = pairs + line(sums, a, N * N)
    for i in range(N):
        for j in range(N):
            put(st, i * N + j, jnp.broadcast_to(sv[pl.ds(i, 1), pl.ds(j, 1)], (N, 128)))
    row = lax.broadcasted_iota(jnp.int32, (N * N, N), 0)
    col = lax.broadcasted_iota(jnp.int32, (N * N, N), 1)
    pb = (row // N == col).astype(f32)
    pc = (row % N == col).astype(f32)
    wide = (((1,), (1,)), ((), ()))

    def outer(p):
        ps = jnp.dot(p, sv[...], precision=exact, preferred_element_type=f32)
        return lax.dot_general(ps, p, wide, precision=exact, preferred_element_type=f32)

    i = lax.broadcasted_iota(jnp.int32, (N * N, N * N), 0)
    j = lax.broadcasted_iota(jnp.int32, (N * N, N * N), 1)
    k = jnp.where(i % N == j % N, outer(pb), 0.0) + jnp.where(i // N == j // N, outer(pc), 0.0)
    kh = k.astype(bf16)
    kk[pl.ds(0, N * N), :] = kh
    kk[pl.ds(N * N, N * N), :] = (k - kh.astype(f32)).astype(bf16)
    rc = [1.0 / coef[pl.ds(q, 1), :] for q in range(2)]
    for a in range(N):
        r = 1.0 / (line(diag, a, N * N) + mbc)
        rt[pl.ds(a * N * N, N * N), :] = r
        for q in range(2):
            for b in range(N):
                t = raw(rs, q, a, b) * rc[q]
                put(g, at(q, a, b), t)
                put(first, at(q, a, b), t * r[b * N : (b + 1) * N] * (1.0 / centre))
    stiff(first, kk, st, part)
    inner_faces(first, coef, part)
    for q in range(2):
        for a in range(N):
            r = rt[pl.ds(a * N * N, N * N), :]
            v = (1.0 + keep) * block(first, q, a) + gain2 * r * (block(g, q, a) - block(part, q, a))
            set_block(part, q, a, v)


def middle(masks, coef, g, rt, rb, first, part, from_n, from_s, from_e, from_w, it, sums_out):
    c = [coef[pl.ds(q, 1), :] for q in range(2)]
    it[...] = part[...]
    wn = [2.0 + 2.0 * from_n[pl.ds(2 * N * N + q, 1), :] / c[q] for q in range(2)]
    ws = [2.0 + 2.0 * from_s[pl.ds(2 * N * N + q, 1), :] / c[q] for q in range(2)]
    we = 2.0 + 2.0 * from_e[pl.ds(N * N, 1), :] / c[1]
    ww = 2.0 + 2.0 * from_w[pl.ds(N * N, 1), :] / c[0]

    def add(q, a, b, w, other):
        k = at(q, a, b)
        put(it, k, tile(it, k) - gain2 * tile(rt, a * N + b) * (w * (tile(first, k) - other)))

    for q in range(2):
        for b in range(N):
            add(q, N - 1, b, wn[q], tile(from_n, q * N + b))
            add(q, 0, b, ws[q], tile(from_s, q * N + b))
    for a in range(N):
        add(1, a, N - 1, we, tile(from_e, a))
        add(0, a, 0, ww, tile(from_w, a))
    own = jnp.zeros((N, 128), f32)
    above = jnp.zeros((N, 128), f32)
    below = jnp.zeros((N, 128), f32)
    for q in range(2):
        z = jnp.zeros((N * N, 128), f32)
        for a in range(N):
            z = z + (block(g, q, a) - rb[pl.ds(a * N * N, N * N), :] * block(it, q, a))
        t = z[:N]
        up = tile(it, at(q, N - 1, 0))
        dn = tile(it, at(q, 0, 0))
        for b in range(1, N):
            t = t + z[b * N : (b + 1) * N]
            up = up + tile(it, at(q, N - 1, b))
            dn = dn + tile(it, at(q, 0, b))
        up = (c[q] * wn[q]) * up
        dn = (c[q] * ws[q]) * dn
        own = own + (c[q] * t - (up + dn))
        above = above + up
        below = below + dn
    sub = lax.broadcasted_iota(jnp.int32, (N, 128), 0)

    def total(x):
        return jnp.sum(x, axis=0, keepdims=True)

    stack = jnp.where(sub == 0, total(own), 0.0)
    stack = jnp.where(sub == 1, total(above), stack)
    stack = jnp.where(sub == 2, total(below), stack)
    stack = jnp.where(sub == 3, c[0] + c[1], stack)
    s = jnp.sum(stack, axis=1, keepdims=True)
    here = masks[pl.ds(0, 1), :]
    means = here * s[0:1] + masks[pl.ds(1, 1), :] * s[1:2] + masks[pl.ds(2, 1), :] * s[2:3]
    sub2 = lax.broadcasted_iota(jnp.int32, (2, 128), 0)
    pair = jnp.where(sub2 == 0, means, here * s[3:4])
    sums_out[...] = jnp.broadcast_to(pair[None], sums_out.shape)


def smooth(coef, st, g, rt, kk, it, post, to_e, to_w):
    stiff(it, kk, st, post)
    inner_faces(it, coef, post)
    for q in range(2):
        for a in range(N):
            r = rt[pl.ds(a * N * N, N * N), :] * (1.0 / centre)
            set_block(post, q, a, block(it, q, a) + r * (block(g, q, a) - block(post, q, a)))
    for a in range(N):
        put(to_e, a, tile(it, at(1, a, N - 1)))
        put(to_e, N + a, tile(post, at(1, a, N - 1)))
        put(to_w, a, tile(it, at(0, a, 0)))
        put(to_w, N + a, tile(post, at(0, a, 0)))


def fold(parts, ready, out):
    total = parts[0] + ready[pl.ds(0, 2), :]
    for k in range(1, parts.shape[0]):
        total = total + parts[k]
    out[...] = jnp.broadcast_to(total[None], out.shape)


def side(coef, rt, it, post_in, from_e, from_w, got_e, got_w, post, to_n, to_s, ready):
    c = [coef[pl.ds(q, 1), :] for q in range(2)]
    ce = from_e[pl.ds(N * N, 1), :]
    cw = from_w[pl.ds(N * N, 1), :]
    we = 2.0 + 2.0 * ce / c[1]
    ww = 2.0 + 2.0 * cw / c[0]
    post[...] = post_in[...]
    for a in range(N):
        for q, b, w, got in ((1, N - 1, we, got_e), (0, 0, ww, got_w)):
            k = at(q, a, b)
            r = tile(rt, a * N + b) * (1.0 / centre)
            put(post, k, tile(post, k) - r * (w * (tile(it, k) - tile(got, a))))
    sub = lax.broadcasted_iota(jnp.int32, (N, 128), 0)
    outer = jnp.where(sub == 0, ce, jnp.where(sub == 1, cw, 0.0))
    for a, to in ((N - 1, to_n), (0, to_s)):
        for q in range(2):
            for b in range(N):
                put(to, q * N + b, tile(it, at(q, a, b)))
                put(to, 2 * N + q * N + b, tile(post, at(q, a, b)))
        put(to, 4 * N, tile(got_e, a))
        put(to, 4 * N + 1, tile(got_w, a))
        put(to, 4 * N + 2, outer)
    ready[...] = jnp.zeros((N, 128), f32)


def coarse(planes, gains, means):
    lane = lax.broadcasted_iota(jnp.int32, (1, 128), 1)
    before = jnp.where(lane == 0, gains, pltpu.roll(gains, 1, 1))
    diag = penalty * before + (penalty + shift_mass) * gains
    upper = jnp.where(lane < planes - 1, -penalty * gains, 0.0)
    diag = jnp.where(lane < planes, diag, 1.0)
    lower = jnp.where(lane == 0, 0.0, pltpu.roll(upper, 1, 1))
    right = jnp.where(lane < planes, means, 0.0)
    step = 1
    while step < planes:
        inv = 1.0 / diag
        lo = -lower * pltpu.roll(inv, step, 1)
        hi = -upper * pltpu.roll(inv, 128 - step, 1)
        right = right + lo * pltpu.roll(right, step, 1) + hi * pltpu.roll(right, 128 - step, 1)
        diag = diag + lo * pltpu.roll(upper, step, 1) + hi * pltpu.roll(lower, 128 - step, 1)
        lower = lo * pltpu.roll(lower, step, 1)
        upper = hi * pltpu.roll(upper, 128 - step, 1)
        step *= 2
    return right / diag


def finish(planes, per_plane, masks, coef, st, g, rt, rb, kk, it, post, ring, from_n, from_s, from_e, from_w, got_e, got_w, got_n, got_s, out, acc, v):
    scaled = ring[0]
    for k in range(1, ring.shape[0]):
        scaled = scaled + ring[k]
    corr = coarse(planes, scaled[1:2] * (1.0 / per_plane), scaled[0:1] * (1.0 / (per_plane * N * N * N)))

    def pick(k):
        return jnp.sum(masks[pl.ds(k, 1), :] * corr, axis=1, keepdims=True) + jnp.zeros((1, 128), f32)

    mid, high, low = pick(0), pick(1), pick(2)
    has_n = masks[pl.ds(3, 1), :]
    has_s = masks[pl.ds(4, 1), :]
    inner = 1.0 / centre
    c = [coef[pl.ds(q, 1), :] for q in range(2)]
    cn = [from_n[pl.ds(2 * N * N + q, 1), :] for q in range(2)]
    cs = [from_s[pl.ds(2 * N * N + q, 1), :] for q in range(2)]
    ce = from_e[pl.ds(N * N, 1), :]
    cw = from_w[pl.ds(N * N, 1), :]
    wn = [2.0 + 2.0 * cn[q] / c[q] for q in range(2)]
    ws = [2.0 + 2.0 * cs[q] / c[q] for q in range(2)]
    we = 2.0 + 2.0 * ce / c[1]
    ww = 2.0 + 2.0 * cw / c[0]

    def r_at(a, b):
        return tile(rt, a * N + b)

    def weight(a, b):
        return 1.0 - inner * r_at(a, b) * tile(rb, a * N + b)

    for q in range(2):
        for a in range(N):
            r = rt[pl.ds(a * N * N, N * N), :]
            set_block(v, q, a, block(post, q, a) + mid * (1.0 - inner * r * rb[pl.ds(a * N * N, N * N), :]))
        for b in range(N):
            for a, w, other, got in ((N - 1, wn[q], high, got_n), (0, ws[q], low, got_s)):
                k = at(q, a, b)
                jump = (tile(it, k) - tile(got, q * N + b)) + (mid - other)
                put(v, k, tile(v, k) - inner * r_at(a, b) * (w * jump))
    stiff(v, kk, st, acc)
    inner_faces(v, coef, acc)

    def add(k, w, other):
        put(acc, k, tile(acc, k) + w * (tile(v, k) - other))

    for q in range(2):
        for a, b0, w, has, got, far, cfar in (
            (N - 1, 0, wn[q], has_n, got_n, high, cn[q]),
            (0, N - 1, ws[q], has_s, got_s, low, cs[q]),
        ):
            back = 2.0 + 2.0 * c[q] / jnp.where(cfar > 0.0, cfar, 1.0)
            for b in range(N):
                k = at(q, a, b)
                jump = (tile(got, q * N + b) - tile(it, k)) + (far - mid)
                other = tile(got, 2 * N + q * N + b) + far * weight(b0, b) - inner * r_at(b0, b) * (back * jump)
                add(k, w, has * other)
    for q, b, far_b, w, got, line, row, cfar in (
        (1, N - 1, 0, we, got_e, 4 * N, 0, ce),
        (0, 0, N - 1, ww, got_w, 4 * N + 1, 1, cw),
    ):
        back = 2.0 + 2.0 * c[q] / cfar
        for a in range(N):
            k = at(q, a, b)
            loss = back * (tile(got, a) - tile(it, k))
            for edge, from_far, other in ((N - 1, got_n, high), (0, got_s, low)):
                if a == edge:
                    wf = 2.0 + 2.0 * from_far[pl.ds((4 * N + 2) * N + row, 1), :] / cfar
                    loss = loss + wf * ((tile(got, a) - tile(from_far, line)) + (mid - other))
            other = tile(got, N + a) + mid * weight(a, far_b) - inner * r_at(a, far_b) * loss
            add(k, w, other)
    for q in range(2):
        for a in range(N):
            r = rt[pl.ds(a * N * N, N * N), :]
            x = block(v, q, a)
            last = x + keep * ((x - block(it, q, a)) - mid) + gain2 * r * (block(g, q, a) - block(acc, q, a))
            for b in range(N):
                out[pl.ds(at(0, a, b) * 2 * N + q, N, stride=2), :] = last[b * N : (b + 1) * N]


def call(kernel, in_kinds, out_shapes, scratch=(), cost=10**6, vmem=24):
    kinds = {"v": pl.BlockSpec(memory_space=pltpu.VMEM), "h": pl.BlockSpec(memory_space=pltpu.HBM)}
    return pl.pallas_call(
        kernel,
        out_shape=out_shapes,
        in_specs=[kinds[k] for k in in_kinds],
        out_specs=[kinds["v"]] * len(out_shapes),
        scratch_shapes=list(scratch),
        compiler_params=pltpu.CompilerParams(vmem_limit_bytes=vmem << 20),
        cost_estimate=pl.CostEstimate(flops=cost, bytes_accessed=10**5, transcendentals=0),
    )


def rows(n, dtype=f32, lanes=128):
    return jax.ShapeDtypeStruct((n, lanes), dtype)


def exchange(block_up, block_down, axis, count, periodic):
    up = [(i, i + 1) for i in range(count - 1)]
    if periodic:
        up.append((count - 1, 0))
    down = [(j, i) for i, j in up]
    return lax.ppermute(block_down, axis, down), lax.ppermute(block_up, axis, up)


def place_masks(place, planes):
    lane = jnp.arange(128)[None, :]
    k = jnp.arange(8)[:, None]
    hot = jnp.where(k == 0, place, jnp.where(k == 1, place + 1, place - 1))
    has = jnp.where(k == 3, place < planes - 1, place > 0)
    return jnp.where(k < 3, lane == hot, has).astype(f32)


def solution(mesh):
    n_sfc, n_sub = mesh.shape["sfc"], mesh.shape["sub"]
    ny = 4 if n_sfc % 16 == 0 else 2
    nz = n_sfc // ny
    mesh4 = Mesh(mesh.devices.reshape(ny, nz, n_sub // 2, 2), ("y", "z", "x", "c"))

    def per_device(right_side, coefficient, stiffness):
        rs = right_side.reshape(ROWS, 128)
        coef = coefficient.reshape(2, 128)
        masks = place_masks(lax.axis_index(SFC), n_sfc)
        field = rows(ROWS)
        layer, strip = rows((2 * N + 1) * N), rows((N + 1) * N)
        to_n, to_s, to_e, to_w = call(
            pack_first,
            "hhh",
            [layer, layer, strip, strip],
            [
                pltpu.VMEM((ROWS, 128), f32),
                pltpu.VMEM((2, 128), f32),
                pltpu.VMEM((N, N), f32),
                pltpu.SemaphoreType.DMA((3,)),
            ],
            vmem=60,
        )(rs, coef, stiffness)
        from_n, from_s = exchange(to_n, to_s, SFC, n_sfc, False)
        from_e, from_w = exchange(to_e, to_w, SUB, n_sub, True)
        table = rows(N * N * N)
        g, rt, rb, kk, st, first, part = call(
            start, "vvv", [field, table, table, rows(2 * N * N, bf16, N * N), table, field, field], cost=10**9
        )(rs, coef, stiffness)
        it, sums = call(middle, "v" * 11, [field, jax.ShapeDtypeStruct((ny * n_sub, 2, 128), f32)])(
            masks, coef, g, rt, rb, first, part, from_n, from_s, from_e, from_w
        )
        near = lax.all_to_all(sums, ("y", "x", "c"), 0, 0)
        post, to_e, to_w = call(smooth, "vvvvvv", [field, rows(2 * N * N), rows(2 * N * N)], cost=10**9)(
            coef, st, g, rt, kk, it
        )
        got_e, got_w = exchange(to_e, to_w, SUB, n_sub, True)
        post, to_n, to_s, ready = call(
            side, "vvvvvvvv", [field, rows((4 * N + 3) * N), rows((4 * N + 3) * N), rows(N)]
        )(
            coef, rt, it, post, from_e, from_w, got_e, got_w
        )
        (near,) = call(fold, "vv", [jax.ShapeDtypeStruct((nz, 2, 128), f32)])(near, ready)
        ring = lax.all_to_all(near, "z", 0, 0)
        got_n, got_s = exchange(to_n, to_s, SFC, n_sfc, False)

        def last(*refs):
            finish(n_sfc, float(2 * n_sub * 128), *refs)

        (out,) = call(last, "v" * 18, [field], [pltpu.VMEM((ROWS, 128), f32), pltpu.VMEM((ROWS, 128), f32)])(
            masks, coef, st, g, rt, rb, kk, it, post, ring, from_n, from_s, from_e, from_w, got_e, got_w, got_n, got_s
        )
        return out.reshape(right_side.shape)

    field_spec = P(None, None, None, SFC, SUB, None)
    return jax.shard_map(
        per_device, mesh=mesh4, in_specs=(field_spec, P(SFC, SUB, None), P()), out_specs=field_spec, check_vma=False
    )
```

```python
import jax
import jax.numpy as jnp
from jax import lax
from jax.experimental import pallas as pl
from jax.experimental.pallas import tpu as pltpu
from jax.sharding import Mesh
from jax.sharding import PartitionSpec as P


N = 8
TILES = 2 * N * N
ROWS = TILES * N
penalty = 4.0
shift_mass = 0.02
centre = 1.25
half = 0.95
rho1 = half / centre
rho2 = 1.0 / (2.0 * centre / half - rho1)
keep = rho2 * rho1
gain2 = 2.0 * rho2 / half
exact = lax.Precision.HIGHEST
f32 = jnp.float32
bf16 = jnp.bfloat16
SFC = ("y", "z")
SUB = ("x", "c")


class Either:
    def __init__(self, cond, one, other):
        self.cond, self.one, self.other = cond, one, other

    def __getitem__(self, key):
        return jnp.where(self.cond, self.one[key], self.other[key])


def both_sides(cond, swap_a, swap_b):
    return Either(cond, swap_a, swap_b), Either(cond, swap_b, swap_a)


def put_both(cond, swap_a, swap_b, t, to_next, to_prev):
    put(swap_a, t, jnp.where(cond, to_next, to_prev))
    put(swap_b, t, jnp.where(cond, to_prev, to_next))


def position():
    plane = lax.axis_index("y") * lax.axis_size("z") + lax.axis_index("z")
    return plane, lax.rem(lax.axis_index("z"), 2) == 0, lax.axis_index("c") == 0


def tile(ref, t):
    return ref[pl.ds(t * N, N), :]


def put(ref, t, value):
    ref[pl.ds(t * N, N), :] = value


def at(q, a, b):
    return (q * N + a) * N + b


def node_columns(sv):
    i = lax.broadcasted_iota(jnp.int32, (N, N), 0)
    j = lax.broadcasted_iota(jnp.int32, (N, N), 1)
    s = sv[...]
    edge = jnp.where((i == j) & ((i == 0) | (i == N - 1)), 2.0, 0.0)
    diag = jnp.sum(jnp.where(i == j, s, 0.0) + edge, axis=1, keepdims=True)
    zero = jnp.zeros((N, 128), f32)
    return diag + zero, jnp.sum(s, axis=1, keepdims=True) + zero


def line(x, k, count=N):
    return jnp.broadcast_to(x[k : k + 1], (count, 128))


def pair_sum(x):
    return jnp.concatenate([line(x, b) + x for b in range(N)], axis=0)


def raw(ref, q, a, b):
    return ref[pl.ds(at(0, a, b) * 2 * N + q, N, stride=2), :]


def pack_first(rs_far, coef_far, sv_far, plane_a, plane_b, span_a, span_b, rs, coef, sv, sems):
    copies = [
        pltpu.make_async_copy(src, dst, sems.at[k])
        for k, (src, dst) in enumerate(((sv_far, sv), (coef_far, coef), (rs_far, rs)))
    ]
    for copy in copies:
        copy.start()
    copies[0].wait()
    copies[1].wait()
    mc, _ = node_columns(sv)
    sub = lax.broadcasted_iota(jnp.int32, (N, 128), 0)
    c = [coef[pl.ds(q, 1), :] for q in range(2)]
    scale = [1.0 / (centre * c[q]) for q in range(2)]
    zero = jnp.zeros((N, 128), f32)
    both = jnp.where(sub == 0, c[0], jnp.where(sub == 1, c[1], zero))
    copies[2].wait()

    def value(q, a, b):
        return raw(rs, q, a, b) * scale[q] / ((line(mc, a) + line(mc, b)) + mc)

    _, even_plane, even_span = position()
    for q in range(2):
        for b in range(N):
            put_both(even_plane, plane_a, plane_b, q * N + b, value(q, N - 1, b), value(q, 0, b))
    put(plane_a, 2 * N, both)
    put(plane_b, 2 * N, both)
    for a in range(N):
        put_both(even_span, span_a, span_b, a, value(1, a, N - 1), value(0, a, 0))
    put_both(even_span, span_a, span_b, N, zero + c[1], zero + c[0])


def stiff(u, kk, st, acc):
    for a in range(N):
        lo = u[pl.ds(at(0, a, 0) * N, N * N), :]
        hi = u[pl.ds(at(1, a, 0) * N, N * N), :]
        x = jnp.concatenate([lo, hi], axis=1)
        xh = x.astype(bf16)
        xl = (x - xh.astype(f32)).astype(bf16)
        main = jnp.dot(kk[...], xh, preferred_element_type=f32)
        rest = jnp.dot(kk[pl.ds(0, N * N), :], xl, preferred_element_type=f32)
        y = main[: N * N] + (main[N * N :] + rest)
        acc[pl.ds(at(0, a, 0) * N, N * N), :] = y[:, :128]
        acc[pl.ds(at(1, a, 0) * N, N * N), :] = y[:, 128:]
    for q in range(2):
        for b in range(N):
            us = [tile(u, at(q, j, b)) for j in range(N)]
            for i in range(N):
                t = tile(acc, at(q, i, b))
                for j in range(N):
                    t = t + tile(st, i * N + j) * us[j]
                put(acc, at(q, i, b), t)


def inner_faces(u, coef, acc):
    c = [coef[pl.ds(q, 1), :] for q in range(2)]
    for q in range(2):
        rc = 2.0 / c[q]
        up = 2.0 + pltpu.roll(c[q], 127, 1) * rc
        down = 2.0 + pltpu.roll(c[q], 1, 1) * rc
        for a in range(N):
            base = at(q, a, 0) * N
            first = pl.ds(base, N, stride=N)
            last = pl.ds(base + N - 1, N, stride=N)
            lower, upper = u[first, :], u[last, :]
            acc[last, :] += up * (upper - pltpu.roll(lower, 127, 1))
            acc[first, :] += down * (lower - pltpu.roll(upper, 1, 1))
    w0 = 2.0 + 2.0 * c[1] / c[0]
    w1 = 2.0 + 2.0 * c[0] / c[1]
    for a in range(N):
        d = tile(u, at(0, a, N - 1)) - tile(u, at(1, a, 0))
        put(acc, at(0, a, N - 1), tile(acc, at(0, a, N - 1)) + w0 * d)
        put(acc, at(1, a, 0), tile(acc, at(1, a, 0)) - w1 * d)


def block(ref, q, a):
    return ref[pl.ds(at(q, a, 0) * N, N * N), :]


def set_block(ref, q, a, value):
    ref[pl.ds(at(q, a, 0) * N, N * N), :] = value


def start(rs, coef, sv, g, rt, rb, kk, st, first, part):
    diag, sums = node_columns(sv)
    mbc = pair_sum(diag)
    pairs = pair_sum(sums)
    for a in range(N):
        rb[pl.ds(a * N * N, N * N), :] = pairs + line(sums, a, N * N)
    for i in range(N):
        for j in range(N):
            put(st, i * N + j, jnp.broadcast_to(sv[pl.ds(i, 1), pl.ds(j, 1)], (N, 128)))
    row = lax.broadcasted_iota(jnp.int32, (N * N, N), 0)
    col = lax.broadcasted_iota(jnp.int32, (N * N, N), 1)
    pb = (row // N == col).astype(f32)
    pc = (row % N == col).astype(f32)
    wide = (((1,), (1,)), ((), ()))

    def outer(p):
        ps = jnp.dot(p, sv[...], precision=exact, preferred_element_type=f32)
        return lax.dot_general(ps, p, wide, precision=exact, preferred_element_type=f32)

    i = lax.broadcasted_iota(jnp.int32, (N * N, N * N), 0)
    j = lax.broadcasted_iota(jnp.int32, (N * N, N * N), 1)
    k = jnp.where(i % N == j % N, outer(pb), 0.0) + jnp.where(i // N == j // N, outer(pc), 0.0)
    kh = k.astype(bf16)
    kk[pl.ds(0, N * N), :] = kh
    kk[pl.ds(N * N, N * N), :] = (k - kh.astype(f32)).astype(bf16)
    rc = [1.0 / coef[pl.ds(q, 1), :] for q in range(2)]
    for a in range(N):
        r = 1.0 / (line(diag, a, N * N) + mbc)
        rt[pl.ds(a * N * N, N * N), :] = r
        for q in range(2):
            for b in range(N):
                t = raw(rs, q, a, b) * rc[q]
                put(g, at(q, a, b), t)
                put(first, at(q, a, b), t * r[b * N : (b + 1) * N] * (1.0 / centre))
    stiff(first, kk, st, part)
    inner_faces(first, coef, part)
    for q in range(2):
        for a in range(N):
            r = rt[pl.ds(a * N * N, N * N), :]
            v = (1.0 + keep) * block(first, q, a) + gain2 * r * (block(g, q, a) - block(part, q, a))
            set_block(part, q, a, v)


def middle(coef, g, rt, rb, first, part, plane_a, plane_b, span_a, span_b, it, sums_out):
    plane, even_plane, even_span = position()
    from_n, from_s = both_sides(even_plane, plane_a, plane_b)
    from_e, from_w = both_sides(even_span, span_a, span_b)
    c = [coef[pl.ds(q, 1), :] for q in range(2)]
    it[...] = part[...]
    wn = [2.0 + 2.0 * from_n[pl.ds(2 * N * N + q, 1), :] / c[q] for q in range(2)]
    ws = [2.0 + 2.0 * from_s[pl.ds(2 * N * N + q, 1), :] / c[q] for q in range(2)]
    we = 2.0 + 2.0 * from_e[pl.ds(N * N, 1), :] / c[1]
    ww = 2.0 + 2.0 * from_w[pl.ds(N * N, 1), :] / c[0]

    def add(q, a, b, w, other):
        k = at(q, a, b)
        put(it, k, tile(it, k) - gain2 * tile(rt, a * N + b) * (w * (tile(first, k) - other)))

    for q in range(2):
        for b in range(N):
            add(q, N - 1, b, wn[q], tile(from_n, q * N + b))
            add(q, 0, b, ws[q], tile(from_s, q * N + b))
    for a in range(N):
        add(1, a, N - 1, we, tile(from_e, a))
        add(0, a, 0, ww, tile(from_w, a))
    own = jnp.zeros((N, 128), f32)
    above = jnp.zeros((N, 128), f32)
    below = jnp.zeros((N, 128), f32)
    for q in range(2):
        z = jnp.zeros((N * N, 128), f32)
        for a in range(N):
            z = z + (block(g, q, a) - rb[pl.ds(a * N * N, N * N), :] * block(it, q, a))
        t = z[:N]
        up = tile(it, at(q, N - 1, 0))
        dn = tile(it, at(q, 0, 0))
        for b in range(1, N):
            t = t + z[b * N : (b + 1) * N]
            up = up + tile(it, at(q, N - 1, b))
            dn = dn + tile(it, at(q, 0, b))
        up = (c[q] * wn[q]) * up
        dn = (c[q] * ws[q]) * dn
        own = own + (c[q] * t - (up + dn))
        above = above + up
        below = below + dn
    sub = lax.broadcasted_iota(jnp.int32, (N, 128), 0)

    def total(x):
        return jnp.sum(x, axis=0, keepdims=True)

    stack = jnp.where(sub == 0, total(own), 0.0)
    stack = jnp.where(sub == 1, total(above), stack)
    stack = jnp.where(sub == 2, total(below), stack)
    stack = jnp.where(sub == 3, c[0] + c[1], stack)
    s = jnp.sum(stack, axis=1, keepdims=True)
    lane = lax.broadcasted_iota(jnp.int32, (1, 128), 1)
    means = jnp.where(lane == plane, s[0:1], 0.0)
    means = means + jnp.where(lane == plane + 1, s[1:2], 0.0) + jnp.where(lane == plane - 1, s[2:3], 0.0)
    sub2 = lax.broadcasted_iota(jnp.int32, (2, 128), 0)
    pair = jnp.where(sub2 == 0, means, jnp.where(lane == plane, s[3:4], 0.0))
    sums_out[...] = jnp.broadcast_to(pair[None], sums_out.shape)


def smooth(coef, st, g, rt, kk, it, post, span_a, span_b):
    stiff(it, kk, st, post)
    inner_faces(it, coef, post)
    for q in range(2):
        for a in range(N):
            r = rt[pl.ds(a * N * N, N * N), :] * (1.0 / centre)
            set_block(post, q, a, block(it, q, a) + r * (block(g, q, a) - block(post, q, a)))
    _, _, even_span = position()
    for a in range(N):
        for k, field in enumerate((it, post)):
            put_both(even_span, span_a, span_b, k * N + a, tile(field, at(1, a, N - 1)), tile(field, at(0, a, 0)))


def fold(parts, ready, out):
    total = parts[0] + ready[pl.ds(0, 2), :]
    for k in range(1, parts.shape[0]):
        total = total + parts[k]
    out[...] = jnp.broadcast_to(total[None], out.shape)


def side(coef, rt, it, post_in, span_a, span_b, far_a, far_b, post, plane_a, plane_b, ready):
    _, even_plane, even_span = position()
    from_e, from_w = both_sides(even_span, span_a, span_b)
    got_e, got_w = both_sides(even_span, far_a, far_b)
    c = [coef[pl.ds(q, 1), :] for q in range(2)]
    ce = from_e[pl.ds(N * N, 1), :]
    cw = from_w[pl.ds(N * N, 1), :]
    we = 2.0 + 2.0 * ce / c[1]
    ww = 2.0 + 2.0 * cw / c[0]
    post[...] = post_in[...]
    for a in range(N):
        for q, b, w, got in ((1, N - 1, we, got_e), (0, 0, ww, got_w)):
            k = at(q, a, b)
            r = tile(rt, a * N + b) * (1.0 / centre)
            put(post, k, tile(post, k) - r * (w * (tile(it, k) - tile(got, a))))
    sub = lax.broadcasted_iota(jnp.int32, (N, 128), 0)
    outer = jnp.where(sub == 0, ce, jnp.where(sub == 1, cw, 0.0))
    for q in range(2):
        for b in range(N):
            for k, field in enumerate((it, post)):
                up, down = tile(field, at(q, N - 1, b)), tile(field, at(q, 0, b))
                put_both(even_plane, plane_a, plane_b, 2 * N * k + q * N + b, up, down)
    for k, got in enumerate((got_e, got_w)):
        put_both(even_plane, plane_a, plane_b, 4 * N + k, tile(got, N - 1), tile(got, 0))
    put(plane_a, 4 * N + 2, outer)
    put(plane_b, 4 * N + 2, outer)
    ready[...] = jnp.zeros((N, 128), f32)


def coarse(planes, gains, means):
    lane = lax.broadcasted_iota(jnp.int32, (1, 128), 1)
    before = jnp.where(lane == 0, gains, pltpu.roll(gains, 1, 1))
    diag = penalty * before + (penalty + shift_mass) * gains
    upper = jnp.where(lane < planes - 1, -penalty * gains, 0.0)
    diag = jnp.where(lane < planes, diag, 1.0)
    lower = jnp.where(lane == 0, 0.0, pltpu.roll(upper, 1, 1))
    right = jnp.where(lane < planes, means, 0.0)
    step = 1
    while step < planes:
        inv = 1.0 / diag
        lo = -lower * pltpu.roll(inv, step, 1)
        hi = -upper * pltpu.roll(inv, 128 - step, 1)
        right = right + lo * pltpu.roll(right, step, 1) + hi * pltpu.roll(right, 128 - step, 1)
        diag = diag + lo * pltpu.roll(upper, step, 1) + hi * pltpu.roll(lower, 128 - step, 1)
        lower = lo * pltpu.roll(lower, step, 1)
        upper = hi * pltpu.roll(upper, 128 - step, 1)
        step *= 2
    return right / diag


def finish(planes, per_plane, coef, st, g, rt, rb, kk, it, post, ring, near_a, near_b, span_a, span_b, far_a, far_b, last_a, last_b, out, acc, v):
    plane, even_plane, even_span = position()
    from_n, from_s = both_sides(even_plane, near_a, near_b)
    from_e, from_w = both_sides(even_span, span_a, span_b)
    got_e, got_w = both_sides(even_span, far_a, far_b)
    got_n, got_s = both_sides(even_plane, last_a, last_b)
    scaled = ring[0]
    for k in range(1, ring.shape[0]):
        scaled = scaled + ring[k]
    corr = coarse(planes, scaled[1:2] * (1.0 / per_plane), scaled[0:1] * (1.0 / (per_plane * N * N * N)))

    lane = lax.broadcasted_iota(jnp.int32, (1, 128), 1)

    def pick(k):
        return jnp.sum(jnp.where(lane == k, corr, 0.0), axis=1, keepdims=True) + jnp.zeros((1, 128), f32)

    mid, high, low = pick(plane), pick(plane + 1), pick(plane - 1)
    has_n = (plane < planes - 1).astype(f32)
    has_s = (plane > 0).astype(f32)
    inner = 1.0 / centre
    c = [coef[pl.ds(q, 1), :] for q in range(2)]
    cn = [from_n[pl.ds(2 * N * N + q, 1), :] for q in range(2)]
    cs = [from_s[pl.ds(2 * N * N + q, 1), :] for q in range(2)]
    ce = from_e[pl.ds(N * N, 1), :]
    cw = from_w[pl.ds(N * N, 1), :]
    wn = [2.0 + 2.0 * cn[q] / c[q] for q in range(2)]
    ws = [2.0 + 2.0 * cs[q] / c[q] for q in range(2)]
    we = 2.0 + 2.0 * ce / c[1]
    ww = 2.0 + 2.0 * cw / c[0]

    def r_at(a, b):
        return tile(rt, a * N + b)

    def weight(a, b):
        return 1.0 - inner * r_at(a, b) * tile(rb, a * N + b)

    for q in range(2):
        for a in range(N):
            r = rt[pl.ds(a * N * N, N * N), :]
            set_block(v, q, a, block(post, q, a) + mid * (1.0 - inner * r * rb[pl.ds(a * N * N, N * N), :]))
        for b in range(N):
            for a, w, other, got in ((N - 1, wn[q], high, got_n), (0, ws[q], low, got_s)):
                k = at(q, a, b)
                jump = (tile(it, k) - tile(got, q * N + b)) + (mid - other)
                put(v, k, tile(v, k) - inner * r_at(a, b) * (w * jump))
    stiff(v, kk, st, acc)
    inner_faces(v, coef, acc)

    def add(k, w, other):
        put(acc, k, tile(acc, k) + w * (tile(v, k) - other))

    for q in range(2):
        for a, b0, w, has, got, far, cfar in (
            (N - 1, 0, wn[q], has_n, got_n, high, cn[q]),
            (0, N - 1, ws[q], has_s, got_s, low, cs[q]),
        ):
            back = 2.0 + 2.0 * c[q] / jnp.where(cfar > 0.0, cfar, 1.0)
            for b in range(N):
                k = at(q, a, b)
                jump = (tile(got, q * N + b) - tile(it, k)) + (far - mid)
                other = tile(got, 2 * N + q * N + b) + far * weight(b0, b) - inner * r_at(b0, b) * (back * jump)
                add(k, w, has * other)
    for q, b, far_b, w, got, line, row, cfar in (
        (1, N - 1, 0, we, got_e, 4 * N, 0, ce),
        (0, 0, N - 1, ww, got_w, 4 * N + 1, 1, cw),
    ):
        back = 2.0 + 2.0 * c[q] / cfar
        for a in range(N):
            k = at(q, a, b)
            loss = back * (tile(got, a) - tile(it, k))
            for edge, from_far, other in ((N - 1, got_n, high), (0, got_s, low)):
                if a == edge:
                    wf = 2.0 + 2.0 * from_far[pl.ds((4 * N + 2) * N + row, 1), :] / cfar
                    loss = loss + wf * ((tile(got, a) - tile(from_far, line)) + (mid - other))
            other = tile(got, N + a) + mid * weight(a, far_b) - inner * r_at(a, far_b) * loss
            add(k, w, other)
    for q in range(2):
        for a in range(N):
            r = rt[pl.ds(a * N * N, N * N), :]
            x = block(v, q, a)
            last = x + keep * ((x - block(it, q, a)) - mid) + gain2 * r * (block(g, q, a) - block(acc, q, a))
            for b in range(N):
                out[pl.ds(at(0, a, b) * 2 * N + q, N, stride=2), :] = last[b * N : (b + 1) * N]


def call(kernel, in_kinds, out_shapes, scratch=(), cost=10**6, vmem=24):
    kinds = {"v": pl.BlockSpec(memory_space=pltpu.VMEM), "h": pl.BlockSpec(memory_space=pltpu.HBM)}
    return pl.pallas_call(
        kernel,
        out_shape=out_shapes,
        in_specs=[kinds[k] for k in in_kinds],
        out_specs=[kinds["v"]] * len(out_shapes),
        scratch_shapes=list(scratch),
        compiler_params=pltpu.CompilerParams(vmem_limit_bytes=vmem << 20),
        cost_estimate=pl.CostEstimate(flops=cost, bytes_accessed=10**5, transcendentals=0),
    )


def rows(n, dtype=f32, lanes=128):
    return jax.ShapeDtypeStruct((n, lanes), dtype)


def swap(block_a, block_b, axis, count, periodic):
    first = [(i, i ^ 1) for i in range(count)]
    second = [(i, i + 1) for i in range(1, count - 1, 2)]
    if periodic:
        second.append((count - 1, 0))
    second = second + [(j, i) for i, j in second]
    return lax.ppermute(block_a, axis, first), lax.ppermute(block_b, axis, second)


def solution(mesh):
    n_sfc, n_sub = mesh.shape["sfc"], mesh.shape["sub"]
    ny = 4 if n_sfc % 16 == 0 else 2
    nz = n_sfc // ny
    mesh4 = Mesh(mesh.devices.reshape(ny, nz, n_sub // 2, 2), ("y", "z", "x", "c"))

    def per_device(right_side, coefficient, stiffness):
        rs = right_side.reshape(ROWS, 128)
        coef = coefficient.reshape(2, 128)
        field = rows(ROWS)
        layer, strip = rows((2 * N + 1) * N), rows((N + 1) * N)
        planes_out = call(
            pack_first,
            "hhh",
            [layer, layer, strip, strip],
            [
                pltpu.VMEM((ROWS, 128), f32),
                pltpu.VMEM((2, 128), f32),
                pltpu.VMEM((N, N), f32),
                pltpu.SemaphoreType.DMA((3,)),
            ],
        )(*(pltpu.with_memory_space_constraint(x, pltpu.HBM) for x in (rs, coef, stiffness)))
        near_planes = swap(*planes_out[:2], SFC, n_sfc, False)
        near_spans = swap(*planes_out[2:], SUB, n_sub, True)
        table = rows(N * N * N)
        g, rt, rb, kk, st, first, part = call(
            start, "vvv", [field, table, table, rows(2 * N * N, bf16, N * N), table, field, field], cost=10**9
        )(rs, coef, stiffness)
        it, sums = call(middle, "v" * 10, [field, jax.ShapeDtypeStruct((ny * n_sub, 2, 128), f32)])(
            coef, g, rt, rb, first, part, *near_planes, *near_spans
        )
        near = lax.all_to_all(sums, ("y", "x", "c"), 0, 0)
        post, *spans_out = call(smooth, "vvvvvv", [field, rows(2 * N * N), rows(2 * N * N)], cost=10**9)(
            coef, st, g, rt, kk, it
        )
        far_spans = swap(*spans_out, SUB, n_sub, True)
        tall = rows((4 * N + 3) * N)
        post, *planes_out, ready = call(side, "v" * 8, [field, tall, tall, rows(N)])(
            coef, rt, it, post, *near_spans, *far_spans
        )
        (near,) = call(fold, "vv", [jax.ShapeDtypeStruct((nz, 2, 128), f32)])(near, ready)
        ring = lax.all_to_all(near, "z", 0, 0)
        far_planes = swap(*planes_out, SFC, n_sfc, False)

        def last(*refs):
            finish(n_sfc, float(2 * n_sub * 128), *refs)

        (out,) = call(last, "v" * 17, [field], [pltpu.VMEM((ROWS, 128), f32), pltpu.VMEM((ROWS, 128), f32)])(
            coef, st, g, rt, rb, kk, it, post, ring, *near_planes, *near_spans, *far_spans, *far_planes
        )
        return out.reshape(right_side.shape)

    field_spec = P(None, None, None, SFC, SUB, None)
    return jax.shard_map(
        per_device, mesh=mesh4, in_specs=(field_spec, P(SFC, SUB, None), P()), out_specs=field_spec, check_vma=False
    )
```

```python
import jax
import jax.numpy as jnp
from jax import lax
from jax.experimental import pallas as pl
from jax.experimental.pallas import tpu as pltpu
from jax.sharding import Mesh
from jax.sharding import PartitionSpec as P


N = 8
TILES = 2 * N * N
ROWS = TILES * N
penalty = 4.0
shift_mass = 0.02
centre = 1.25
half = 0.95
rho1 = half / centre
rho2 = 1.0 / (2.0 * centre / half - rho1)
keep = rho2 * rho1
gain2 = 2.0 * rho2 / half
exact = lax.Precision.HIGHEST
f32 = jnp.float32
bf16 = jnp.bfloat16
SFC = ("y", "z")
SUB = ("x", "c")


def plane_index():
    return lax.axis_index("y") * lax.axis_size("z") + lax.axis_index("z")


def tile(ref, t):
    return ref[pl.ds(t * N, N), :]


def put(ref, t, value):
    ref[pl.ds(t * N, N), :] = value


def at(q, a, b):
    return (q * N + a) * N + b


def node_columns(sv):
    i = lax.broadcasted_iota(jnp.int32, (N, N), 0)
    j = lax.broadcasted_iota(jnp.int32, (N, N), 1)
    s = sv[...]
    edge = jnp.where((i == j) & ((i == 0) | (i == N - 1)), 2.0, 0.0)
    diag = jnp.sum(jnp.where(i == j, s, 0.0) + edge, axis=1, keepdims=True)
    zero = jnp.zeros((N, 128), f32)
    return diag + zero, jnp.sum(s, axis=1, keepdims=True) + zero


def line(x, k, count=N):
    return jnp.broadcast_to(x[k : k + 1], (count, 128))


def pair_sum(x):
    return jnp.concatenate([line(x, b) + x for b in range(N)], axis=0)


def raw(ref, q, a, b):
    return ref[pl.ds(at(0, a, b) * 2 * N + q, N, stride=2), :]


def pack_first(rs_far, coef_far, sv_far, to_n, to_s, to_e, to_w, rs, coef, sv, sems):
    copies = [
        pltpu.make_async_copy(src, dst, sems.at[k])
        for k, (src, dst) in enumerate(((sv_far, sv), (coef_far, coef), (rs_far, rs)))
    ]
    for copy in copies:
        copy.start()
    copies[0].wait()
    copies[1].wait()
    mc, _ = node_columns(sv)
    sub = lax.broadcasted_iota(jnp.int32, (N, 128), 0)
    c = [coef[pl.ds(q, 1), :] for q in range(2)]
    scale = [1.0 / (centre * c[q]) for q in range(2)]
    zero = jnp.zeros((N, 128), f32)
    both = jnp.where(sub == 0, c[0], jnp.where(sub == 1, c[1], zero))
    copies[2].wait()

    def value(q, a, b):
        return raw(rs, q, a, b) * scale[q] / ((line(mc, a) + line(mc, b)) + mc)

    for q in range(2):
        for b in range(N):
            put(to_n, q * N + b, value(q, N - 1, b))
            put(to_s, q * N + b, value(q, 0, b))
    put(to_n, 2 * N, both)
    put(to_s, 2 * N, both)
    for a in range(N):
        put(to_e, a, value(1, a, N - 1))
        put(to_w, a, value(0, a, 0))
    put(to_e, N, zero + c[1])
    put(to_w, N, zero + c[0])


def stiff(u, kk, st, acc):
    for a in range(N):
        lo = u[pl.ds(at(0, a, 0) * N, N * N), :]
        hi = u[pl.ds(at(1, a, 0) * N, N * N), :]
        x = jnp.concatenate([lo, hi], axis=1)
        xh = x.astype(bf16)
        xl = (x - xh.astype(f32)).astype(bf16)
        main = jnp.dot(kk[...], xh, preferred_element_type=f32)
        rest = jnp.dot(kk[pl.ds(0, N * N), :], xl, preferred_element_type=f32)
        y = main[: N * N] + (main[N * N :] + rest)
        acc[pl.ds(at(0, a, 0) * N, N * N), :] = y[:, :128]
        acc[pl.ds(at(1, a, 0) * N, N * N), :] = y[:, 128:]
    for q in range(2):
        for b in range(N):
            us = [tile(u, at(q, j, b)) for j in range(N)]
            for i in range(N):
                t = tile(acc, at(q, i, b))
                for j in range(N):
                    t = t + tile(st, i * N + j) * us[j]
                put(acc, at(q, i, b), t)


def inner_faces(u, coef, acc):
    c = [coef[pl.ds(q, 1), :] for q in range(2)]
    for q in range(2):
        rc = 2.0 / c[q]
        up = 2.0 + pltpu.roll(c[q], 127, 1) * rc
        down = 2.0 + pltpu.roll(c[q], 1, 1) * rc
        for a in range(N):
            base = at(q, a, 0) * N
            first = pl.ds(base, N, stride=N)
            last = pl.ds(base + N - 1, N, stride=N)
            lower, upper = u[first, :], u[last, :]
            acc[last, :] += up * (upper - pltpu.roll(lower, 127, 1))
            acc[first, :] += down * (lower - pltpu.roll(upper, 1, 1))
    w0 = 2.0 + 2.0 * c[1] / c[0]
    w1 = 2.0 + 2.0 * c[0] / c[1]
    for a in range(N):
        d = tile(u, at(0, a, N - 1)) - tile(u, at(1, a, 0))
        put(acc, at(0, a, N - 1), tile(acc, at(0, a, N - 1)) + w0 * d)
        put(acc, at(1, a, 0), tile(acc, at(1, a, 0)) - w1 * d)


def block(ref, q, a):
    return ref[pl.ds(at(q, a, 0) * N, N * N), :]


def set_block(ref, q, a, value):
    ref[pl.ds(at(q, a, 0) * N, N * N), :] = value


def start(rs, coef, sv, g, rt, rb, kk, st, first, part):
    diag, sums = node_columns(sv)
    mbc = pair_sum(diag)
    pairs = pair_sum(sums)
    for a in range(N):
        rb[pl.ds(a * N * N, N * N), :] = pairs + line(sums, a, N * N)
    for i in range(N):
        for j in range(N):
            put(st, i * N + j, jnp.broadcast_to(sv[pl.ds(i, 1), pl.ds(j, 1)], (N, 128)))
    row = lax.broadcasted_iota(jnp.int32, (N * N, N), 0)
    col = lax.broadcasted_iota(jnp.int32, (N * N, N), 1)
    pb = (row // N == col).astype(f32)
    pc = (row % N == col).astype(f32)
    wide = (((1,), (1,)), ((), ()))

    def outer(p):
        ps = jnp.dot(p, sv[...], precision=exact, preferred_element_type=f32)
        return lax.dot_general(ps, p, wide, precision=exact, preferred_element_type=f32)

    i = lax.broadcasted_iota(jnp.int32, (N * N, N * N), 0)
    j = lax.broadcasted_iota(jnp.int32, (N * N, N * N), 1)
    k = jnp.where(i % N == j % N, outer(pb), 0.0) + jnp.where(i // N == j // N, outer(pc), 0.0)
    kh = k.astype(bf16)
    kk[pl.ds(0, N * N), :] = kh
    kk[pl.ds(N * N, N * N), :] = (k - kh.astype(f32)).astype(bf16)
    rc = [1.0 / coef[pl.ds(q, 1), :] for q in range(2)]
    for a in range(N):
        r = 1.0 / (line(diag, a, N * N) + mbc)
        rt[pl.ds(a * N * N, N * N), :] = r
        for q in range(2):
            for b in range(N):
                t = raw(rs, q, a, b) * rc[q]
                put(g, at(q, a, b), t)
                put(first, at(q, a, b), t * r[b * N : (b + 1) * N] * (1.0 / centre))
    stiff(first, kk, st, part)
    inner_faces(first, coef, part)
    for q in range(2):
        for a in range(N):
            r = rt[pl.ds(a * N * N, N * N), :]
            v = (1.0 + keep) * block(first, q, a) + gain2 * r * (block(g, q, a) - block(part, q, a))
            set_block(part, q, a, v)


def middle(coef, g, rt, rb, first, part, from_n, from_s, from_e, from_w, it, sums_out):
    plane = plane_index()
    c = [coef[pl.ds(q, 1), :] for q in range(2)]
    it[...] = part[...]
    wn = [2.0 + 2.0 * from_n[pl.ds(2 * N * N + q, 1), :] / c[q] for q in range(2)]
    ws = [2.0 + 2.0 * from_s[pl.ds(2 * N * N + q, 1), :] / c[q] for q in range(2)]
    we = 2.0 + 2.0 * from_e[pl.ds(N * N, 1), :] / c[1]
    ww = 2.0 + 2.0 * from_w[pl.ds(N * N, 1), :] / c[0]

    def add(q, a, b, w, other):
        k = at(q, a, b)
        put(it, k, tile(it, k) - gain2 * tile(rt, a * N + b) * (w * (tile(first, k) - other)))

    for q in range(2):
        for b in range(N):
            add(q, N - 1, b, wn[q], tile(from_n, q * N + b))
            add(q, 0, b, ws[q], tile(from_s, q * N + b))
    for a in range(N):
        add(1, a, N - 1, we, tile(from_e, a))
        add(0, a, 0, ww, tile(from_w, a))
    own = jnp.zeros((N, 128), f32)
    above = jnp.zeros((N, 128), f32)
    below = jnp.zeros((N, 128), f32)
    for q in range(2):
        z = jnp.zeros((N * N, 128), f32)
        for a in range(N):
            z = z + (block(g, q, a) - rb[pl.ds(a * N * N, N * N), :] * block(it, q, a))
        t = z[:N]
        up = tile(it, at(q, N - 1, 0))
        dn = tile(it, at(q, 0, 0))
        for b in range(1, N):
            t = t + z[b * N : (b + 1) * N]
            up = up + tile(it, at(q, N - 1, b))
            dn = dn + tile(it, at(q, 0, b))
        up = (c[q] * wn[q]) * up
        dn = (c[q] * ws[q]) * dn
        own = own + (c[q] * t - (up + dn))
        above = above + up
        below = below + dn
    sub = lax.broadcasted_iota(jnp.int32, (N, 128), 0)

    def total(x):
        return jnp.sum(x, axis=0, keepdims=True)

    stack = jnp.where(sub == 0, total(own), 0.0)
    stack = jnp.where(sub == 1, total(above), stack)
    stack = jnp.where(sub == 2, total(below), stack)
    stack = jnp.where(sub == 3, c[0] + c[1], stack)
    s = jnp.sum(stack, axis=1, keepdims=True)
    lane = lax.broadcasted_iota(jnp.int32, (1, 128), 1)
    means = jnp.where(lane == plane, s[0:1], 0.0)
    means = means + jnp.where(lane == plane + 1, s[1:2], 0.0) + jnp.where(lane == plane - 1, s[2:3], 0.0)
    sub2 = lax.broadcasted_iota(jnp.int32, (2, 128), 0)
    pair = jnp.where(sub2 == 0, means, jnp.where(lane == plane, s[3:4], 0.0))
    sums_out[...] = jnp.broadcast_to(pair[None], sums_out.shape)


def smooth(coef, st, g, rt, kk, it, post, to_e, to_w):
    stiff(it, kk, st, post)
    inner_faces(it, coef, post)
    for q in range(2):
        for a in range(N):
            r = rt[pl.ds(a * N * N, N * N), :] * (1.0 / centre)
            set_block(post, q, a, block(it, q, a) + r * (block(g, q, a) - block(post, q, a)))
    for a in range(N):
        for k, field in enumerate((it, post)):
            put(to_e, k * N + a, tile(field, at(1, a, N - 1)))
            put(to_w, k * N + a, tile(field, at(0, a, 0)))


def fold(parts, out):
    total = parts[0]
    for k in range(1, parts.shape[0]):
        total = total + parts[k]
    out[...] = jnp.broadcast_to(total[None], out.shape)


def side(coef, rt, it, post_in, from_e, from_w, got_e, got_w, post, to_n, to_s):
    c = [coef[pl.ds(q, 1), :] for q in range(2)]
    ce = from_e[pl.ds(N * N, 1), :]
    cw = from_w[pl.ds(N * N, 1), :]
    we = 2.0 + 2.0 * ce / c[1]
    ww = 2.0 + 2.0 * cw / c[0]
    post[...] = post_in[...]
    for a in range(N):
        for q, b, w, got in ((1, N - 1, we, got_e), (0, 0, ww, got_w)):
            k = at(q, a, b)
            r = tile(rt, a * N + b) * (1.0 / centre)
            put(post, k, tile(post, k) - r * (w * (tile(it, k) - tile(got, a))))
    sub = lax.broadcasted_iota(jnp.int32, (N, 128), 0)
    outer = jnp.where(sub == 0, ce, jnp.where(sub == 1, cw, 0.0))
    for a, to in ((N - 1, to_n), (0, to_s)):
        for q in range(2):
            for b in range(N):
                put(to, q * N + b, tile(it, at(q, a, b)))
                put(to, 2 * N + q * N + b, tile(post, at(q, a, b)))
        put(to, 4 * N, tile(got_e, a))
        put(to, 4 * N + 1, tile(got_w, a))
        put(to, 4 * N + 2, outer)


def coarse(planes, gains, means):
    lane = lax.broadcasted_iota(jnp.int32, (1, 128), 1)
    before = jnp.where(lane == 0, gains, pltpu.roll(gains, 1, 1))
    diag = penalty * before + (penalty + shift_mass) * gains
    upper = jnp.where(lane < planes - 1, -penalty * gains, 0.0)
    diag = jnp.where(lane < planes, diag, 1.0)
    lower = jnp.where(lane == 0, 0.0, pltpu.roll(upper, 1, 1))
    right = jnp.where(lane < planes, means, 0.0)
    step = 1
    while step < planes:
        inv = 1.0 / diag
        lo = -lower * pltpu.roll(inv, step, 1)
        hi = -upper * pltpu.roll(inv, 128 - step, 1)
        right = right + lo * pltpu.roll(right, step, 1) + hi * pltpu.roll(right, 128 - step, 1)
        diag = diag + lo * pltpu.roll(upper, step, 1) + hi * pltpu.roll(lower, 128 - step, 1)
        lower = lo * pltpu.roll(lower, step, 1)
        upper = hi * pltpu.roll(upper, 128 - step, 1)
        step *= 2
    return right / diag


def finish(planes, per_plane, coef, st, g, rt, rb, kk, it, post, ring, from_n, from_s, from_e, from_w, got_e, got_w, got_n, got_s, out, acc, v):
    plane = plane_index()
    scaled = ring[0]
    for k in range(1, ring.shape[0]):
        scaled = scaled + ring[k]
    corr = coarse(planes, scaled[1:2] * (1.0 / per_plane), scaled[0:1] * (1.0 / (per_plane * N * N * N)))

    lane = lax.broadcasted_iota(jnp.int32, (1, 128), 1)

    def pick(k):
        return jnp.sum(jnp.where(lane == k, corr, 0.0), axis=1, keepdims=True) + jnp.zeros((1, 128), f32)

    mid, high, low = pick(plane), pick(plane + 1), pick(plane - 1)
    has_n = (plane < planes - 1).astype(f32)
    has_s = (plane > 0).astype(f32)
    inner = 1.0 / centre
    c = [coef[pl.ds(q, 1), :] for q in range(2)]
    cn = [from_n[pl.ds(2 * N * N + q, 1), :] for q in range(2)]
    cs = [from_s[pl.ds(2 * N * N + q, 1), :] for q in range(2)]
    ce = from_e[pl.ds(N * N, 1), :]
    cw = from_w[pl.ds(N * N, 1), :]
    wn = [2.0 + 2.0 * cn[q] / c[q] for q in range(2)]
    ws = [2.0 + 2.0 * cs[q] / c[q] for q in range(2)]
    we = 2.0 + 2.0 * ce / c[1]
    ww = 2.0 + 2.0 * cw / c[0]

    def r_at(a, b):
        return tile(rt, a * N + b)

    def weight(a, b):
        return 1.0 - inner * r_at(a, b) * tile(rb, a * N + b)

    for q in range(2):
        for a in range(N):
            r = rt[pl.ds(a * N * N, N * N), :]
            set_block(v, q, a, block(post, q, a) + mid * (1.0 - inner * r * rb[pl.ds(a * N * N, N * N), :]))
        for b in range(N):
            for a, w, other, got in ((N - 1, wn[q], high, got_n), (0, ws[q], low, got_s)):
                k = at(q, a, b)
                jump = (tile(it, k) - tile(got, q * N + b)) + (mid - other)
                put(v, k, tile(v, k) - inner * r_at(a, b) * (w * jump))
    stiff(v, kk, st, acc)
    inner_faces(v, coef, acc)

    def add(k, w, other):
        put(acc, k, tile(acc, k) + w * (tile(v, k) - other))

    for q in range(2):
        for a, b0, w, has, got, far, cfar in (
            (N - 1, 0, wn[q], has_n, got_n, high, cn[q]),
            (0, N - 1, ws[q], has_s, got_s, low, cs[q]),
        ):
            back = 2.0 + 2.0 * c[q] / jnp.where(cfar > 0.0, cfar, 1.0)
            for b in range(N):
                k = at(q, a, b)
                jump = (tile(got, q * N + b) - tile(it, k)) + (far - mid)
                other = tile(got, 2 * N + q * N + b) + far * weight(b0, b) - inner * r_at(b0, b) * (back * jump)
                add(k, w, has * other)
    for q, b, far_b, w, got, line, row, cfar in (
        (1, N - 1, 0, we, got_e, 4 * N, 0, ce),
        (0, 0, N - 1, ww, got_w, 4 * N + 1, 1, cw),
    ):
        back = 2.0 + 2.0 * c[q] / cfar
        for a in range(N):
            k = at(q, a, b)
            loss = back * (tile(got, a) - tile(it, k))
            for edge, from_far, other in ((N - 1, got_n, high), (0, got_s, low)):
                if a == edge:
                    wf = 2.0 + 2.0 * from_far[pl.ds((4 * N + 2) * N + row, 1), :] / cfar
                    loss = loss + wf * ((tile(got, a) - tile(from_far, line)) + (mid - other))
            other = tile(got, N + a) + mid * weight(a, far_b) - inner * r_at(a, far_b) * loss
            add(k, w, other)
    for q in range(2):
        for a in range(N):
            r = rt[pl.ds(a * N * N, N * N), :]
            x = block(v, q, a)
            last = x + keep * ((x - block(it, q, a)) - mid) + gain2 * r * (block(g, q, a) - block(acc, q, a))
            for b in range(N):
                out[pl.ds(at(0, a, b) * 2 * N + q, N, stride=2), :] = last[b * N : (b + 1) * N]


def call(kernel, in_kinds, out_shapes, scratch=(), cost=10**6, vmem=24):
    kinds = {"v": pl.BlockSpec(memory_space=pltpu.VMEM), "h": pl.BlockSpec(memory_space=pltpu.HBM)}
    return pl.pallas_call(
        kernel,
        out_shape=out_shapes,
        in_specs=[kinds[k] for k in in_kinds],
        out_specs=[kinds["v"]] * len(out_shapes),
        scratch_shapes=list(scratch),
        compiler_params=pltpu.CompilerParams(vmem_limit_bytes=vmem << 20),
        cost_estimate=pl.CostEstimate(flops=cost, bytes_accessed=10**5, transcendentals=0),
    )


def rows(n, dtype=f32, lanes=128):
    return jax.ShapeDtypeStruct((n, lanes), dtype)


def exchange(block_up, block_down, axis, count, periodic):
    up = [(i, i + 1) for i in range(count - 1)]
    if periodic:
        up.append((count - 1, 0))
    down = [(j, i) for i, j in up]
    return lax.ppermute(block_down, axis, down), lax.ppermute(block_up, axis, up)


def solution(mesh):
    n_sfc, n_sub = mesh.shape["sfc"], mesh.shape["sub"]
    ny = 4 if n_sfc % 16 == 0 else 2
    nz = n_sfc // ny
    mesh4 = Mesh(mesh.devices.reshape(ny, nz, n_sub // 2, 2), ("y", "z", "x", "c"))

    def per_device(right_side, coefficient, stiffness):
        rs = right_side.reshape(ROWS, 128)
        coef = coefficient.reshape(2, 128)
        field = rows(ROWS)
        layer, strip = rows((2 * N + 1) * N), rows((N + 1) * N)
        planes_out = call(
            pack_first,
            "hhh",
            [layer, layer, strip, strip],
            [
                pltpu.VMEM((ROWS, 128), f32),
                pltpu.VMEM((2, 128), f32),
                pltpu.VMEM((N, N), f32),
                pltpu.SemaphoreType.DMA((3,)),
            ],
        )(*(pltpu.with_memory_space_constraint(x, pltpu.HBM) for x in (rs, coef, stiffness)))
        near_planes = exchange(*planes_out[:2], SFC, n_sfc, False)
        near_spans = exchange(*planes_out[2:], SUB, n_sub, True)
        table = rows(N * N * N)
        g, rt, rb, kk, st, first, part = call(
            start, "vvv", [field, table, table, rows(2 * N * N, bf16, N * N), table, field, field], cost=10**9
        )(rs, coef, stiffness)
        it, sums = call(middle, "v" * 10, [field, jax.ShapeDtypeStruct((ny * n_sub, 2, 128), f32)])(
            coef, g, rt, rb, first, part, *near_planes, *near_spans
        )
        near = lax.all_to_all(sums, ("y", "x", "c"), 0, 0)
        (near,) = call(fold, "v", [jax.ShapeDtypeStruct((nz, 2, 128), f32)])(near)
        near, it = lax.optimization_barrier((near, it))
        ring = lax.all_to_all(near, "z", 0, 0)
        post, *spans_out = call(smooth, "vvvvvv", [field, rows(2 * N * N), rows(2 * N * N)], cost=10**9)(
            coef, st, g, rt, kk, it
        )
        far_spans = exchange(*spans_out, SUB, n_sub, True)
        tall = rows((4 * N + 3) * N)
        post, *planes_out = call(side, "v" * 8, [field, tall, tall])(coef, rt, it, post, *near_spans, *far_spans)
        far_planes = exchange(*planes_out, SFC, n_sfc, False)

        def last(*refs):
            finish(n_sfc, float(2 * n_sub * 128), *refs)

        (out,) = call(last, "v" * 17, [field], [pltpu.VMEM((ROWS, 128), f32), pltpu.VMEM((ROWS, 128), f32)])(
            coef, st, g, rt, rb, kk, it, post, ring, *near_planes, *near_spans, *far_spans, *far_planes
        )
        return out.reshape(right_side.shape)

    field_spec = P(None, None, None, SFC, SUB, None)
    return jax.shard_map(
        per_device, mesh=mesh4, in_specs=(field_spec, P(SFC, SUB, None), P()), out_specs=field_spec, check_vma=False
    )
```

```python
import jax
import jax.numpy as jnp
from jax import lax
from jax.experimental import pallas as pl
from jax.experimental.pallas import tpu as pltpu
from jax.sharding import Mesh
from jax.sharding import PartitionSpec as P


N = 8
TILES = 2 * N * N
ROWS = TILES * N
penalty = 4.0
shift_mass = 0.02
centre = 1.25
half = 0.95
rho1 = half / centre
rho2 = 1.0 / (2.0 * centre / half - rho1)
keep = rho2 * rho1
gain2 = 2.0 * rho2 / half
exact = lax.Precision.HIGHEST
f32 = jnp.float32
bf16 = jnp.bfloat16
SFC = ("y", "z")
SUB = ("x", "c")


def plane_index():
    return lax.axis_index("y") * lax.axis_size("z") + lax.axis_index("z")


def tile(ref, t):
    return ref[pl.ds(t * N, N), :]


def put(ref, t, value):
    ref[pl.ds(t * N, N), :] = value


def at(q, a, b):
    return (q * N + a) * N + b


def node_columns(sv):
    i = lax.broadcasted_iota(jnp.int32, (N, N), 0)
    j = lax.broadcasted_iota(jnp.int32, (N, N), 1)
    s = sv[...]
    edge = jnp.where((i == j) & ((i == 0) | (i == N - 1)), 2.0, 0.0)
    diag = jnp.sum(jnp.where(i == j, s, 0.0) + edge, axis=1, keepdims=True)
    zero = jnp.zeros((N, 128), f32)
    return diag + zero, jnp.sum(s, axis=1, keepdims=True) + zero


def line(x, k, count=N):
    return jnp.broadcast_to(x[k : k + 1], (count, 128))


def pair_sum(x):
    return jnp.concatenate([line(x, b) + x for b in range(N)], axis=0)


def raw(ref, q, a, b):
    return ref[pl.ds(at(0, a, b) * 2 * N + q, N, stride=2), :]


def pack_first(rs_far, coef_far, sv_far, to_n, to_s, to_e, to_w, rs, coef, sv, sems):
    copies = [
        pltpu.make_async_copy(src, dst, sems.at[k])
        for k, (src, dst) in enumerate(((sv_far, sv), (coef_far, coef), (rs_far, rs)))
    ]
    for copy in copies:
        copy.start()
    copies[0].wait()
    copies[1].wait()
    mc, _ = node_columns(sv)
    sub = lax.broadcasted_iota(jnp.int32, (N, 128), 0)
    c = [coef[pl.ds(q, 1), :] for q in range(2)]
    scale = [1.0 / (centre * c[q]) for q in range(2)]
    zero = jnp.zeros((N, 128), f32)
    both = jnp.where(sub == 0, c[0], jnp.where(sub == 1, c[1], zero))
    copies[2].wait()

    def value(q, a, b):
        return raw(rs, q, a, b) * scale[q] / ((line(mc, a) + line(mc, b)) + mc)

    for q in range(2):
        for b in range(N):
            put(to_n, q * N + b, value(q, N - 1, b))
            put(to_s, q * N + b, value(q, 0, b))
    put(to_n, 2 * N, both)
    put(to_s, 2 * N, both)
    for a in range(N):
        put(to_e, a, value(1, a, N - 1))
        put(to_w, a, value(0, a, 0))
    put(to_e, N, zero + c[1])
    put(to_w, N, zero + c[0])


def stiff(u, kk, st, acc):
    for a in range(N):
        lo = u[pl.ds(at(0, a, 0) * N, N * N), :]
        hi = u[pl.ds(at(1, a, 0) * N, N * N), :]
        x = jnp.concatenate([lo, hi], axis=1)
        xh = x.astype(bf16)
        xl = (x - xh.astype(f32)).astype(bf16)
        main = jnp.dot(kk[...], xh, preferred_element_type=f32)
        rest = jnp.dot(kk[pl.ds(0, N * N), :], xl, preferred_element_type=f32)
        y = main[: N * N] + (main[N * N :] + rest)
        acc[pl.ds(at(0, a, 0) * N, N * N), :] = y[:, :128]
        acc[pl.ds(at(1, a, 0) * N, N * N), :] = y[:, 128:]
    for q in range(2):
        for b in range(N):
            us = [tile(u, at(q, j, b)) for j in range(N)]
            for i in range(N):
                t = tile(acc, at(q, i, b))
                for j in range(N):
                    t = t + tile(st, i * N + j) * us[j]
                put(acc, at(q, i, b), t)


def inner_faces(u, coef, acc):
    c = [coef[pl.ds(q, 1), :] for q in range(2)]
    for q in range(2):
        rc = 2.0 / c[q]
        up = 2.0 + pltpu.roll(c[q], 127, 1) * rc
        down = 2.0 + pltpu.roll(c[q], 1, 1) * rc
        for a in range(N):
            base = at(q, a, 0) * N
            first = pl.ds(base, N, stride=N)
            last = pl.ds(base + N - 1, N, stride=N)
            lower, upper = u[first, :], u[last, :]
            acc[last, :] += up * (upper - pltpu.roll(lower, 127, 1))
            acc[first, :] += down * (lower - pltpu.roll(upper, 1, 1))
    w0 = 2.0 + 2.0 * c[1] / c[0]
    w1 = 2.0 + 2.0 * c[0] / c[1]
    for a in range(N):
        d = tile(u, at(0, a, N - 1)) - tile(u, at(1, a, 0))
        put(acc, at(0, a, N - 1), tile(acc, at(0, a, N - 1)) + w0 * d)
        put(acc, at(1, a, 0), tile(acc, at(1, a, 0)) - w1 * d)


def block(ref, q, a):
    return ref[pl.ds(at(q, a, 0) * N, N * N), :]


def set_block(ref, q, a, value):
    ref[pl.ds(at(q, a, 0) * N, N * N), :] = value


def start(rs, coef, sv, g, rt, rb, kk, st, first, part):
    diag, sums = node_columns(sv)
    mbc = pair_sum(diag)
    pairs = pair_sum(sums)
    for a in range(N):
        rb[pl.ds(a * N * N, N * N), :] = pairs + line(sums, a, N * N)
    for i in range(N):
        for j in range(N):
            put(st, i * N + j, jnp.broadcast_to(sv[pl.ds(i, 1), pl.ds(j, 1)], (N, 128)))
    row = lax.broadcasted_iota(jnp.int32, (N * N, N), 0)
    col = lax.broadcasted_iota(jnp.int32, (N * N, N), 1)
    pb = (row // N == col).astype(f32)
    pc = (row % N == col).astype(f32)
    wide = (((1,), (1,)), ((), ()))

    def outer(p):
        ps = jnp.dot(p, sv[...], precision=exact, preferred_element_type=f32)
        return lax.dot_general(ps, p, wide, precision=exact, preferred_element_type=f32)

    i = lax.broadcasted_iota(jnp.int32, (N * N, N * N), 0)
    j = lax.broadcasted_iota(jnp.int32, (N * N, N * N), 1)
    k = jnp.where(i % N == j % N, outer(pb), 0.0) + jnp.where(i // N == j // N, outer(pc), 0.0)
    kh = k.astype(bf16)
    kk[pl.ds(0, N * N), :] = kh
    kk[pl.ds(N * N, N * N), :] = (k - kh.astype(f32)).astype(bf16)
    rc = [1.0 / coef[pl.ds(q, 1), :] for q in range(2)]
    for a in range(N):
        r = 1.0 / (line(diag, a, N * N) + mbc)
        rt[pl.ds(a * N * N, N * N), :] = r
        for q in range(2):
            for b in range(N):
                t = raw(rs, q, a, b) * rc[q]
                put(g, at(q, a, b), t)
                put(first, at(q, a, b), t * r[b * N : (b + 1) * N] * (1.0 / centre))
    stiff(first, kk, st, part)
    inner_faces(first, coef, part)
    for q in range(2):
        for a in range(N):
            r = rt[pl.ds(a * N * N, N * N), :]
            v = (1.0 + keep) * block(first, q, a) + gain2 * r * (block(g, q, a) - block(part, q, a))
            set_block(part, q, a, v)


def middle(coef, g, rt, rb, first, part, from_n, from_s, from_e, from_w, it, sums_out):
    plane = plane_index()
    c = [coef[pl.ds(q, 1), :] for q in range(2)]
    it[...] = part[...]
    wn = [2.0 + 2.0 * from_n[pl.ds(2 * N * N + q, 1), :] / c[q] for q in range(2)]
    ws = [2.0 + 2.0 * from_s[pl.ds(2 * N * N + q, 1), :] / c[q] for q in range(2)]
    we = 2.0 + 2.0 * from_e[pl.ds(N * N, 1), :] / c[1]
    ww = 2.0 + 2.0 * from_w[pl.ds(N * N, 1), :] / c[0]

    def add(q, a, b, w, other):
        k = at(q, a, b)
        put(it, k, tile(it, k) - gain2 * tile(rt, a * N + b) * (w * (tile(first, k) - other)))

    for q in range(2):
        for b in range(N):
            add(q, N - 1, b, wn[q], tile(from_n, q * N + b))
            add(q, 0, b, ws[q], tile(from_s, q * N + b))
    for a in range(N):
        add(1, a, N - 1, we, tile(from_e, a))
        add(0, a, 0, ww, tile(from_w, a))
    own = jnp.zeros((N, 128), f32)
    above = jnp.zeros((N, 128), f32)
    below = jnp.zeros((N, 128), f32)
    for q in range(2):
        z = jnp.zeros((N * N, 128), f32)
        for a in range(N):
            z = z + (block(g, q, a) - rb[pl.ds(a * N * N, N * N), :] * block(it, q, a))
        t = z[:N]
        up = tile(it, at(q, N - 1, 0))
        dn = tile(it, at(q, 0, 0))
        for b in range(1, N):
            t = t + z[b * N : (b + 1) * N]
            up = up + tile(it, at(q, N - 1, b))
            dn = dn + tile(it, at(q, 0, b))
        up = (c[q] * wn[q]) * up
        dn = (c[q] * ws[q]) * dn
        own = own + (c[q] * t - (up + dn))
        above = above + up
        below = below + dn
    sub = lax.broadcasted_iota(jnp.int32, (N, 128), 0)

    def total(x):
        return jnp.sum(x, axis=0, keepdims=True)

    stack = jnp.where(sub == 0, total(own), 0.0)
    stack = jnp.where(sub == 1, total(above), stack)
    stack = jnp.where(sub == 2, total(below), stack)
    stack = jnp.where(sub == 3, c[0] + c[1], stack)
    s = jnp.sum(stack, axis=1, keepdims=True)
    lane = lax.broadcasted_iota(jnp.int32, (1, 128), 1)
    means = jnp.where(lane == plane, s[0:1], 0.0)
    means = means + jnp.where(lane == plane + 1, s[1:2], 0.0) + jnp.where(lane == plane - 1, s[2:3], 0.0)
    sub2 = lax.broadcasted_iota(jnp.int32, (2, 128), 0)
    pair = jnp.where(sub2 == 0, means, jnp.where(lane == plane, s[3:4], 0.0))
    sums_out[...] = jnp.broadcast_to(pair[None], sums_out.shape)


def smooth(coef, st, g, rt, kk, it, post, to_e, to_w):
    stiff(it, kk, st, post)
    inner_faces(it, coef, post)
    for q in range(2):
        for a in range(N):
            r = rt[pl.ds(a * N * N, N * N), :] * (1.0 / centre)
            set_block(post, q, a, block(it, q, a) + r * (block(g, q, a) - block(post, q, a)))
    for a in range(N):
        for k, field in enumerate((it, post)):
            put(to_e, k * N + a, tile(field, at(1, a, N - 1)))
            put(to_w, k * N + a, tile(field, at(0, a, 0)))


def fold(parts, out):
    total = parts[0]
    for k in range(1, parts.shape[0]):
        total = total + parts[k]
    out[...] = jnp.broadcast_to(total[None], out.shape)


def side(coef, rt, it, post_in, from_e, from_w, got_e, got_w, post, to_n, to_s):
    c = [coef[pl.ds(q, 1), :] for q in range(2)]
    ce = from_e[pl.ds(N * N, 1), :]
    cw = from_w[pl.ds(N * N, 1), :]
    we = 2.0 + 2.0 * ce / c[1]
    ww = 2.0 + 2.0 * cw / c[0]
    post[...] = post_in[...]
    for a in range(N):
        for q, b, w, got in ((1, N - 1, we, got_e), (0, 0, ww, got_w)):
            k = at(q, a, b)
            r = tile(rt, a * N + b) * (1.0 / centre)
            put(post, k, tile(post, k) - r * (w * (tile(it, k) - tile(got, a))))
    sub = lax.broadcasted_iota(jnp.int32, (N, 128), 0)
    outer = jnp.where(sub == 0, ce, jnp.where(sub == 1, cw, 0.0))
    for a, to in ((N - 1, to_n), (0, to_s)):
        for q in range(2):
            for b in range(N):
                put(to, q * N + b, tile(it, at(q, a, b)))
                put(to, 2 * N + q * N + b, tile(post, at(q, a, b)))
        put(to, 4 * N, tile(got_e, a))
        put(to, 4 * N + 1, tile(got_w, a))
        put(to, 4 * N + 2, outer)


def coarse(planes, gains, means):
    lane = lax.broadcasted_iota(jnp.int32, (1, 128), 1)
    before = jnp.where(lane == 0, gains, pltpu.roll(gains, 1, 1))
    diag = penalty * before + (penalty + shift_mass) * gains
    upper = jnp.where(lane < planes - 1, -penalty * gains, 0.0)
    diag = jnp.where(lane < planes, diag, 1.0)
    lower = jnp.where(lane == 0, 0.0, pltpu.roll(upper, 1, 1))
    right = jnp.where(lane < planes, means, 0.0)
    step = 1
    while step < planes:
        inv = 1.0 / diag
        lo = -lower * pltpu.roll(inv, step, 1)
        hi = -upper * pltpu.roll(inv, 128 - step, 1)
        right = right + lo * pltpu.roll(right, step, 1) + hi * pltpu.roll(right, 128 - step, 1)
        diag = diag + lo * pltpu.roll(upper, step, 1) + hi * pltpu.roll(lower, 128 - step, 1)
        lower = lo * pltpu.roll(lower, step, 1)
        upper = hi * pltpu.roll(upper, 128 - step, 1)
        step *= 2
    return right / diag


def tables(rt, rb, kk, st, wt, t1, t7, t0, u, acc):
    lane = lax.broadcasted_iota(jnp.int32, (N * N, 128), 1)
    for a in range(N):
        r = rt[pl.ds(a * N * N, N * N), :] * (1.0 / centre)
        w = 1.0 - r * rb[pl.ds(a * N * N, N * N), :]
        wt[pl.ds(a * N * N, N * N), :] = w
        x = jnp.where(lane == 0, w, 0.0)
        if a == N - 1:
            x = jnp.where(lane == 1, -r, x)
        if a == 0:
            x = jnp.where(lane == 2, -r, x)
        set_block(u, 0, a, x)
        set_block(u, 1, a, jnp.zeros((N * N, 128), f32))
    stiff(u, kk, st, acc)
    for a in range(N):
        x = block(acc, 0, a)
        for k, out in enumerate((t1, t7, t0)):
            out[pl.ds(a * N * N, N * N), :] = jnp.broadcast_to(x[:, k : k + 1], (N * N, 128))


def face_weights(coef, from_n, from_s, from_e, from_w):
    c = [coef[pl.ds(q, 1), :] for q in range(2)]
    cn = [from_n[pl.ds(2 * N * N + q, 1), :] for q in range(2)]
    cs = [from_s[pl.ds(2 * N * N + q, 1), :] for q in range(2)]
    ce = from_e[pl.ds(N * N, 1), :]
    cw = from_w[pl.ds(N * N, 1), :]
    wn = [2.0 + 2.0 * cn[q] / c[q] for q in range(2)]
    ws = [2.0 + 2.0 * cs[q] / c[q] for q in range(2)]
    we = 2.0 + 2.0 * ce / c[1]
    ww = 2.0 + 2.0 * cw / c[0]
    return c, cn, cs, ce, cw, wn, ws, we, ww


def back_weight(own, far):
    return 2.0 + 2.0 * own / jnp.where(far > 0.0, far, 1.0)


def ahead(planes, coef, st, g, rt, kk, it, post, from_n, from_s, from_e, from_w, got_e, got_w, got_n, got_s, base, faces, acc, v):
    plane = plane_index()
    has_n = (plane < planes - 1).astype(f32)
    has_s = (plane > 0).astype(f32)
    inner = 1.0 / centre
    c, cn, cs, ce, cw, wn, ws, we, ww = face_weights(coef, from_n, from_s, from_e, from_w)

    def r_at(a, b):
        return tile(rt, a * N + b)

    v[...] = post[...]
    for q in range(2):
        for b in range(N):
            for a, w, got in ((N - 1, wn[q], got_n), (0, ws[q], got_s)):
                k = at(q, a, b)
                put(v, k, tile(v, k) - inner * r_at(a, b) * (w * (tile(it, k) - tile(got, q * N + b))))
    stiff(v, kk, st, acc)
    inner_faces(v, coef, acc)

    def add(k, w, other):
        put(acc, k, tile(acc, k) + w * (tile(v, k) - other))

    for q in range(2):
        for a, b0, w, has, got, cfar in (
            (N - 1, 0, wn[q], has_n, got_n, cn[q]),
            (0, N - 1, ws[q], has_s, got_s, cs[q]),
        ):
            back = back_weight(c[q], cfar)
            faces[pl.ds((2 if a else 4) + q, 1), :] = w
            faces[pl.ds((6 if a else 8) + q, 1), :] = back
            for b in range(N):
                k = at(q, a, b)
                jump = tile(got, q * N + b) - tile(it, k)
                add(k, w, has * (tile(got, 2 * N + q * N + b) - inner * r_at(b0, b) * (back * jump)))
    for q, b, far_b, w, got, line, row, cfar in (
        (1, N - 1, 0, we, got_e, 4 * N, 0, ce),
        (0, 0, N - 1, ww, got_w, 4 * N + 1, 1, cw),
    ):
        back = back_weight(c[q], cfar)
        faces[pl.ds(row, 1), :] = w
        for a in range(N):
            k = at(q, a, b)
            loss = back * (tile(got, a) - tile(it, k))
            for edge, from_far in ((N - 1, got_n), (0, got_s)):
                if a == edge:
                    wf = 2.0 + 2.0 * from_far[pl.ds((4 * N + 2) * N + row, 1), :] / cfar
                    faces[pl.ds((10 if a else 12) + row, 1), :] = wf
                    loss = loss + wf * (tile(got, a) - tile(from_far, line))
            add(k, w, tile(got, N + a) - inner * r_at(a, far_b) * loss)
    for q in range(2):
        for a in range(N):
            r = rt[pl.ds(a * N * N, N * N), :]
            x = (1.0 + keep) * block(v, q, a) - keep * block(it, q, a)
            set_block(base, q, a, x + gain2 * r * (block(g, q, a) - block(acc, q, a)))


def finish(planes, per_plane, coef, rt, wt, t1, t7, t0, base, faces, ring, out, acc, v):
    scaled = ring[0]
    for k in range(1, ring.shape[0]):
        scaled = scaled + ring[k]
    corr = coarse(planes, scaled[1:2] * (1.0 / per_plane), scaled[0:1] * (1.0 / (per_plane * N * N * N)))
    plane = plane_index()
    lane = lax.broadcasted_iota(jnp.int32, (1, 128), 1)

    def pick(k):
        return jnp.sum(jnp.where(lane == k, corr, 0.0), axis=1, keepdims=True) + jnp.zeros((1, 128), f32)

    mid, high, low = pick(plane), pick(plane + 1), pick(plane - 1)
    has_n = (plane < planes - 1).astype(f32)
    has_s = (plane > 0).astype(f32)
    inner = 1.0 / centre

    def face(k):
        return faces[pl.ds(k, 1), :]

    we, ww = face(0), face(1)
    wn, ws = [face(2), face(3)], [face(4), face(5)]

    def r_at(a, b):
        return tile(rt, a * N + b)

    for q in range(2):
        up, down = wn[q] * (mid - high), ws[q] * (mid - low)
        for a in range(N):
            rows_a = pl.ds(a * N * N, N * N)
            x = mid * wt[rows_a, :]
            if a == N - 1:
                x = x - inner * rt[rows_a, :] * up
            if a == 0:
                x = x - inner * rt[rows_a, :] * down
            set_block(v, q, a, x)
            set_block(acc, q, a, mid * t1[rows_a, :] + up * t7[rows_a, :] + down * t0[rows_a, :])
    inner_faces(v, coef, acc)

    def add(k, w, other):
        put(acc, k, tile(acc, k) + w * (tile(v, k) - other))

    for q in range(2):
        for a, b0, w, has, far in ((N - 1, 0, wn[q], has_n, high), (0, N - 1, ws[q], has_s, low)):
            step = face((6 if a else 8) + q) * (far - mid)
            for b in range(N):
                add(at(q, a, b), w, has * (far * tile(wt, b0 * N + b) - inner * r_at(b0, b) * step))
    for q, b, far_b, w, row in ((1, N - 1, 0, we, 0), (0, 0, N - 1, ww, 1)):
        for a in range(N):
            other = mid * tile(wt, a * N + far_b)
            for edge, far in ((N - 1, high), (0, low)):
                if a == edge:
                    other = other - inner * r_at(a, far_b) * (face((10 if a else 12) + row) * (mid - far))
            add(at(q, a, b), w, other)
    for q in range(2):
        for a in range(N):
            r = rt[pl.ds(a * N * N, N * N), :]
            x = block(base, q, a) + ((1.0 + keep) * block(v, q, a) - keep * mid)
            last = x - gain2 * r * block(acc, q, a)
            for b in range(N):
                out[pl.ds(at(0, a, b) * 2 * N + q, N, stride=2), :] = last[b * N : (b + 1) * N]


def call(kernel, in_kinds, out_shapes, scratch=(), cost=10**6, vmem=24):
    kinds = {"v": pl.BlockSpec(memory_space=pltpu.VMEM), "h": pl.BlockSpec(memory_space=pltpu.HBM)}
    return pl.pallas_call(
        kernel,
        out_shape=out_shapes,
        in_specs=[kinds[k] for k in in_kinds],
        out_specs=[kinds["v"]] * len(out_shapes),
        scratch_shapes=list(scratch),
        compiler_params=pltpu.CompilerParams(vmem_limit_bytes=vmem << 20),
        cost_estimate=pl.CostEstimate(flops=cost, bytes_accessed=10**5, transcendentals=0),
    )


def rows(n, dtype=f32, lanes=128):
    return jax.ShapeDtypeStruct((n, lanes), dtype)


def exchange(block_up, block_down, axis, count, periodic):
    up = [(i, i + 1) for i in range(count - 1)]
    if periodic:
        up.append((count - 1, 0))
    down = [(j, i) for i, j in up]
    return lax.ppermute(block_down, axis, down), lax.ppermute(block_up, axis, up)


def solution(mesh):
    n_sfc, n_sub = mesh.shape["sfc"], mesh.shape["sub"]
    ny = 4 if n_sfc % 16 == 0 else 2
    nz = n_sfc // ny
    mesh4 = Mesh(mesh.devices.reshape(ny, nz, n_sub // 2, 2), ("y", "z", "x", "c"))

    def per_device(right_side, coefficient, stiffness):
        rs = right_side.reshape(ROWS, 128)
        coef = coefficient.reshape(2, 128)
        field = rows(ROWS)
        layer, strip = rows((2 * N + 1) * N), rows((N + 1) * N)
        planes_out = call(
            pack_first,
            "hhh",
            [layer, layer, strip, strip],
            [
                pltpu.VMEM((ROWS, 128), f32),
                pltpu.VMEM((2, 128), f32),
                pltpu.VMEM((N, N), f32),
                pltpu.SemaphoreType.DMA((3,)),
            ],
        )(*(pltpu.with_memory_space_constraint(x, pltpu.HBM) for x in (rs, coef, stiffness)))
        near_planes = exchange(*planes_out[:2], SFC, n_sfc, False)
        near_spans = exchange(*planes_out[2:], SUB, n_sub, True)
        table = rows(N * N * N)
        g, rt, rb, kk, st, first, part = call(
            start, "vvv", [field, table, table, rows(2 * N * N, bf16, N * N), table, field, field], cost=10**9
        )(rs, coef, stiffness)
        it, sums = call(middle, "v" * 10, [field, jax.ShapeDtypeStruct((ny * n_sub, 2, 128), f32)])(
            coef, g, rt, rb, first, part, *near_planes, *near_spans
        )
        near = lax.all_to_all(sums, ("y", "x", "c"), 0, 0)
        (near,) = call(fold, "v", [jax.ShapeDtypeStruct((nz, 2, 128), f32)])(near)
        near, it = lax.optimization_barrier((near, it))
        ring = lax.all_to_all(near, "z", 0, 0)
        post, *spans_out = call(smooth, "vvvvvv", [field, rows(2 * N * N), rows(2 * N * N)], cost=10**9)(
            coef, st, g, rt, kk, it
        )
        far_spans = exchange(*spans_out, SUB, n_sub, True)
        tall = rows((4 * N + 3) * N)
        post, *planes_out = call(side, "v" * 8, [field, tall, tall])(coef, rt, it, post, *near_spans, *far_spans)
        far_planes = exchange(*planes_out, SFC, n_sfc, False)

        scratch = [pltpu.VMEM((ROWS, 128), f32), pltpu.VMEM((ROWS, 128), f32)]
        parts = call(tables, "vvvv", [table] * 4, scratch)(rt, rb, kk, st)

        def early(*refs):
            ahead(n_sfc, *refs)

        def last(*refs):
            finish(n_sfc, float(2 * n_sub * 128), *refs)

        base, faces = call(early, "v" * 15, [field, rows(2 * N)], scratch)(
            coef, st, g, rt, kk, it, post, *near_planes, *near_spans, *far_spans, *far_planes
        )
        (out,) = call(last, "v" * 9, [field], scratch)(coef, rt, *parts, base, faces, ring)
        return out.reshape(right_side.shape)

    field_spec = P(None, None, None, SFC, SUB, None)
    return jax.shard_map(
        per_device, mesh=mesh4, in_specs=(field_spec, P(SFC, SUB, None), P()), out_specs=field_spec, check_vma=False
    )
```

```python
import jax
import jax.numpy as jnp
from jax import lax
from jax.experimental import pallas as pl
from jax.experimental.pallas import tpu as pltpu
from jax.sharding import Mesh
from jax.sharding import PartitionSpec as P


N = 8
TILES = 2 * N * N
ROWS = TILES * N
penalty = 4.0
shift_mass = 0.02
centre = 1.25
half = 0.95
rho1 = half / centre
rho2 = 1.0 / (2.0 * centre / half - rho1)
keep = rho2 * rho1
gain2 = 2.0 * rho2 / half
exact = lax.Precision.HIGHEST
f32 = jnp.float32
bf16 = jnp.bfloat16
SFC = ("y", "z")
SUB = ("x", "c")


def plane_index():
    return lax.axis_index("y") * lax.axis_size("z") + lax.axis_index("z")


def tile(ref, t):
    return ref[pl.ds(t * N, N), :]


def put(ref, t, value):
    ref[pl.ds(t * N, N), :] = value


def at(q, a, b):
    return (q * N + a) * N + b


def node_columns(sv):
    i = lax.broadcasted_iota(jnp.int32, (N, N), 0)
    j = lax.broadcasted_iota(jnp.int32, (N, N), 1)
    s = sv[...]
    edge = jnp.where((i == j) & ((i == 0) | (i == N - 1)), 2.0, 0.0)
    diag = jnp.sum(jnp.where(i == j, s, 0.0) + edge, axis=1, keepdims=True)
    zero = jnp.zeros((N, 128), f32)
    return diag + zero, jnp.sum(s, axis=1, keepdims=True) + zero


def line(x, k, count=N):
    return jnp.broadcast_to(x[k : k + 1], (count, 128))


def pair_sum(x):
    return jnp.concatenate([line(x, b) + x for b in range(N)], axis=0)


def raw(ref, q, a, b):
    return ref[pl.ds(at(0, a, b) * 2 * N + q, N, stride=2), :]


def pack_first(rs_far, coef_far, sv_far, to_n, to_s, to_e, to_w, rs, coef, sv, sems):
    copies = [
        pltpu.make_async_copy(src, dst, sems.at[k])
        for k, (src, dst) in enumerate(((sv_far, sv), (coef_far, coef), (rs_far, rs)))
    ]
    for copy in copies:
        copy.start()
    copies[0].wait()
    copies[1].wait()
    mc, _ = node_columns(sv)
    sub = lax.broadcasted_iota(jnp.int32, (N, 128), 0)
    c = [coef[pl.ds(q, 1), :] for q in range(2)]
    scale = [1.0 / (centre * c[q]) for q in range(2)]
    zero = jnp.zeros((N, 128), f32)
    both = jnp.where(sub == 0, c[0], jnp.where(sub == 1, c[1], zero))
    copies[2].wait()

    def value(q, a, b):
        return raw(rs, q, a, b) * scale[q] / ((line(mc, a) + line(mc, b)) + mc)

    for q in range(2):
        for b in range(N):
            put(to_n, q * N + b, value(q, N - 1, b))
            put(to_s, q * N + b, value(q, 0, b))
    put(to_n, 2 * N, both)
    put(to_s, 2 * N, both)
    for a in range(N):
        put(to_e, a, value(1, a, N - 1))
        put(to_w, a, value(0, a, 0))
    put(to_e, N, zero + c[1])
    put(to_w, N, zero + c[0])


def stiff(u, kk, st, acc):
    for a in range(N):
        lo = u[pl.ds(at(0, a, 0) * N, N * N), :]
        hi = u[pl.ds(at(1, a, 0) * N, N * N), :]
        x = jnp.concatenate([lo, hi], axis=1)
        xh = x.astype(bf16)
        xl = (x - xh.astype(f32)).astype(bf16)
        main = jnp.dot(kk[...], xh, preferred_element_type=f32)
        rest = jnp.dot(kk[pl.ds(0, N * N), :], xl, preferred_element_type=f32)
        y = main[: N * N] + (main[N * N :] + rest)
        acc[pl.ds(at(0, a, 0) * N, N * N), :] = y[:, :128]
        acc[pl.ds(at(1, a, 0) * N, N * N), :] = y[:, 128:]
    for q in range(2):
        for b in range(N):
            us = [tile(u, at(q, j, b)) for j in range(N)]
            for i in range(N):
                t = tile(acc, at(q, i, b))
                for j in range(N):
                    t = t + tile(st, i * N + j) * us[j]
                put(acc, at(q, i, b), t)


def inner_faces(u, coef, acc):
    c = [coef[pl.ds(q, 1), :] for q in range(2)]
    for q in range(2):
        rc = 2.0 / c[q]
        up = 2.0 + pltpu.roll(c[q], 127, 1) * rc
        down = 2.0 + pltpu.roll(c[q], 1, 1) * rc
        for a in range(N):
            base = at(q, a, 0) * N
            first = pl.ds(base, N, stride=N)
            last = pl.ds(base + N - 1, N, stride=N)
            lower, upper = u[first, :], u[last, :]
            acc[last, :] += up * (upper - pltpu.roll(lower, 127, 1))
            acc[first, :] += down * (lower - pltpu.roll(upper, 1, 1))
    w0 = 2.0 + 2.0 * c[1] / c[0]
    w1 = 2.0 + 2.0 * c[0] / c[1]
    for a in range(N):
        d = tile(u, at(0, a, N - 1)) - tile(u, at(1, a, 0))
        put(acc, at(0, a, N - 1), tile(acc, at(0, a, N - 1)) + w0 * d)
        put(acc, at(1, a, 0), tile(acc, at(1, a, 0)) - w1 * d)


def block(ref, q, a):
    return ref[pl.ds(at(q, a, 0) * N, N * N), :]


def set_block(ref, q, a, value):
    ref[pl.ds(at(q, a, 0) * N, N * N), :] = value


def start(rs, coef, sv, g, rt, rb, kk, st, first, part):
    diag, sums = node_columns(sv)
    mbc = pair_sum(diag)
    pairs = pair_sum(sums)
    for a in range(N):
        rb[pl.ds(a * N * N, N * N), :] = pairs + line(sums, a, N * N)
    for i in range(N):
        for j in range(N):
            put(st, i * N + j, jnp.broadcast_to(sv[pl.ds(i, 1), pl.ds(j, 1)], (N, 128)))
    row = lax.broadcasted_iota(jnp.int32, (N * N, N), 0)
    col = lax.broadcasted_iota(jnp.int32, (N * N, N), 1)
    pb = (row // N == col).astype(f32)
    pc = (row % N == col).astype(f32)
    wide = (((1,), (1,)), ((), ()))

    def outer(p):
        ps = jnp.dot(p, sv[...], precision=exact, preferred_element_type=f32)
        return lax.dot_general(ps, p, wide, precision=exact, preferred_element_type=f32)

    i = lax.broadcasted_iota(jnp.int32, (N * N, N * N), 0)
    j = lax.broadcasted_iota(jnp.int32, (N * N, N * N), 1)
    k = jnp.where(i % N == j % N, outer(pb), 0.0) + jnp.where(i // N == j // N, outer(pc), 0.0)
    kh = k.astype(bf16)
    kk[pl.ds(0, N * N), :] = kh
    kk[pl.ds(N * N, N * N), :] = (k - kh.astype(f32)).astype(bf16)
    rc = [1.0 / coef[pl.ds(q, 1), :] for q in range(2)]
    for a in range(N):
        r = 1.0 / (line(diag, a, N * N) + mbc)
        rt[pl.ds(a * N * N, N * N), :] = r
        for q in range(2):
            for b in range(N):
                t = raw(rs, q, a, b) * rc[q]
                put(g, at(q, a, b), t)
                put(first, at(q, a, b), t * r[b * N : (b + 1) * N] * (1.0 / centre))
    stiff(first, kk, st, part)
    inner_faces(first, coef, part)
    for q in range(2):
        for a in range(N):
            r = rt[pl.ds(a * N * N, N * N), :]
            v = (1.0 + keep) * block(first, q, a) + gain2 * r * (block(g, q, a) - block(part, q, a))
            set_block(part, q, a, v)


def middle(coef, g, rt, rb, first, part, from_n, from_s, from_e, from_w, it, sums_out):
    plane = plane_index()
    c = [coef[pl.ds(q, 1), :] for q in range(2)]
    it[...] = part[...]
    wn = [2.0 + 2.0 * from_n[pl.ds(2 * N * N + q, 1), :] / c[q] for q in range(2)]
    ws = [2.0 + 2.0 * from_s[pl.ds(2 * N * N + q, 1), :] / c[q] for q in range(2)]
    we = 2.0 + 2.0 * from_e[pl.ds(N * N, 1), :] / c[1]
    ww = 2.0 + 2.0 * from_w[pl.ds(N * N, 1), :] / c[0]

    def add(q, a, b, w, other):
        k = at(q, a, b)
        put(it, k, tile(it, k) - gain2 * tile(rt, a * N + b) * (w * (tile(first, k) - other)))

    for q in range(2):
        for b in range(N):
            add(q, N - 1, b, wn[q], tile(from_n, q * N + b))
            add(q, 0, b, ws[q], tile(from_s, q * N + b))
    for a in range(N):
        add(1, a, N - 1, we, tile(from_e, a))
        add(0, a, 0, ww, tile(from_w, a))
    own = jnp.zeros((N, 128), f32)
    above = jnp.zeros((N, 128), f32)
    below = jnp.zeros((N, 128), f32)
    for q in range(2):
        z = jnp.zeros((N * N, 128), f32)
        for a in range(N):
            z = z + (block(g, q, a) - rb[pl.ds(a * N * N, N * N), :] * block(it, q, a))
        t = z[:N]
        up = tile(it, at(q, N - 1, 0))
        dn = tile(it, at(q, 0, 0))
        for b in range(1, N):
            t = t + z[b * N : (b + 1) * N]
            up = up + tile(it, at(q, N - 1, b))
            dn = dn + tile(it, at(q, 0, b))
        up = (c[q] * wn[q]) * up
        dn = (c[q] * ws[q]) * dn
        own = own + (c[q] * t - (up + dn))
        above = above + up
        below = below + dn
    sub = lax.broadcasted_iota(jnp.int32, (N, 128), 0)

    def total(x):
        return jnp.sum(x, axis=0, keepdims=True)

    stack = jnp.where(sub == 0, total(own), 0.0)
    stack = jnp.where(sub == 1, total(above), stack)
    stack = jnp.where(sub == 2, total(below), stack)
    stack = jnp.where(sub == 3, c[0] + c[1], stack)
    s = jnp.sum(stack, axis=1, keepdims=True)
    lane = lax.broadcasted_iota(jnp.int32, (1, 128), 1)
    means = jnp.where(lane == plane, s[0:1], 0.0)
    means = means + jnp.where(lane == plane + 1, s[1:2], 0.0) + jnp.where(lane == plane - 1, s[2:3], 0.0)
    sub2 = lax.broadcasted_iota(jnp.int32, (2, 128), 0)
    pair = jnp.where(sub2 == 0, means, jnp.where(lane == plane, s[3:4], 0.0))
    sums_out[...] = jnp.broadcast_to(pair[None], sums_out.shape)


def smooth(coef, st, g, rt, kk, it, post, to_e, to_w):
    stiff(it, kk, st, post)
    inner_faces(it, coef, post)
    for q in range(2):
        for a in range(N):
            r = rt[pl.ds(a * N * N, N * N), :] * (1.0 / centre)
            set_block(post, q, a, block(it, q, a) + r * (block(g, q, a) - block(post, q, a)))
    for a in range(N):
        for k, field in enumerate((it, post)):
            put(to_e, k * N + a, tile(field, at(1, a, N - 1)))
            put(to_w, k * N + a, tile(field, at(0, a, 0)))


def fold(parts, out):
    total = parts[0]
    for k in range(1, parts.shape[0]):
        total = total + parts[k]
    out[...] = jnp.broadcast_to(total[None], out.shape)


def side(coef, rt, it, post_in, from_e, from_w, got_e, got_w, post, to_n, to_s):
    c = [coef[pl.ds(q, 1), :] for q in range(2)]
    ce = from_e[pl.ds(N * N, 1), :]
    cw = from_w[pl.ds(N * N, 1), :]
    we = 2.0 + 2.0 * ce / c[1]
    ww = 2.0 + 2.0 * cw / c[0]
    post[...] = post_in[...]
    for a in range(N):
        for q, b, w, got in ((1, N - 1, we, got_e), (0, 0, ww, got_w)):
            k = at(q, a, b)
            r = tile(rt, a * N + b) * (1.0 / centre)
            put(post, k, tile(post, k) - r * (w * (tile(it, k) - tile(got, a))))
    sub = lax.broadcasted_iota(jnp.int32, (N, 128), 0)
    outer = jnp.where(sub == 0, ce, jnp.where(sub == 1, cw, 0.0))
    for a, to in ((N - 1, to_n), (0, to_s)):
        for q in range(2):
            for b in range(N):
                put(to, q * N + b, tile(it, at(q, a, b)))
                put(to, 2 * N + q * N + b, tile(post, at(q, a, b)))
        put(to, 4 * N, tile(got_e, a))
        put(to, 4 * N + 1, tile(got_w, a))
        put(to, 4 * N + 2, outer)


def coarse(planes, gains, means):
    lane = lax.broadcasted_iota(jnp.int32, (1, 128), 1)
    before = jnp.where(lane == 0, gains, pltpu.roll(gains, 1, 1))
    diag = penalty * before + (penalty + shift_mass) * gains
    upper = jnp.where(lane < planes - 1, -penalty * gains, 0.0)
    diag = jnp.where(lane < planes, diag, 1.0)
    lower = jnp.where(lane == 0, 0.0, pltpu.roll(upper, 1, 1))
    right = jnp.where(lane < planes, means, 0.0)
    step = 1
    while step < planes:
        inv = 1.0 / diag
        lo = -lower * pltpu.roll(inv, step, 1)
        hi = -upper * pltpu.roll(inv, 128 - step, 1)
        right = right + lo * pltpu.roll(right, step, 1) + hi * pltpu.roll(right, 128 - step, 1)
        diag = diag + lo * pltpu.roll(upper, step, 1) + hi * pltpu.roll(lower, 128 - step, 1)
        lower = lo * pltpu.roll(lower, step, 1)
        upper = hi * pltpu.roll(upper, 128 - step, 1)
        step *= 2
    return right / diag


def tables(rt, rb, kk, st, wt, t1, t7, t0, u, acc):
    lane = lax.broadcasted_iota(jnp.int32, (N * N, 128), 1)
    for a in range(N):
        r = rt[pl.ds(a * N * N, N * N), :] * (1.0 / centre)
        w = 1.0 - r * rb[pl.ds(a * N * N, N * N), :]
        wt[pl.ds(a * N * N, N * N), :] = w
        x = jnp.where(lane == 0, w, 0.0)
        if a == N - 1:
            x = jnp.where(lane == 1, -r, x)
        if a == 0:
            x = jnp.where(lane == 2, -r, x)
        set_block(u, 0, a, x)
        set_block(u, 1, a, jnp.zeros((N * N, 128), f32))
    stiff(u, kk, st, acc)
    for a in range(N):
        x = block(acc, 0, a)
        for k, out in enumerate((t1, t7, t0)):
            out[pl.ds(a * N * N, N * N), :] = jnp.broadcast_to(x[:, k : k + 1], (N * N, 128))


def face_weights(coef, from_n, from_s, from_e, from_w):
    c = [coef[pl.ds(q, 1), :] for q in range(2)]
    cn = [from_n[pl.ds(2 * N * N + q, 1), :] for q in range(2)]
    cs = [from_s[pl.ds(2 * N * N + q, 1), :] for q in range(2)]
    ce = from_e[pl.ds(N * N, 1), :]
    cw = from_w[pl.ds(N * N, 1), :]
    wn = [2.0 + 2.0 * cn[q] / c[q] for q in range(2)]
    ws = [2.0 + 2.0 * cs[q] / c[q] for q in range(2)]
    we = 2.0 + 2.0 * ce / c[1]
    ww = 2.0 + 2.0 * cw / c[0]
    return c, cn, cs, ce, cw, wn, ws, we, ww


def back_weight(own, far):
    return 2.0 + 2.0 * own / jnp.where(far > 0.0, far, 1.0)


def ahead(planes, coef, st, g, rt, kk, it, post, from_n, from_s, from_e, from_w, got_e, got_w, got_n, got_s, base, faces, acc, v):
    plane = plane_index()
    has_n = (plane < planes - 1).astype(f32)
    has_s = (plane > 0).astype(f32)
    inner = 1.0 / centre
    c, cn, cs, ce, cw, wn, ws, we, ww = face_weights(coef, from_n, from_s, from_e, from_w)

    def r_at(a, b):
        return tile(rt, a * N + b)

    v[...] = post[...]
    for q in range(2):
        for b in range(N):
            for a, w, got in ((N - 1, wn[q], got_n), (0, ws[q], got_s)):
                k = at(q, a, b)
                put(v, k, tile(v, k) - inner * r_at(a, b) * (w * (tile(it, k) - tile(got, q * N + b))))
    stiff(v, kk, st, acc)
    inner_faces(v, coef, acc)

    def add(k, w, other):
        put(acc, k, tile(acc, k) + w * (tile(v, k) - other))

    for q in range(2):
        for a, b0, w, has, got, cfar in (
            (N - 1, 0, wn[q], has_n, got_n, cn[q]),
            (0, N - 1, ws[q], has_s, got_s, cs[q]),
        ):
            back = back_weight(c[q], cfar)
            faces[pl.ds((2 if a else 4) + q, 1), :] = w
            faces[pl.ds((6 if a else 8) + q, 1), :] = back
            for b in range(N):
                k = at(q, a, b)
                jump = tile(got, q * N + b) - tile(it, k)
                add(k, w, has * (tile(got, 2 * N + q * N + b) - inner * r_at(b0, b) * (back * jump)))
    for q, b, far_b, w, got, line, row, cfar in (
        (1, N - 1, 0, we, got_e, 4 * N, 0, ce),
        (0, 0, N - 1, ww, got_w, 4 * N + 1, 1, cw),
    ):
        back = back_weight(c[q], cfar)
        faces[pl.ds(row, 1), :] = w
        for a in range(N):
            k = at(q, a, b)
            loss = back * (tile(got, a) - tile(it, k))
            for edge, from_far in ((N - 1, got_n), (0, got_s)):
                if a == edge:
                    wf = 2.0 + 2.0 * from_far[pl.ds((4 * N + 2) * N + row, 1), :] / cfar
                    faces[pl.ds((10 if a else 12) + row, 1), :] = wf
                    loss = loss + wf * (tile(got, a) - tile(from_far, line))
            add(k, w, tile(got, N + a) - inner * r_at(a, far_b) * loss)
    for q in range(2):
        for a in range(N):
            r = rt[pl.ds(a * N * N, N * N), :]
            x = (1.0 + keep) * block(v, q, a) - keep * block(it, q, a)
            set_block(base, q, a, x + gain2 * r * (block(g, q, a) - block(acc, q, a)))


def finish(planes, per_plane, coef, rt, wt, t1, t7, t0, base, faces, ring, out, acc, v):
    scaled = ring[0]
    for k in range(1, ring.shape[0]):
        scaled = scaled + ring[k]
    corr = coarse(planes, scaled[1:2] * (1.0 / per_plane), scaled[0:1] * (1.0 / (per_plane * N * N * N)))
    plane = plane_index()
    lane = lax.broadcasted_iota(jnp.int32, (1, 128), 1)

    def pick(k):
        return jnp.sum(jnp.where(lane == k, corr, 0.0), axis=1, keepdims=True) + jnp.zeros((1, 128), f32)

    mid, high, low = pick(plane), pick(plane + 1), pick(plane - 1)
    has_n = (plane < planes - 1).astype(f32)
    has_s = (plane > 0).astype(f32)
    inner = 1.0 / centre

    def face(k):
        return faces[pl.ds(k, 1), :]

    we, ww = face(0), face(1)
    wn, ws = [face(2), face(3)], [face(4), face(5)]

    def r_at(a, b):
        return tile(rt, a * N + b)

    for q in range(2):
        up, down = wn[q] * (mid - high), ws[q] * (mid - low)
        for a in range(N):
            rows_a = pl.ds(a * N * N, N * N)
            x = mid * wt[rows_a, :]
            if a == N - 1:
                x = x - inner * rt[rows_a, :] * up
            if a == 0:
                x = x - inner * rt[rows_a, :] * down
            set_block(v, q, a, x)
            set_block(acc, q, a, mid * t1[rows_a, :] + up * t7[rows_a, :] + down * t0[rows_a, :])
    inner_faces(v, coef, acc)

    def add(k, w, other):
        put(acc, k, tile(acc, k) + w * (tile(v, k) - other))

    for q in range(2):
        for a, b0, w, has, far in ((N - 1, 0, wn[q], has_n, high), (0, N - 1, ws[q], has_s, low)):
            step = face((6 if a else 8) + q) * (far - mid)
            for b in range(N):
                add(at(q, a, b), w, has * (far * tile(wt, b0 * N + b) - inner * r_at(b0, b) * step))
    for q, b, far_b, w, row in ((1, N - 1, 0, we, 0), (0, 0, N - 1, ww, 1)):
        for a in range(N):
            other = mid * tile(wt, a * N + far_b)
            for edge, far in ((N - 1, high), (0, low)):
                if a == edge:
                    other = other - inner * r_at(a, far_b) * (face((10 if a else 12) + row) * (mid - far))
            add(at(q, a, b), w, other)
    for q in range(2):
        for a in range(N):
            r = rt[pl.ds(a * N * N, N * N), :]
            x = block(base, q, a) + ((1.0 + keep) * block(v, q, a) - keep * mid)
            last = x - gain2 * r * block(acc, q, a)
            for b in range(N):
                out[pl.ds(at(0, a, b) * 2 * N + q, N, stride=2), :] = last[b * N : (b + 1) * N]


def call(kernel, in_kinds, out_shapes, scratch=(), cost=10**6, vmem=24):
    kinds = {"v": pl.BlockSpec(memory_space=pltpu.VMEM), "h": pl.BlockSpec(memory_space=pltpu.HBM)}
    return pl.pallas_call(
        kernel,
        out_shape=out_shapes,
        in_specs=[kinds[k] for k in in_kinds],
        out_specs=[kinds["v"]] * len(out_shapes),
        scratch_shapes=list(scratch),
        compiler_params=pltpu.CompilerParams(vmem_limit_bytes=vmem << 20),
        cost_estimate=pl.CostEstimate(flops=cost, bytes_accessed=10**5, transcendentals=0),
    )


def rows(n, dtype=f32, lanes=128):
    return jax.ShapeDtypeStruct((n, lanes), dtype)


def exchange(block_up, block_down, axis, count, periodic):
    up = [(i, i + 1) for i in range(count - 1)]
    if periodic:
        up.append((count - 1, 0))
    down = [(j, i) for i, j in up]
    return lax.ppermute(block_down, axis, down), lax.ppermute(block_up, axis, up)


def solution(mesh):
    n_sfc, n_sub = mesh.shape["sfc"], mesh.shape["sub"]
    ny = 4 if n_sfc % 16 == 0 else 2
    nz = n_sfc // ny
    mesh4 = Mesh(mesh.devices.reshape(ny, nz, n_sub // 2, 2), ("y", "z", "x", "c"))

    def per_device(right_side, coefficient, stiffness):
        rs = right_side.reshape(ROWS, 128)
        coef = coefficient.reshape(2, 128)
        field = rows(ROWS)
        layer, strip = rows((2 * N + 1) * N), rows((N + 1) * N)
        planes_out = call(
            pack_first,
            "hhh",
            [layer, layer, strip, strip],
            [
                pltpu.VMEM((ROWS, 128), f32),
                pltpu.VMEM((2, 128), f32),
                pltpu.VMEM((N, N), f32),
                pltpu.SemaphoreType.DMA((3,)),
            ],
        )(*(pltpu.with_memory_space_constraint(x, pltpu.HBM) for x in (rs, coef, stiffness)))
        near_planes = exchange(*planes_out[:2], SFC, n_sfc, False)
        near_spans = exchange(*planes_out[2:], SUB, n_sub, True)
        table = rows(N * N * N)
        g, rt, rb, kk, st, first, part = call(
            start, "vvv", [field, table, table, rows(2 * N * N, bf16, N * N), table, field, field], cost=10**9
        )(rs, coef, stiffness)
        it, sums = call(middle, "v" * 10, [field, jax.ShapeDtypeStruct((ny * n_sub, 2, 128), f32)])(
            coef, g, rt, rb, first, part, *near_planes, *near_spans
        )
        near = lax.all_to_all(sums, ("y", "x", "c"), 0, 0)
        (near,) = call(fold, "v", [jax.ShapeDtypeStruct((nz, 2, 128), f32)])(near)
        near, it = lax.optimization_barrier((near, it))
        turned = [(k + nz // 2) % nz for k in range(nz)]
        ring = lax.all_to_all(near, "z", 0, 0, axis_index_groups=[turned])
        post, *spans_out = call(smooth, "vvvvvv", [field, rows(2 * N * N), rows(2 * N * N)], cost=10**9)(
            coef, st, g, rt, kk, it
        )
        far_spans = exchange(*spans_out, SUB, n_sub, True)
        tall = rows((4 * N + 3) * N)
        post, *planes_out = call(side, "v" * 8, [field, tall, tall])(coef, rt, it, post, *near_spans, *far_spans)
        far_planes = exchange(*planes_out, SFC, n_sfc, False)

        scratch = [pltpu.VMEM((ROWS, 128), f32), pltpu.VMEM((ROWS, 128), f32)]
        parts = call(tables, "vvvv", [table] * 4, scratch)(rt, rb, kk, st)

        def early(*refs):
            ahead(n_sfc, *refs)

        def last(*refs):
            finish(n_sfc, float(2 * n_sub * 128), *refs)

        base, faces = call(early, "v" * 15, [field, rows(2 * N)], scratch)(
            coef, st, g, rt, kk, it, post, *near_planes, *near_spans, *far_spans, *far_planes
        )
        (out,) = call(last, "v" * 9, [field], scratch)(coef, rt, *parts, base, faces, ring)
        return out.reshape(right_side.shape)

    field_spec = P(None, None, None, SFC, SUB, None)
    return jax.shard_map(
        per_device, mesh=mesh4, in_specs=(field_spec, P(SFC, SUB, None), P()), out_specs=field_spec, check_vma=False
    )
```

```python
import jax
import jax.numpy as jnp
from jax import lax
from jax.experimental import pallas as pl
from jax.experimental.pallas import tpu as pltpu
from jax.sharding import Mesh
from jax.sharding import PartitionSpec as P


N = 8
TILES = 2 * N * N
ROWS = TILES * N
penalty = 4.0
shift_mass = 0.02
centre = 1.25
half = 0.95
rho1 = half / centre
rho2 = 1.0 / (2.0 * centre / half - rho1)
keep = rho2 * rho1
gain2 = 2.0 * rho2 / half
exact = lax.Precision.HIGHEST
f32 = jnp.float32
bf16 = jnp.bfloat16
SFC = ("y", "z")
SUB = ("x", "c")


def plane_index():
    return lax.axis_index("y") * lax.axis_size("z") + lax.axis_index("z")


def tile(ref, t):
    return ref[pl.ds(t * N, N), :]


def put(ref, t, value):
    ref[pl.ds(t * N, N), :] = value


def at(q, a, b):
    return (q * N + a) * N + b


def node_columns(sv):
    i = lax.broadcasted_iota(jnp.int32, (N, N), 0)
    j = lax.broadcasted_iota(jnp.int32, (N, N), 1)
    s = sv[...]
    edge = jnp.where((i == j) & ((i == 0) | (i == N - 1)), 2.0, 0.0)
    diag = jnp.sum(jnp.where(i == j, s, 0.0) + edge, axis=1, keepdims=True)
    zero = jnp.zeros((N, 128), f32)
    return diag + zero, jnp.sum(s, axis=1, keepdims=True) + zero


def line(x, k, count=N):
    return jnp.broadcast_to(x[k : k + 1], (count, 128))


def pair_sum(x):
    return jnp.concatenate([line(x, b) + x for b in range(N)], axis=0)


def raw(ref, q, a, b):
    return ref[pl.ds(at(0, a, b) * 2 * N + q, N, stride=2), :]


def pack_first(rs_far, coef_far, sv_far, to_n, to_s, to_e, to_w, rs, coef, sv, sems):
    copies = [
        pltpu.make_async_copy(src, dst, sems.at[k])
        for k, (src, dst) in enumerate(((sv_far, sv), (coef_far, coef), (rs_far, rs)))
    ]
    for copy in copies:
        copy.start()
    copies[0].wait()
    copies[1].wait()
    mc, _ = node_columns(sv)
    sub = lax.broadcasted_iota(jnp.int32, (N, 128), 0)
    c = [coef[pl.ds(q, 1), :] for q in range(2)]
    scale = [1.0 / (centre * c[q]) for q in range(2)]
    zero = jnp.zeros((N, 128), f32)
    both = jnp.where(sub == 0, c[0], jnp.where(sub == 1, c[1], zero))
    copies[2].wait()

    def value(q, a, b):
        return raw(rs, q, a, b) * scale[q] / ((line(mc, a) + line(mc, b)) + mc)

    for q in range(2):
        for b in range(N):
            put(to_n, q * N + b, value(q, N - 1, b))
            put(to_s, q * N + b, value(q, 0, b))
    put(to_n, 2 * N, both)
    put(to_s, 2 * N, both)
    for a in range(N):
        put(to_e, a, value(1, a, N - 1))
        put(to_w, a, value(0, a, 0))
    put(to_e, N, zero + c[1])
    put(to_w, N, zero + c[0])


def stiff(u, kk, st, acc):
    for a in range(N):
        lo = u[pl.ds(at(0, a, 0) * N, N * N), :]
        hi = u[pl.ds(at(1, a, 0) * N, N * N), :]
        x = jnp.concatenate([lo, hi], axis=1)
        xh = x.astype(bf16)
        xl = (x - xh.astype(f32)).astype(bf16)
        main = jnp.dot(kk[...], xh, preferred_element_type=f32)
        rest = jnp.dot(kk[pl.ds(0, N * N), :], xl, preferred_element_type=f32)
        y = main[: N * N] + (main[N * N :] + rest)
        acc[pl.ds(at(0, a, 0) * N, N * N), :] = y[:, :128]
        acc[pl.ds(at(1, a, 0) * N, N * N), :] = y[:, 128:]
    for q in range(2):
        for b in range(N):
            us = [tile(u, at(q, j, b)) for j in range(N)]
            for i in range(N):
                t = tile(acc, at(q, i, b))
                for j in range(N):
                    t = t + tile(st, i * N + j) * us[j]
                put(acc, at(q, i, b), t)


def inner_faces(u, coef, acc):
    c = [coef[pl.ds(q, 1), :] for q in range(2)]
    for q in range(2):
        rc = 2.0 / c[q]
        up = 2.0 + pltpu.roll(c[q], 127, 1) * rc
        down = 2.0 + pltpu.roll(c[q], 1, 1) * rc
        for a in range(N):
            base = at(q, a, 0) * N
            first = pl.ds(base, N, stride=N)
            last = pl.ds(base + N - 1, N, stride=N)
            lower, upper = u[first, :], u[last, :]
            acc[last, :] += up * (upper - pltpu.roll(lower, 127, 1))
            acc[first, :] += down * (lower - pltpu.roll(upper, 1, 1))
    w0 = 2.0 + 2.0 * c[1] / c[0]
    w1 = 2.0 + 2.0 * c[0] / c[1]
    for a in range(N):
        d = tile(u, at(0, a, N - 1)) - tile(u, at(1, a, 0))
        put(acc, at(0, a, N - 1), tile(acc, at(0, a, N - 1)) + w0 * d)
        put(acc, at(1, a, 0), tile(acc, at(1, a, 0)) - w1 * d)


def block(ref, q, a):
    return ref[pl.ds(at(q, a, 0) * N, N * N), :]


def set_block(ref, q, a, value):
    ref[pl.ds(at(q, a, 0) * N, N * N), :] = value


def start(rs, coef, sv, g, rt, rb, kk, st, first, part):
    diag, sums = node_columns(sv)
    mbc = pair_sum(diag)
    pairs = pair_sum(sums)
    for a in range(N):
        rb[pl.ds(a * N * N, N * N), :] = pairs + line(sums, a, N * N)
    for i in range(N):
        for j in range(N):
            put(st, i * N + j, jnp.broadcast_to(sv[pl.ds(i, 1), pl.ds(j, 1)], (N, 128)))
    row = lax.broadcasted_iota(jnp.int32, (N * N, N), 0)
    col = lax.broadcasted_iota(jnp.int32, (N * N, N), 1)
    pb = (row // N == col).astype(f32)
    pc = (row % N == col).astype(f32)
    wide = (((1,), (1,)), ((), ()))

    def outer(p):
        ps = jnp.dot(p, sv[...], precision=exact, preferred_element_type=f32)
        return lax.dot_general(ps, p, wide, precision=exact, preferred_element_type=f32)

    i = lax.broadcasted_iota(jnp.int32, (N * N, N * N), 0)
    j = lax.broadcasted_iota(jnp.int32, (N * N, N * N), 1)
    k = jnp.where(i % N == j % N, outer(pb), 0.0) + jnp.where(i // N == j // N, outer(pc), 0.0)
    kh = k.astype(bf16)
    kk[pl.ds(0, N * N), :] = kh
    kk[pl.ds(N * N, N * N), :] = (k - kh.astype(f32)).astype(bf16)
    rc = [1.0 / coef[pl.ds(q, 1), :] for q in range(2)]
    for a in range(N):
        r = 1.0 / (line(diag, a, N * N) + mbc)
        rt[pl.ds(a * N * N, N * N), :] = r
        for q in range(2):
            for b in range(N):
                t = raw(rs, q, a, b) * rc[q]
                put(g, at(q, a, b), t)
                put(first, at(q, a, b), t * r[b * N : (b + 1) * N] * (1.0 / centre))
    stiff(first, kk, st, part)
    inner_faces(first, coef, part)
    for q in range(2):
        for a in range(N):
            r = rt[pl.ds(a * N * N, N * N), :]
            v = (1.0 + keep) * block(first, q, a) + gain2 * r * (block(g, q, a) - block(part, q, a))
            set_block(part, q, a, v)


def middle(coef, g, rt, rb, first, part, from_n, from_s, from_e, from_w, it, sums_out):
    plane = plane_index()
    c = [coef[pl.ds(q, 1), :] for q in range(2)]
    it[...] = part[...]
    wn = [2.0 + 2.0 * from_n[pl.ds(2 * N * N + q, 1), :] / c[q] for q in range(2)]
    ws = [2.0 + 2.0 * from_s[pl.ds(2 * N * N + q, 1), :] / c[q] for q in range(2)]
    we = 2.0 + 2.0 * from_e[pl.ds(N * N, 1), :] / c[1]
    ww = 2.0 + 2.0 * from_w[pl.ds(N * N, 1), :] / c[0]

    def add(q, a, b, w, other):
        k = at(q, a, b)
        put(it, k, tile(it, k) - gain2 * tile(rt, a * N + b) * (w * (tile(first, k) - other)))

    for q in range(2):
        for b in range(N):
            add(q, N - 1, b, wn[q], tile(from_n, q * N + b))
            add(q, 0, b, ws[q], tile(from_s, q * N + b))
    for a in range(N):
        add(1, a, N - 1, we, tile(from_e, a))
        add(0, a, 0, ww, tile(from_w, a))
    own = jnp.zeros((N, 128), f32)
    above = jnp.zeros((N, 128), f32)
    below = jnp.zeros((N, 128), f32)
    for q in range(2):
        z = jnp.zeros((N * N, 128), f32)
        for a in range(N):
            z = z + (block(g, q, a) - rb[pl.ds(a * N * N, N * N), :] * block(it, q, a))
        t = z[:N]
        up = tile(it, at(q, N - 1, 0))
        dn = tile(it, at(q, 0, 0))
        for b in range(1, N):
            t = t + z[b * N : (b + 1) * N]
            up = up + tile(it, at(q, N - 1, b))
            dn = dn + tile(it, at(q, 0, b))
        up = (c[q] * wn[q]) * up
        dn = (c[q] * ws[q]) * dn
        own = own + (c[q] * t - (up + dn))
        above = above + up
        below = below + dn
    sub = lax.broadcasted_iota(jnp.int32, (N, 128), 0)

    def total(x):
        return jnp.sum(x, axis=0, keepdims=True)

    stack = jnp.where(sub == 0, total(own), 0.0)
    stack = jnp.where(sub == 1, total(above), stack)
    stack = jnp.where(sub == 2, total(below), stack)
    stack = jnp.where(sub == 3, c[0] + c[1], stack)
    s = jnp.sum(stack, axis=1, keepdims=True)
    lane = lax.broadcasted_iota(jnp.int32, (1, 128), 1)
    means = jnp.where(lane == plane, s[0:1], 0.0)
    means = means + jnp.where(lane == plane + 1, s[1:2], 0.0) + jnp.where(lane == plane - 1, s[2:3], 0.0)
    sub2 = lax.broadcasted_iota(jnp.int32, (2, 128), 0)
    pair = jnp.where(sub2 == 0, means, jnp.where(lane == plane, s[3:4], 0.0))
    sums_out[...] = jnp.broadcast_to(pair[None], sums_out.shape)


def smooth(coef, st, g, rt, kk, it, post, to_e, to_w):
    stiff(it, kk, st, post)
    inner_faces(it, coef, post)
    for q in range(2):
        for a in range(N):
            r = rt[pl.ds(a * N * N, N * N), :] * (1.0 / centre)
            set_block(post, q, a, block(it, q, a) + r * (block(g, q, a) - block(post, q, a)))
    for a in range(N):
        for k, field in enumerate((it, post)):
            put(to_e, k * N + a, tile(field, at(1, a, N - 1)))
            put(to_w, k * N + a, tile(field, at(0, a, 0)))


def fold(parts, out):
    total = parts[0]
    for k in range(1, parts.shape[0]):
        total = total + parts[k]
    out[...] = jnp.broadcast_to(total[None], out.shape)


def side(coef, rt, it, post_in, from_e, from_w, got_e, got_w, post, to_n, to_s):
    c = [coef[pl.ds(q, 1), :] for q in range(2)]
    ce = from_e[pl.ds(N * N, 1), :]
    cw = from_w[pl.ds(N * N, 1), :]
    we = 2.0 + 2.0 * ce / c[1]
    ww = 2.0 + 2.0 * cw / c[0]
    post[...] = post_in[...]
    for a in range(N):
        for q, b, w, got in ((1, N - 1, we, got_e), (0, 0, ww, got_w)):
            k = at(q, a, b)
            r = tile(rt, a * N + b) * (1.0 / centre)
            put(post, k, tile(post, k) - r * (w * (tile(it, k) - tile(got, a))))
    sub = lax.broadcasted_iota(jnp.int32, (N, 128), 0)
    outer = jnp.where(sub == 0, ce, jnp.where(sub == 1, cw, 0.0))
    for a, to in ((N - 1, to_n), (0, to_s)):
        for q in range(2):
            for b in range(N):
                put(to, q * N + b, tile(it, at(q, a, b)))
                put(to, 2 * N + q * N + b, tile(post, at(q, a, b)))
        put(to, 4 * N, tile(got_e, a))
        put(to, 4 * N + 1, tile(got_w, a))
        put(to, 4 * N + 2, outer)


def coarse(planes, gains, means):
    lane = lax.broadcasted_iota(jnp.int32, (1, 128), 1)
    before = jnp.where(lane == 0, gains, pltpu.roll(gains, 1, 1))
    diag = penalty * before + (penalty + shift_mass) * gains
    upper = jnp.where(lane < planes - 1, -penalty * gains, 0.0)
    diag = jnp.where(lane < planes, diag, 1.0)
    lower = jnp.where(lane == 0, 0.0, pltpu.roll(upper, 1, 1))
    right = jnp.where(lane < planes, means, 0.0)
    step = 1
    while step < planes:
        inv = 1.0 / diag
        lo = -lower * pltpu.roll(inv, step, 1)
        hi = -upper * pltpu.roll(inv, 128 - step, 1)
        right = right + lo * pltpu.roll(right, step, 1) + hi * pltpu.roll(right, 128 - step, 1)
        diag = diag + lo * pltpu.roll(upper, step, 1) + hi * pltpu.roll(lower, 128 - step, 1)
        lower = lo * pltpu.roll(lower, step, 1)
        upper = hi * pltpu.roll(upper, 128 - step, 1)
        step *= 2
    return right / diag


def tables(rt, rb, kk, st, wt, t1, t7, t0, u, acc):
    lane = lax.broadcasted_iota(jnp.int32, (N * N, 128), 1)
    for a in range(N):
        r = rt[pl.ds(a * N * N, N * N), :] * (1.0 / centre)
        w = 1.0 - r * rb[pl.ds(a * N * N, N * N), :]
        wt[pl.ds(a * N * N, N * N), :] = w
        x = jnp.where(lane == 0, w, 0.0)
        if a == N - 1:
            x = jnp.where(lane == 1, -r, x)
        if a == 0:
            x = jnp.where(lane == 2, -r, x)
        set_block(u, 0, a, x)
        set_block(u, 1, a, jnp.zeros((N * N, 128), f32))
    stiff(u, kk, st, acc)
    for a in range(N):
        x = block(acc, 0, a)
        for k, out in enumerate((t1, t7, t0)):
            out[pl.ds(a * N * N, N * N), :] = jnp.broadcast_to(x[:, k : k + 1], (N * N, 128))


def face_weights(coef, from_n, from_s, from_e, from_w):
    c = [coef[pl.ds(q, 1), :] for q in range(2)]
    cn = [from_n[pl.ds(2 * N * N + q, 1), :] for q in range(2)]
    cs = [from_s[pl.ds(2 * N * N + q, 1), :] for q in range(2)]
    ce = from_e[pl.ds(N * N, 1), :]
    cw = from_w[pl.ds(N * N, 1), :]
    wn = [2.0 + 2.0 * cn[q] / c[q] for q in range(2)]
    ws = [2.0 + 2.0 * cs[q] / c[q] for q in range(2)]
    we = 2.0 + 2.0 * ce / c[1]
    ww = 2.0 + 2.0 * cw / c[0]
    return c, cn, cs, ce, cw, wn, ws, we, ww


def back_weight(own, far):
    return 2.0 + 2.0 * own / jnp.where(far > 0.0, far, 1.0)


def ahead(planes, coef, st, g, rt, kk, it, post, from_n, from_s, from_e, from_w, got_e, got_w, got_n, got_s, base, faces, acc, v):
    plane = plane_index()
    has_n = (plane < planes - 1).astype(f32)
    has_s = (plane > 0).astype(f32)
    inner = 1.0 / centre
    c, cn, cs, ce, cw, wn, ws, we, ww = face_weights(coef, from_n, from_s, from_e, from_w)

    def r_at(a, b):
        return tile(rt, a * N + b)

    v[...] = post[...]
    for q in range(2):
        for b in range(N):
            for a, w, got in ((N - 1, wn[q], got_n), (0, ws[q], got_s)):
                k = at(q, a, b)
                put(v, k, tile(v, k) - inner * r_at(a, b) * (w * (tile(it, k) - tile(got, q * N + b))))
    stiff(v, kk, st, acc)
    inner_faces(v, coef, acc)

    def add(k, w, other):
        put(acc, k, tile(acc, k) + w * (tile(v, k) - other))

    for q in range(2):
        for a, b0, w, has, got, cfar in (
            (N - 1, 0, wn[q], has_n, got_n, cn[q]),
            (0, N - 1, ws[q], has_s, got_s, cs[q]),
        ):
            back = back_weight(c[q], cfar)
            faces[pl.ds((2 if a else 4) + q, 1), :] = w
            faces[pl.ds((6 if a else 8) + q, 1), :] = back
            for b in range(N):
                k = at(q, a, b)
                jump = tile(got, q * N + b) - tile(it, k)
                add(k, w, has * (tile(got, 2 * N + q * N + b) - inner * r_at(b0, b) * (back * jump)))
    for q, b, far_b, w, got, line, row, cfar in (
        (1, N - 1, 0, we, got_e, 4 * N, 0, ce),
        (0, 0, N - 1, ww, got_w, 4 * N + 1, 1, cw),
    ):
        back = back_weight(c[q], cfar)
        faces[pl.ds(row, 1), :] = w
        for a in range(N):
            k = at(q, a, b)
            loss = back * (tile(got, a) - tile(it, k))
            for edge, from_far in ((N - 1, got_n), (0, got_s)):
                if a == edge:
                    wf = 2.0 + 2.0 * from_far[pl.ds((4 * N + 2) * N + row, 1), :] / cfar
                    faces[pl.ds((10 if a else 12) + row, 1), :] = wf
                    loss = loss + wf * (tile(got, a) - tile(from_far, line))
            add(k, w, tile(got, N + a) - inner * r_at(a, far_b) * loss)
    for q in range(2):
        for a in range(N):
            r = rt[pl.ds(a * N * N, N * N), :]
            x = (1.0 + keep) * block(v, q, a) - keep * block(it, q, a)
            set_block(base, q, a, x + gain2 * r * (block(g, q, a) - block(acc, q, a)))


def finish(planes, per_plane, coef, rt, wt, t1, t7, t0, base, faces, ring, out, acc, v):
    scaled = ring[0]
    for k in range(1, ring.shape[0]):
        scaled = scaled + ring[k]
    corr = coarse(planes, scaled[1:2] * (1.0 / per_plane), scaled[0:1] * (1.0 / (per_plane * N * N * N)))
    plane = plane_index()
    lane = lax.broadcasted_iota(jnp.int32, (1, 128), 1)

    def pick(k):
        return jnp.sum(jnp.where(lane == k, corr, 0.0), axis=1, keepdims=True) + jnp.zeros((1, 128), f32)

    mid, high, low = pick(plane), pick(plane + 1), pick(plane - 1)
    has_n = (plane < planes - 1).astype(f32)
    has_s = (plane > 0).astype(f32)
    inner = 1.0 / centre

    def face(k):
        return faces[pl.ds(k, 1), :]

    we, ww = face(0), face(1)
    wn, ws = [face(2), face(3)], [face(4), face(5)]

    def r_at(a, b):
        return tile(rt, a * N + b)

    for q in range(2):
        up, down = wn[q] * (mid - high), ws[q] * (mid - low)
        for a in range(N):
            rows_a = pl.ds(a * N * N, N * N)
            x = mid * wt[rows_a, :]
            if a == N - 1:
                x = x - inner * rt[rows_a, :] * up
            if a == 0:
                x = x - inner * rt[rows_a, :] * down
            set_block(v, q, a, x)
            set_block(acc, q, a, mid * t1[rows_a, :] + up * t7[rows_a, :] + down * t0[rows_a, :])
    inner_faces(v, coef, acc)

    def add(k, w, other):
        put(acc, k, tile(acc, k) + w * (tile(v, k) - other))

    for q in range(2):
        for a, b0, w, has, far in ((N - 1, 0, wn[q], has_n, high), (0, N - 1, ws[q], has_s, low)):
            step = face((6 if a else 8) + q) * (far - mid)
            for b in range(N):
                add(at(q, a, b), w, has * (far * tile(wt, b0 * N + b) - inner * r_at(b0, b) * step))
    for q, b, far_b, w, row in ((1, N - 1, 0, we, 0), (0, 0, N - 1, ww, 1)):
        for a in range(N):
            other = mid * tile(wt, a * N + far_b)
            for edge, far in ((N - 1, high), (0, low)):
                if a == edge:
                    other = other - inner * r_at(a, far_b) * (face((10 if a else 12) + row) * (mid - far))
            add(at(q, a, b), w, other)
    for q in range(2):
        for a in range(N):
            r = rt[pl.ds(a * N * N, N * N), :]
            x = block(base, q, a) + ((1.0 + keep) * block(v, q, a) - keep * mid)
            last = x - gain2 * r * block(acc, q, a)
            for b in range(N):
                out[pl.ds(at(0, a, b) * 2 * N + q, N, stride=2), :] = last[b * N : (b + 1) * N]


def call(kernel, in_kinds, out_shapes, scratch=(), cost=10**6, vmem=24):
    kinds = {"v": pl.BlockSpec(memory_space=pltpu.VMEM), "h": pl.BlockSpec(memory_space=pltpu.HBM)}
    return pl.pallas_call(
        kernel,
        out_shape=out_shapes,
        in_specs=[kinds[k] for k in in_kinds],
        out_specs=[kinds["v"]] * len(out_shapes),
        scratch_shapes=list(scratch),
        compiler_params=pltpu.CompilerParams(vmem_limit_bytes=vmem << 20),
        cost_estimate=pl.CostEstimate(flops=cost, bytes_accessed=10**5, transcendentals=0),
    )


def rows(n, dtype=f32, lanes=128):
    return jax.ShapeDtypeStruct((n, lanes), dtype)


def exchange(block_up, block_down, axis, count, periodic):
    up = [(i, i + 1) for i in range(count - 1)]
    if periodic:
        up.append((count - 1, 0))
    down = [(j, i) for i, j in up]
    return lax.ppermute(block_down, axis, down), lax.ppermute(block_up, axis, up)


def solution(mesh):
    n_sfc, n_sub = mesh.shape["sfc"], mesh.shape["sub"]
    ny = 4 if n_sfc % 16 == 0 else 2
    nz = n_sfc // ny
    mesh4 = Mesh(mesh.devices.reshape(ny, nz, n_sub // 2, 2), ("y", "z", "x", "c"))

    def per_device(right_side, coefficient, stiffness):
        rs = right_side.reshape(ROWS, 128)
        coef = coefficient.reshape(2, 128)
        field = rows(ROWS)
        layer, strip = rows((2 * N + 1) * N), rows((N + 1) * N)
        planes_out = call(
            pack_first,
            "hhh",
            [layer, layer, strip, strip],
            [
                pltpu.VMEM((ROWS, 128), f32),
                pltpu.VMEM((2, 128), f32),
                pltpu.VMEM((N, N), f32),
                pltpu.SemaphoreType.DMA((3,)),
            ],
        )(*(pltpu.with_memory_space_constraint(x, pltpu.HBM) for x in (rs, coef, stiffness)))
        near_planes = exchange(*planes_out[:2], SFC, n_sfc, False)
        near_spans = exchange(*planes_out[2:], SUB, n_sub, True)
        table = rows(N * N * N)
        g, rt, rb, kk, st, first, part = call(
            start, "vvv", [field, table, table, rows(2 * N * N, bf16, N * N), table, field, field], cost=10**9
        )(rs, coef, stiffness)
        it, sums = call(middle, "v" * 10, [field, jax.ShapeDtypeStruct((ny * n_sub, 2, 128), f32)])(
            coef, g, rt, rb, first, part, *near_planes, *near_spans
        )
        near = lax.all_to_all(sums, ("y", "x", "c"), 0, 0)
        (near,) = call(fold, "v", [jax.ShapeDtypeStruct((nz, 2, 128), f32)])(near)
        near, it = lax.optimization_barrier((near, it))
        turned = [(k + nz // 6) % nz for k in range(nz)]
        ring = lax.all_to_all(near, "z", 0, 0, axis_index_groups=[turned])
        post, *spans_out = call(smooth, "vvvvvv", [field, rows(2 * N * N), rows(2 * N * N)], cost=10**9)(
            coef, st, g, rt, kk, it
        )
        far_spans = exchange(*spans_out, SUB, n_sub, True)
        tall = rows((4 * N + 3) * N)
        post, *planes_out = call(side, "v" * 8, [field, tall, tall])(coef, rt, it, post, *near_spans, *far_spans)
        far_planes = exchange(*planes_out, SFC, n_sfc, False)

        scratch = [pltpu.VMEM((ROWS, 128), f32), pltpu.VMEM((ROWS, 128), f32)]
        parts = call(tables, "vvvv", [table] * 4, scratch)(rt, rb, kk, st)

        def early(*refs):
            ahead(n_sfc, *refs)

        def last(*refs):
            finish(n_sfc, float(2 * n_sub * 128), *refs)

        base, faces = call(early, "v" * 15, [field, rows(2 * N)], scratch)(
            coef, st, g, rt, kk, it, post, *near_planes, *near_spans, *far_spans, *far_planes
        )
        (out,) = call(last, "v" * 9, [field], scratch)(coef, rt, *parts, base, faces, ring)
        return out.reshape(right_side.shape)

    field_spec = P(None, None, None, SFC, SUB, None)
    return jax.shard_map(
        per_device, mesh=mesh4, in_specs=(field_spec, P(SFC, SUB, None), P()), out_specs=field_spec, check_vma=False
    )
```

```python
import jax
import jax.numpy as jnp
from jax import lax
from jax.experimental import pallas as pl
from jax.experimental.pallas import tpu as pltpu
from jax.sharding import Mesh
from jax.sharding import PartitionSpec as P


N = 8
TILES = 2 * N * N
ROWS = TILES * N
penalty = 4.0
shift_mass = 0.02
centre = 1.25
half = 0.95
rho1 = half / centre
rho2 = 1.0 / (2.0 * centre / half - rho1)
keep = rho2 * rho1
gain2 = 2.0 * rho2 / half
exact = lax.Precision.HIGHEST
f32 = jnp.float32
bf16 = jnp.bfloat16
SFC = ("y", "z")
SUB = ("x", "c")


def plane_index():
    return lax.axis_index("y") * lax.axis_size("z") + lax.axis_index("z")


def tile(ref, t):
    return ref[pl.ds(t * N, N), :]


def put(ref, t, value):
    ref[pl.ds(t * N, N), :] = value


def at(q, a, b):
    return (q * N + a) * N + b


def node_columns(sv):
    i = lax.broadcasted_iota(jnp.int32, (N, N), 0)
    j = lax.broadcasted_iota(jnp.int32, (N, N), 1)
    s = sv[...]
    edge = jnp.where((i == j) & ((i == 0) | (i == N - 1)), 2.0, 0.0)
    diag = jnp.sum(jnp.where(i == j, s, 0.0) + edge, axis=1, keepdims=True)
    zero = jnp.zeros((N, 128), f32)
    return diag + zero, jnp.sum(s, axis=1, keepdims=True) + zero


def line(x, k, count=N):
    return jnp.broadcast_to(x[k : k + 1], (count, 128))


def pair_sum(x):
    return jnp.concatenate([line(x, b) + x for b in range(N)], axis=0)


def raw(ref, q, a, b):
    return ref[pl.ds(at(0, a, b) * 2 * N + q, N, stride=2), :]


def pack_first(rs_far, coef_far, sv_far, to_n, to_s, to_e, to_w, rs, coef, sv, sems):
    copies = [
        pltpu.make_async_copy(src, dst, sems.at[k])
        for k, (src, dst) in enumerate(((sv_far, sv), (coef_far, coef), (rs_far, rs)))
    ]
    for copy in copies:
        copy.start()
    copies[0].wait()
    copies[1].wait()
    mc, _ = node_columns(sv)
    sub = lax.broadcasted_iota(jnp.int32, (N, 128), 0)
    c = [coef[pl.ds(q, 1), :] for q in range(2)]
    scale = [1.0 / (centre * c[q]) for q in range(2)]
    zero = jnp.zeros((N, 128), f32)
    both = jnp.where(sub == 0, c[0], jnp.where(sub == 1, c[1], zero))
    copies[2].wait()

    def value(q, a, b):
        return raw(rs, q, a, b) * scale[q] / ((line(mc, a) + line(mc, b)) + mc)

    for q in range(2):
        for b in range(N):
            put(to_n, q * N + b, value(q, N - 1, b))
            put(to_s, q * N + b, value(q, 0, b))
    put(to_n, 2 * N, both)
    put(to_s, 2 * N, both)
    for a in range(N):
        put(to_e, a, value(1, a, N - 1))
        put(to_w, a, value(0, a, 0))
    put(to_e, N, zero + c[1])
    put(to_w, N, zero + c[0])


def stiff(u, kk, st, acc):
    for a in range(N):
        lo = u[pl.ds(at(0, a, 0) * N, N * N), :]
        hi = u[pl.ds(at(1, a, 0) * N, N * N), :]
        x = jnp.concatenate([lo, hi], axis=1)
        xh = x.astype(bf16)
        xl = (x - xh.astype(f32)).astype(bf16)
        main = jnp.dot(kk[...], xh, preferred_element_type=f32)
        rest = jnp.dot(kk[pl.ds(0, N * N), :], xl, preferred_element_type=f32)
        y = main[: N * N] + (main[N * N :] + rest)
        acc[pl.ds(at(0, a, 0) * N, N * N), :] = y[:, :128]
        acc[pl.ds(at(1, a, 0) * N, N * N), :] = y[:, 128:]
    for q in range(2):
        for b in range(N):
            us = [tile(u, at(q, j, b)) for j in range(N)]
            for i in range(N):
                t = tile(acc, at(q, i, b))
                for j in range(N):
                    t = t + tile(st, i * N + j) * us[j]
                put(acc, at(q, i, b), t)


def inner_faces(u, coef, acc):
    c = [coef[pl.ds(q, 1), :] for q in range(2)]
    for q in range(2):
        rc = 2.0 / c[q]
        up = 2.0 + pltpu.roll(c[q], 127, 1) * rc
        down = 2.0 + pltpu.roll(c[q], 1, 1) * rc
        for a in range(N):
            base = at(q, a, 0) * N
            first = pl.ds(base, N, stride=N)
            last = pl.ds(base + N - 1, N, stride=N)
            lower, upper = u[first, :], u[last, :]
            acc[last, :] += up * (upper - pltpu.roll(lower, 127, 1))
            acc[first, :] += down * (lower - pltpu.roll(upper, 1, 1))
    w0 = 2.0 + 2.0 * c[1] / c[0]
    w1 = 2.0 + 2.0 * c[0] / c[1]
    for a in range(N):
        d = tile(u, at(0, a, N - 1)) - tile(u, at(1, a, 0))
        put(acc, at(0, a, N - 1), tile(acc, at(0, a, N - 1)) + w0 * d)
        put(acc, at(1, a, 0), tile(acc, at(1, a, 0)) - w1 * d)


def block(ref, q, a):
    return ref[pl.ds(at(q, a, 0) * N, N * N), :]


def set_block(ref, q, a, value):
    ref[pl.ds(at(q, a, 0) * N, N * N), :] = value


def start(rs, coef, sv, g, rt, rb, kk, st, first, part):
    diag, sums = node_columns(sv)
    mbc = pair_sum(diag)
    pairs = pair_sum(sums)
    for a in range(N):
        rb[pl.ds(a * N * N, N * N), :] = pairs + line(sums, a, N * N)
    for i in range(N):
        for j in range(N):
            put(st, i * N + j, jnp.broadcast_to(sv[pl.ds(i, 1), pl.ds(j, 1)], (N, 128)))
    row = lax.broadcasted_iota(jnp.int32, (N * N, N), 0)
    col = lax.broadcasted_iota(jnp.int32, (N * N, N), 1)
    pb = (row // N == col).astype(f32)
    pc = (row % N == col).astype(f32)
    wide = (((1,), (1,)), ((), ()))

    def outer(p):
        ps = jnp.dot(p, sv[...], precision=exact, preferred_element_type=f32)
        return lax.dot_general(ps, p, wide, precision=exact, preferred_element_type=f32)

    i = lax.broadcasted_iota(jnp.int32, (N * N, N * N), 0)
    j = lax.broadcasted_iota(jnp.int32, (N * N, N * N), 1)
    k = jnp.where(i % N == j % N, outer(pb), 0.0) + jnp.where(i // N == j // N, outer(pc), 0.0)
    kh = k.astype(bf16)
    kk[pl.ds(0, N * N), :] = kh
    kk[pl.ds(N * N, N * N), :] = (k - kh.astype(f32)).astype(bf16)
    rc = [1.0 / coef[pl.ds(q, 1), :] for q in range(2)]
    for a in range(N):
        r = 1.0 / (line(diag, a, N * N) + mbc)
        rt[pl.ds(a * N * N, N * N), :] = r
        for q in range(2):
            for b in range(N):
                t = raw(rs, q, a, b) * rc[q]
                put(g, at(q, a, b), t)
                put(first, at(q, a, b), t * r[b * N : (b + 1) * N] * (1.0 / centre))
    stiff(first, kk, st, part)
    inner_faces(first, coef, part)
    for q in range(2):
        for a in range(N):
            r = rt[pl.ds(a * N * N, N * N), :]
            v = (1.0 + keep) * block(first, q, a) + gain2 * r * (block(g, q, a) - block(part, q, a))
            set_block(part, q, a, v)


def middle(coef, g, rt, rb, first, part, from_n, from_s, from_e, from_w, it, sums_out):
    plane = plane_index()
    c = [coef[pl.ds(q, 1), :] for q in range(2)]
    it[...] = part[...]
    wn = [2.0 + 2.0 * from_n[pl.ds(2 * N * N + q, 1), :] / c[q] for q in range(2)]
    ws = [2.0 + 2.0 * from_s[pl.ds(2 * N * N + q, 1), :] / c[q] for q in range(2)]
    we = 2.0 + 2.0 * from_e[pl.ds(N * N, 1), :] / c[1]
    ww = 2.0 + 2.0 * from_w[pl.ds(N * N, 1), :] / c[0]

    def add(q, a, b, w, other):
        k = at(q, a, b)
        put(it, k, tile(it, k) - gain2 * tile(rt, a * N + b) * (w * (tile(first, k) - other)))

    for q in range(2):
        for b in range(N):
            add(q, N - 1, b, wn[q], tile(from_n, q * N + b))
            add(q, 0, b, ws[q], tile(from_s, q * N + b))
    for a in range(N):
        add(1, a, N - 1, we, tile(from_e, a))
        add(0, a, 0, ww, tile(from_w, a))
    own = jnp.zeros((N, 128), f32)
    above = jnp.zeros((N, 128), f32)
    below = jnp.zeros((N, 128), f32)
    for q in range(2):
        z = jnp.zeros((N * N, 128), f32)
        for a in range(N):
            z = z + (block(g, q, a) - rb[pl.ds(a * N * N, N * N), :] * block(it, q, a))
        t = z[:N]
        up = tile(it, at(q, N - 1, 0))
        dn = tile(it, at(q, 0, 0))
        for b in range(1, N):
            t = t + z[b * N : (b + 1) * N]
            up = up + tile(it, at(q, N - 1, b))
            dn = dn + tile(it, at(q, 0, b))
        up = (c[q] * wn[q]) * up
        dn = (c[q] * ws[q]) * dn
        own = own + (c[q] * t - (up + dn))
        above = above + up
        below = below + dn
    sub = lax.broadcasted_iota(jnp.int32, (N, 128), 0)

    def total(x):
        return jnp.sum(x, axis=0, keepdims=True)

    stack = jnp.where(sub == 0, total(own), 0.0)
    stack = jnp.where(sub == 1, total(above), stack)
    stack = jnp.where(sub == 2, total(below), stack)
    stack = jnp.where(sub == 3, c[0] + c[1], stack)
    s = jnp.sum(stack, axis=1, keepdims=True)
    lane = lax.broadcasted_iota(jnp.int32, (1, 128), 1)
    means = jnp.where(lane == plane, s[0:1], 0.0)
    means = means + jnp.where(lane == plane + 1, s[1:2], 0.0) + jnp.where(lane == plane - 1, s[2:3], 0.0)
    sub2 = lax.broadcasted_iota(jnp.int32, (2, 128), 0)
    pair = jnp.where(sub2 == 0, means, jnp.where(lane == plane, s[3:4], 0.0))
    sums_out[...] = jnp.broadcast_to(pair[None], sums_out.shape)


def smooth(coef, st, g, rt, kk, it, post, to_e, to_w):
    stiff(it, kk, st, post)
    inner_faces(it, coef, post)
    for q in range(2):
        for a in range(N):
            r = rt[pl.ds(a * N * N, N * N), :] * (1.0 / centre)
            set_block(post, q, a, block(it, q, a) + r * (block(g, q, a) - block(post, q, a)))
    for a in range(N):
        for k, field in enumerate((it, post)):
            put(to_e, k * N + a, tile(field, at(1, a, N - 1)))
            put(to_w, k * N + a, tile(field, at(0, a, 0)))


def fold(parts, out):
    total = parts[0]
    for k in range(1, parts.shape[0]):
        total = total + parts[k]
    out[...] = jnp.broadcast_to(total[None], out.shape)


def side(coef, rt, it, post_in, from_e, from_w, got_e, got_w, post, to_n, to_s):
    c = [coef[pl.ds(q, 1), :] for q in range(2)]
    ce = from_e[pl.ds(N * N, 1), :]
    cw = from_w[pl.ds(N * N, 1), :]
    we = 2.0 + 2.0 * ce / c[1]
    ww = 2.0 + 2.0 * cw / c[0]
    post[...] = post_in[...]
    for a in range(N):
        for q, b, w, got in ((1, N - 1, we, got_e), (0, 0, ww, got_w)):
            k = at(q, a, b)
            r = tile(rt, a * N + b) * (1.0 / centre)
            put(post, k, tile(post, k) - r * (w * (tile(it, k) - tile(got, a))))
    sub = lax.broadcasted_iota(jnp.int32, (N, 128), 0)
    outer = jnp.where(sub == 0, ce, jnp.where(sub == 1, cw, 0.0))
    for a, to in ((N - 1, to_n), (0, to_s)):
        for q in range(2):
            for b in range(N):
                put(to, q * N + b, tile(it, at(q, a, b)))
                put(to, 2 * N + q * N + b, tile(post, at(q, a, b)))
        put(to, 4 * N, tile(got_e, a))
        put(to, 4 * N + 1, tile(got_w, a))
        put(to, 4 * N + 2, outer)


def coarse(planes, gains, means):
    lane = lax.broadcasted_iota(jnp.int32, (1, 128), 1)
    before = jnp.where(lane == 0, gains, pltpu.roll(gains, 1, 1))
    diag = penalty * before + (penalty + shift_mass) * gains
    upper = jnp.where(lane < planes - 1, -penalty * gains, 0.0)
    diag = jnp.where(lane < planes, diag, 1.0)
    lower = jnp.where(lane == 0, 0.0, pltpu.roll(upper, 1, 1))
    right = jnp.where(lane < planes, means, 0.0)
    step = 1
    while step < planes:
        inv = 1.0 / diag
        lo = -lower * pltpu.roll(inv, step, 1)
        hi = -upper * pltpu.roll(inv, 128 - step, 1)
        right = right + lo * pltpu.roll(right, step, 1) + hi * pltpu.roll(right, 128 - step, 1)
        diag = diag + lo * pltpu.roll(upper, step, 1) + hi * pltpu.roll(lower, 128 - step, 1)
        lower = lo * pltpu.roll(lower, step, 1)
        upper = hi * pltpu.roll(upper, 128 - step, 1)
        step *= 2
    return right / diag


def tables(rt, rb, kk, st, wt, t1, t7, t0, u, acc):
    lane = lax.broadcasted_iota(jnp.int32, (N * N, 128), 1)
    for a in range(N):
        r = rt[pl.ds(a * N * N, N * N), :] * (1.0 / centre)
        w = 1.0 - r * rb[pl.ds(a * N * N, N * N), :]
        wt[pl.ds(a * N * N, N * N), :] = w
        x = jnp.where(lane == 0, w, 0.0)
        if a == N - 1:
            x = jnp.where(lane == 1, -r, x)
        if a == 0:
            x = jnp.where(lane == 2, -r, x)
        set_block(u, 0, a, x)
        set_block(u, 1, a, jnp.zeros((N * N, 128), f32))
    stiff(u, kk, st, acc)
    for a in range(N):
        x = block(acc, 0, a)
        for k, out in enumerate((t1, t7, t0)):
            out[pl.ds(a * N * N, N * N), :] = jnp.broadcast_to(x[:, k : k + 1], (N * N, 128))


def face_weights(coef, from_n, from_s, from_e, from_w):
    c = [coef[pl.ds(q, 1), :] for q in range(2)]
    cn = [from_n[pl.ds(2 * N * N + q, 1), :] for q in range(2)]
    cs = [from_s[pl.ds(2 * N * N + q, 1), :] for q in range(2)]
    ce = from_e[pl.ds(N * N, 1), :]
    cw = from_w[pl.ds(N * N, 1), :]
    wn = [2.0 + 2.0 * cn[q] / c[q] for q in range(2)]
    ws = [2.0 + 2.0 * cs[q] / c[q] for q in range(2)]
    we = 2.0 + 2.0 * ce / c[1]
    ww = 2.0 + 2.0 * cw / c[0]
    return c, cn, cs, ce, cw, wn, ws, we, ww


def back_weight(own, far):
    return 2.0 + 2.0 * own / jnp.where(far > 0.0, far, 1.0)


def ahead(planes, coef, st, g, rt, kk, it, post, from_n, from_s, from_e, from_w, got_e, got_w, got_n, got_s, base, faces, acc, v):
    plane = plane_index()
    has_n = (plane < planes - 1).astype(f32)
    has_s = (plane > 0).astype(f32)
    inner = 1.0 / centre
    c, cn, cs, ce, cw, wn, ws, we, ww = face_weights(coef, from_n, from_s, from_e, from_w)

    def r_at(a, b):
        return tile(rt, a * N + b)

    v[...] = post[...]
    for q in range(2):
        for b in range(N):
            for a, w, got in ((N - 1, wn[q], got_n), (0, ws[q], got_s)):
                k = at(q, a, b)
                put(v, k, tile(v, k) - inner * r_at(a, b) * (w * (tile(it, k) - tile(got, q * N + b))))
    stiff(v, kk, st, acc)
    inner_faces(v, coef, acc)

    def add(k, w, other):
        put(acc, k, tile(acc, k) + w * (tile(v, k) - other))

    for q in range(2):
        for a, b0, w, has, got, cfar in (
            (N - 1, 0, wn[q], has_n, got_n, cn[q]),
            (0, N - 1, ws[q], has_s, got_s, cs[q]),
        ):
            back = back_weight(c[q], cfar)
            faces[pl.ds((2 if a else 4) + q, 1), :] = w
            faces[pl.ds((6 if a else 8) + q, 1), :] = back
            for b in range(N):
                k = at(q, a, b)
                jump = tile(got, q * N + b) - tile(it, k)
                add(k, w, has * (tile(got, 2 * N + q * N + b) - inner * r_at(b0, b) * (back * jump)))
    for q, b, far_b, w, got, line, row, cfar in (
        (1, N - 1, 0, we, got_e, 4 * N, 0, ce),
        (0, 0, N - 1, ww, got_w, 4 * N + 1, 1, cw),
    ):
        back = back_weight(c[q], cfar)
        faces[pl.ds(row, 1), :] = w
        for a in range(N):
            k = at(q, a, b)
            loss = back * (tile(got, a) - tile(it, k))
            for edge, from_far in ((N - 1, got_n), (0, got_s)):
                if a == edge:
                    wf = 2.0 + 2.0 * from_far[pl.ds((4 * N + 2) * N + row, 1), :] / cfar
                    faces[pl.ds((10 if a else 12) + row, 1), :] = wf
                    loss = loss + wf * (tile(got, a) - tile(from_far, line))
            add(k, w, tile(got, N + a) - inner * r_at(a, far_b) * loss)
    for q in range(2):
        for a in range(N):
            r = rt[pl.ds(a * N * N, N * N), :]
            x = (1.0 + keep) * block(v, q, a) - keep * block(it, q, a)
            set_block(base, q, a, x + gain2 * r * (block(g, q, a) - block(acc, q, a)))


def finish(planes, per_plane, coef, rt, wt, t1, t7, t0, base, faces, ring, out, acc, v):
    scaled = ring[0]
    for k in range(1, ring.shape[0]):
        scaled = scaled + ring[k]
    corr = coarse(planes, scaled[1:2] * (1.0 / per_plane), scaled[0:1] * (1.0 / (per_plane * N * N * N)))
    plane = plane_index()
    lane = lax.broadcasted_iota(jnp.int32, (1, 128), 1)

    def pick(k):
        return jnp.sum(jnp.where(lane == k, corr, 0.0), axis=1, keepdims=True) + jnp.zeros((1, 128), f32)

    mid, high, low = pick(plane), pick(plane + 1), pick(plane - 1)
    has_n = (plane < planes - 1).astype(f32)
    has_s = (plane > 0).astype(f32)
    inner = 1.0 / centre

    def face(k):
        return faces[pl.ds(k, 1), :]

    we, ww = face(0), face(1)
    wn, ws = [face(2), face(3)], [face(4), face(5)]

    def r_at(a, b):
        return tile(rt, a * N + b)

    for q in range(2):
        up, down = wn[q] * (mid - high), ws[q] * (mid - low)
        for a in range(N):
            rows_a = pl.ds(a * N * N, N * N)
            x = mid * wt[rows_a, :]
            if a == N - 1:
                x = x - inner * rt[rows_a, :] * up
            if a == 0:
                x = x - inner * rt[rows_a, :] * down
            set_block(v, q, a, x)
            set_block(acc, q, a, mid * t1[rows_a, :] + up * t7[rows_a, :] + down * t0[rows_a, :])
    inner_faces(v, coef, acc)

    def add(k, w, other):
        put(acc, k, tile(acc, k) + w * (tile(v, k) - other))

    for q in range(2):
        for a, b0, w, has, far in ((N - 1, 0, wn[q], has_n, high), (0, N - 1, ws[q], has_s, low)):
            step = face((6 if a else 8) + q) * (far - mid)
            for b in range(N):
                add(at(q, a, b), w, has * (far * tile(wt, b0 * N + b) - inner * r_at(b0, b) * step))
    for q, b, far_b, w, row in ((1, N - 1, 0, we, 0), (0, 0, N - 1, ww, 1)):
        for a in range(N):
            other = mid * tile(wt, a * N + far_b)
            for edge, far in ((N - 1, high), (0, low)):
                if a == edge:
                    other = other - inner * r_at(a, far_b) * (face((10 if a else 12) + row) * (mid - far))
            add(at(q, a, b), w, other)
    for q in range(2):
        for a in range(N):
            r = rt[pl.ds(a * N * N, N * N), :]
            x = block(base, q, a) + ((1.0 + keep) * block(v, q, a) - keep * mid)
            last = x - gain2 * r * block(acc, q, a)
            for b in range(N):
                out[pl.ds(at(0, a, b) * 2 * N + q, N, stride=2), :] = last[b * N : (b + 1) * N]


def call(kernel, in_kinds, out_shapes, scratch=(), cost=10**6, vmem=24):
    kinds = {"v": pl.BlockSpec(memory_space=pltpu.VMEM), "h": pl.BlockSpec(memory_space=pltpu.HBM)}
    return pl.pallas_call(
        kernel,
        out_shape=out_shapes,
        in_specs=[kinds[k] for k in in_kinds],
        out_specs=[kinds["v"]] * len(out_shapes),
        scratch_shapes=list(scratch),
        compiler_params=pltpu.CompilerParams(vmem_limit_bytes=vmem << 20),
        cost_estimate=pl.CostEstimate(flops=cost, bytes_accessed=10**5, transcendentals=0),
    )


def rows(n, dtype=f32, lanes=128):
    return jax.ShapeDtypeStruct((n, lanes), dtype)


def exchange(block_up, block_down, axis, count, periodic):
    up = [(i, i + 1) for i in range(count - 1)]
    if periodic:
        up.append((count - 1, 0))
    down = [(j, i) for i, j in up]
    return lax.ppermute(block_down, axis, down), lax.ppermute(block_up, axis, up)


def solution(mesh):
    n_sfc, n_sub = mesh.shape["sfc"], mesh.shape["sub"]
    ny = 4 if n_sfc % 16 == 0 else 2
    nz = n_sfc // ny
    mesh4 = Mesh(mesh.devices.reshape(ny, nz, n_sub // 2, 2), ("y", "z", "x", "c"))

    def per_device(right_side, coefficient, stiffness):
        rs = right_side.reshape(ROWS, 128)
        coef = coefficient.reshape(2, 128)
        field = rows(ROWS)
        layer, strip = rows((2 * N + 1) * N), rows((N + 1) * N)
        planes_out = call(
            pack_first,
            "hhh",
            [layer, layer, strip, strip],
            [
                pltpu.VMEM((ROWS, 128), f32),
                pltpu.VMEM((2, 128), f32),
                pltpu.VMEM((N, N), f32),
                pltpu.SemaphoreType.DMA((3,)),
            ],
        )(*(pltpu.with_memory_space_constraint(x, pltpu.HBM) for x in (rs, coef, stiffness)))
        near_planes = exchange(*planes_out[:2], SFC, n_sfc, False)
        near_spans = exchange(*planes_out[2:], SUB, n_sub, True)
        table = rows(N * N * N)
        g, rt, rb, kk, st, first, part = call(
            start, "vvv", [field, table, table, rows(2 * N * N, bf16, N * N), table, field, field], cost=10**9
        )(rs, coef, stiffness)
        it, sums = call(middle, "v" * 10, [field, jax.ShapeDtypeStruct((ny * n_sub, 2, 128), f32)])(
            coef, g, rt, rb, first, part, *near_planes, *near_spans
        )
        near = lax.all_to_all(sums, ("y", "x", "c"), 0, 0)
        (near,) = call(fold, "v", [jax.ShapeDtypeStruct((nz, 2, 128), f32)])(near)
        near, it = lax.optimization_barrier((near, it))
        turned = [(k + nz // 16) % nz for k in range(nz)]
        ring = lax.all_to_all(near, "z", 0, 0, axis_index_groups=[turned])
        post, *spans_out = call(smooth, "vvvvvv", [field, rows(2 * N * N), rows(2 * N * N)], cost=10**9)(
            coef, st, g, rt, kk, it
        )
        far_spans = exchange(*spans_out, SUB, n_sub, True)
        tall = rows((4 * N + 3) * N)
        post, *planes_out = call(side, "v" * 8, [field, tall, tall])(coef, rt, it, post, *near_spans, *far_spans)
        far_planes = exchange(*planes_out, SFC, n_sfc, False)

        scratch = [pltpu.VMEM((ROWS, 128), f32), pltpu.VMEM((ROWS, 128), f32)]
        parts = call(tables, "vvvv", [table] * 4, scratch)(rt, rb, kk, st)

        def early(*refs):
            ahead(n_sfc, *refs)

        def last(*refs):
            finish(n_sfc, float(2 * n_sub * 128), *refs)

        base, faces = call(early, "v" * 15, [field, rows(2 * N)], scratch)(
            coef, st, g, rt, kk, it, post, *near_planes, *near_spans, *far_spans, *far_planes
        )
        (out,) = call(last, "v" * 9, [field], scratch)(coef, rt, *parts, base, faces, ring)
        return out.reshape(right_side.shape)

    field_spec = P(None, None, None, SFC, SUB, None)
    return jax.shard_map(
        per_device, mesh=mesh4, in_specs=(field_spec, P(SFC, SUB, None), P()), out_specs=field_spec, check_vma=False
    )
```
